32 devices in a mesh: batch: 4 (over z), ctx: 2 (over y), seq: 4 (over x, core).
Axes of the slice: x: 2, y: 2, z: 4, core: 2. Of those that a mesh axis runs over, the one named last changes fastest.
Arguments:
- inputs: bfloat16 [4, 1024, 2048], P('batch', ('ctx', 'seq')), may hold values from -6 to 6
- w_qkv: bfloat16 [2048, 2304], P(('batch', 'ctx')), may hold values from -0.1875 to 0.1875
- q_bias: bfloat16 [2048], P(('batch', 'ctx')), may hold values from -1.25 to 1.25
- v_bias: bfloat16 [128], P(('batch', 'ctx')), may hold values from -1.25 to 1.25
- w_out: bfloat16 [2048, 2048], P(('batch', 'ctx')), may hold values from -0.5 to 0.5
- out_bias: bfloat16 [2048], P(('batch', 'ctx')), may hold values from -1.25 to 1.25
- gain_attn: bfloat16 [2048], P(('batch', 'ctx')), may hold values from 0.5 to 1.5
- shift_attn: bfloat16 [2048], P(('batch', 'ctx')), may hold values from -1.25 to 1.25
- w_fc: bfloat16 [2048, 8192], P(('batch', 'ctx')), may hold values from -0.125 to 0.125
- fc_bias: bfloat16 [8192], P(('batch', 'ctx')), may hold values from -1.25 to 1.25
- w_proj: bfloat16 [8192, 2048], P(('batch', 'ctx')), may hold values from -0.0625 to 0.0625
- proj_bias: bfloat16 [2048], P(('batch', 'ctx')), may hold values from -1.25 to 1.25
- gain_mlp: bfloat16 [2048], P(('batch', 'ctx')), may hold values from 0.5 to 1.5
- shift_mlp: bfloat16 [2048], P(('batch', 'ctx')), may hold values from -1.25 to 1.25
- cotangent: bfloat16 [4, 1024, 2048], P('batch', ('ctx', 'seq')), may hold values from -6 to 6
Outputs:
- layer_out: bfloat16 [4, 1024, 2048], P('batch', ('ctx', 'seq'))
- input_grad: float32 [4, 1024, 2048], P('batch', ('ctx', 'seq'))
- grad_w_qkv: float32 [2048, 2304], P(('batch', 'ctx'))
- grad_q_bias: float32 [2048], P(('batch', 'ctx'))
- grad_v_bias: float32 [128], P(('batch', 'ctx'))
- grad_w_out: float32 [2048, 2048], P(('batch', 'ctx'))
- grad_out_bias: float32 [2048], P(('batch', 'ctx'))
- grad_gain_attn: float32 [2048], P(('batch', 'ctx'))
- grad_shift_attn: float32 [2048], P(('batch', 'ctx'))
- grad_w_fc: float32 [2048, 8192], P(('batch', 'ctx'))
- grad_fc_bias: float32 [8192], P(('batch', 'ctx'))
- grad_w_proj: float32 [8192, 2048], P(('batch', 'ctx'))
- grad_proj_bias: float32 [2048], P(('batch', 'ctx'))
- grad_gain_mlp: float32 [2048], P(('batch', 'ctx'))
- grad_shift_mlp: float32 [2048], P(('batch', 'ctx'))
The draws below stay inside these ranges and needn't reach their ends.
All inputs are finite; a program needn't handle non-finite values.
Results may differ from the reference program's by a relative error of at most 0.02.
Values may be sent and summed in bfloat16 or wider, within the bound.
A program may use at most 320 MiB of HBM per device.

```python
import math
import jax
import jax.numpy as jnp
from jax import lax

D = 2048
HEADS = 16
HD = 128
FF = 8192
LENGTH = 1024
SEQS = 4


def shard_levels(stream_key, dims, shards, least, largest):
    def one(dim, parts):
        draws = jax.random.uniform(jax.random.fold_in(jax.random.fold_in(stream_key, 6), dim), (parts,), jnp.float32, least / len(shards), largest / len(shards))
        return jnp.repeat(jnp.exp(draws), dims[dim] // parts).reshape((-1,) + (1,) * (len(dims) - dim - 1))

    loudness = one(*shards[0])
    for cut in shards[1:]:
        loudness = loudness * one(*cut)
    return loudness


def normal_values(key, dims, width, most, shards=(), held_as=jnp.bfloat16):
    values = jax.random.normal(key, dims, jnp.float32) * width
    if len(shards) > 0:
        values = shard_levels(key, dims, shards, -0.22, 0.18) * values
    return jnp.clip(values, min=-most, max=most).astype(held_as)


def setup_inputs(seed: int = 0) -> dict:
    splits = jax.random.split(jax.random.key(seed), 16)
    inputs = normal_values(splits[0], (SEQS, LENGTH, D), 1.0, 6.0, ((0, 4), (1, 8)))
    w_qkv = normal_values(splits[1], (D, D + 2 * HD), (D // 2) ** -0.5, 0.1875, ((0, 8),))
    q_bias = normal_values(splits[2], (D,), 0.2, 1.25, ((0, 8),))
    v_bias = normal_values(splits[3], (HD,), 0.2, 1.25, ((0, 8),))
    w_out = normal_values(splits[4], (D, D), (D // 16) ** -0.5, 0.5, ((0, 8),))
    out_bias = normal_values(splits[5], (D,), 0.2, 1.25, ((0, 8),))
    gain_attn = jnp.clip(1.0 + 0.1 * jax.random.normal(splits[6], (D,), jnp.float32), 0.5, 1.5).astype(jnp.bfloat16)
    shift_attn = normal_values(splits[7], (D,), 0.2, 1.25, ((0, 8),))
    w_fc = normal_values(splits[8], (D, FF), D ** -0.5, 0.125, ((0, 8),))
    fc_bias = normal_values(splits[9], (FF,), 0.2, 1.25, ((0, 8),))
    w_proj = normal_values(splits[10], (FF, D), FF ** -0.5, 0.0625, ((0, 8),))
    proj_bias = normal_values(splits[11], (D,), 0.2, 1.25, ((0, 8),))
    gain_mlp = jnp.clip(1.0 + 0.1 * jax.random.normal(splits[12], (D,), jnp.float32), 0.5, 1.5).astype(jnp.bfloat16)
    shift_mlp = normal_values(splits[13], (D,), 0.2, 1.25, ((0, 8),))
    cotangent = normal_values(splits[14], (SEQS, LENGTH, D), 1.0, 6.0, ((0, 4), (1, 8)))
    return dict(inputs=inputs, w_qkv=w_qkv, q_bias=q_bias, v_bias=v_bias, w_out=w_out, out_bias=out_bias, gain_attn=gain_attn, shift_attn=shift_attn, w_fc=w_fc, fc_bias=fc_bias, w_proj=w_proj, proj_bias=proj_bias, gain_mlp=gain_mlp, shift_mlp=shift_mlp, cotangent=cotangent)


@jax.custom_vjp
def low(v):
    return lax.optimization_barrier(v.astype(jnp.bfloat16)).astype(jnp.float32)

@jax.custom_vjp
def low_back(v):
    return v

def low_keep(v):
    return (low(v), None)

def low_pass(kept, grad):
    return (grad,)

def back_keep(v):
    return (v, None)

def back_low(kept, grad):
    return (low(grad),)
low.defvjp(low_keep, low_pass)
low_back.defvjp(back_keep, back_low)
highest = lax.Precision.HIGHEST

def high_dot(left, right):
    return jnp.dot(left, right, precision=highest, preferred_element_type=jnp.float32)

def layer_norm(values, gain_vec, shift_vec):
    center = lax.optimization_barrier(jnp.mean(values, axis=-1, keepdims=True))
    centred = values - center
    spread = lax.optimization_barrier(jnp.mean(centred * centred, axis=-1, keepdims=True))
    return centred * lax.rsqrt(spread + 1e-05) * gain_vec + shift_vec

def gelu_tanh(values):
    return 0.5 * values * (1.0 + jnp.tanh(math.sqrt(2.0 / math.pi) * (values + 0.044715 * values * values * values)))

def attend(queries, keyval):
    qblock = min(512, LENGTH)
    blocks = LENGTH // qblock
    key_rows = keyval[:, :HD]
    value_rows = keyval[:, HD:]
    key_pos = jnp.arange(LENGTH)
    score_scale = 1.0 / math.sqrt(HD)

    def one_block(block_in):
        block_queries, first_row = block_in
        raw_scores = jnp.einsum('qhd,kd->hqk', block_queries, key_rows, precision=highest)
        scores = low_back(raw_scores) * score_scale
        query_pos = first_row + jnp.arange(qblock)
        allowed = key_pos[None, :] <= query_pos[:, None]
        scores = jnp.where(allowed[None], scores, -1e+30)
        maxima = lax.optimization_barrier(jnp.max(scores, axis=-1, keepdims=True))
        shifted = jnp.exp(scores - maxima)
        weights = shifted / lax.optimization_barrier(jnp.sum(shifted, axis=-1, keepdims=True))
        return jnp.einsum('hqk,kd->qhd', low(weights), value_rows, precision=highest)
    grouped = queries.reshape(blocks, qblock, HEADS, HD)
    starts = jnp.arange(blocks) * qblock
    results = lax.map(jax.checkpoint(one_block), (grouped, starts))
    return results.reshape(LENGTH, HEADS * HD)

def layer_forward(sequence, params):
    w_qkv, q_bias, v_bias, w_out, out_bias, gain_attn, shift_attn, w_fc, fc_bias, w_proj, proj_bias, gain_mlp, shift_mlp = params
    normed = low(layer_norm(sequence, gain_attn, shift_attn))
    mixed_rows = high_dot(normed, w_qkv)
    query_rows = low_back(low(mixed_rows[:, :D] + q_bias))
    key_rows = low_back(low(mixed_rows[:, D:D + HD]))
    value_rows = low_back(low(mixed_rows[:, D + HD:] + v_bias))
    keyval = jnp.concatenate([key_rows, value_rows], axis=1)
    attended = low_back(low(attend(query_rows.reshape(LENGTH, HEADS, HD), keyval)))
    residual = sequence + low_back(high_dot(attended, w_out)) + out_bias
    normed_mlp = low(layer_norm(residual, gain_mlp, shift_mlp))
    hidden = low_back(high_dot(normed_mlp, w_fc) + fc_bias)
    active = low(gelu_tanh(hidden))
    return residual + low_back(high_dot(active, w_proj)) + proj_bias

def reference(inputs, w_qkv, q_bias, v_bias, w_out, out_bias, gain_attn, shift_attn, w_fc, fc_bias, w_proj, proj_bias, gain_mlp, shift_mlp, cotangent):
    params = (w_qkv.astype(jnp.float32), q_bias.astype(jnp.float32), v_bias.astype(jnp.float32), w_out.astype(jnp.float32), out_bias.astype(jnp.float32), gain_attn.astype(jnp.float32), shift_attn.astype(jnp.float32), w_fc.astype(jnp.float32), fc_bias.astype(jnp.float32), w_proj.astype(jnp.float32), proj_bias.astype(jnp.float32), gain_mlp.astype(jnp.float32), shift_mlp.astype(jnp.float32))

    def forward(sequences, weights):

        def per_sequence(sequence):
            return layer_forward(sequence, weights)
        return lax.map(jax.checkpoint(per_sequence), sequences)
    result, pullback = jax.vjp(forward, inputs.astype(jnp.float32), params)
    grad_inputs, grad_params = pullback(cotangent.astype(jnp.float32))
    g_qkv, g_qbias, g_vbias, g_wout, g_obias, g_gain_one, g_shift_one, g_wfc, g_fcbias, g_wproj, g_projbias, g_gain_two, g_shift_two = grad_params
    return (result.astype(jnp.bfloat16), grad_inputs, g_qkv, g_qbias, g_vbias, g_wout, g_obias, g_gain_one, g_shift_one, g_wfc, g_fcbias, g_wproj, g_projbias, g_gain_two, g_shift_two)
```

```python
import functools
import math

import jax
import jax.numpy as jnp
from jax import lax
from jax.experimental import pallas as pl
from jax.experimental.pallas import tpu as pltpu
from jax.sharding import PartitionSpec as P

D = 2048
HEADS = 16
HD = 128
MESH = pl.DeviceIdType.MESH
BF = jnp.bfloat16
F32 = jnp.float32
ANY = pl.ANY
VMEM = pltpu.VMEM
DMA = pltpu.SemaphoreType.DMA


class ZY:
    def __init__(self, mesh):
        self.no, self.ni = mesh.shape["batch"], mesh.shape["ctx"]

    def me(self):
        return lax.axis_index("batch"), lax.axis_index("ctx")

    def dev(self, o, i):
        return {"batch": o, "ctx": i}


class SEQ:
    def __init__(self, mesh):
        self.no, self.ni = mesh.shape["seq"] // 2, 2

    def me(self):
        s = lax.axis_index("seq")
        return s // 2, lax.rem(s, 2)

    def dev(self, o, i):
        return {"seq": 2 * o + i}


def rcopy(src, dst, ss, rs, dev):
    return pltpu.make_async_remote_copy(
        src_ref=src, dst_ref=dst, send_sem=ss, recv_sem=rs, device_id=dev, device_id_type=MESH
    )


def gather_steps(grp, src, view, ss, rs, ls):
    o, i = grp.me()
    no = grp.no
    mate = grp.dev(o, 1 - i)
    own = pltpu.make_async_copy(src, view(o, i), ls.at[0])
    own.start()
    sent = []
    for d in range(1, no):
        c = rcopy(src, view(o, i), ss.at[d], rs.at[d], grp.dev(lax.rem(o + d, no), i))
        c.start()
        sent.append(c)
    c = rcopy(src, view(o, i), ss.at[0], rs.at[0], mate)
    c.start()
    sent.append(c)
    yield
    for d in range(1, no):
        f = lax.rem(o - d + no, no)
        rcopy(view(f, i), view(f, i), ss.at[d], rs.at[d], mate).wait_recv()
        c = rcopy(view(f, i), view(f, i), ss.at[no + d - 1], rs.at[no + d - 1], mate)
        c.start()
        sent.append(c)
        yield
    rcopy(view(o, 1 - i), view(o, 1 - i), ss.at[0], rs.at[0], mate).wait_recv()
    for d in range(1, no):
        f = lax.rem(o - d + no, no)
        v = view(f, 1 - i)
        rcopy(v, v, ss.at[no + d - 1], rs.at[no + d - 1], mate).wait_recv()
    for c in sent:
        c.wait_send()
    own.wait()


def gather_sems(grp):
    n = 2 * grp.no - 1
    return [DMA((n,)), DMA((n,)), DMA((1,))]


def add_rows(dst, a, b, rows, step=16):
    def one(r, _):
        at = pl.ds(pl.multiple_of(r * step, step), step)
        dst[at] = (a[at].astype(F32) + b[at].astype(F32)).astype(dst.dtype)
        return 0

    lax.fori_loop(0, rows // step, one, 0)


def scatter_steps(grp, part, out, near, mid, far, ss, rs):
    o, i = grp.me()
    no = grp.no
    mate = grp.dev(o, 1 - i)
    sent = []
    order = list(range(1, no)) + [0]
    rows = out.shape[0]
    for d in order:
        t = lax.rem(o + d, no)
        c = rcopy(part(t, 1 - i), near.at[d], ss.at[d], rs.at[d], mate)
        c.start()
        sent.append(c)
    yield
    for d in order:
        t = lax.rem(o + d, no)
        rcopy(near.at[d], near.at[d], ss.at[d], rs.at[d], mate).wait_recv()
        if d == 0:
            add_rows(out, part(t, i), near.at[d], rows)
        else:
            add_rows(mid.at[d - 1], part(t, i), near.at[d], rows)
            c = rcopy(
                mid.at[d - 1], far.at[d - 1], ss.at[no + d - 1], rs.at[no + d - 1], grp.dev(t, i)
            )
            c.start()
            sent.append(c)
        yield
    for d in range(1, no):
        v = far.at[d - 1]
        rcopy(v, v, ss.at[no + d - 1], rs.at[no + d - 1], mate).wait_recv()
        add_rows(out, out, v, rows)
    for c in sent:
        c.wait_send()


def scatter_scratch(grp, shape, dtype):
    n = 2 * grp.no - 1
    return [
        VMEM((grp.no,) + shape, dtype),
        VMEM((grp.no - 1,) + shape, dtype),
        VMEM((grp.no - 1,) + shape, dtype),
        DMA((n,)),
        DMA((n,)),
    ]


def exchange_steps(grp, src, dst, ss, rs, ls):
    o, i = grp.me()
    no, ni = grp.no, grp.ni
    sent = []
    own = pltpu.make_async_copy(src(o, i), dst(o, i), ls.at[0])
    own.start()
    for a in range(no):
        for b in range(ni):
            if a == 0 and b == 0:
                continue
            to, ti = lax.rem(o + a, no), lax.rem(i + b, ni)
            k = a * ni + b - 1
            c = rcopy(src(to, ti), dst(o, i), ss.at[k], rs.at[k], grp.dev(to, ti))
            c.start()
            sent.append(c)
    yield
    for a in range(no):
        for b in range(ni):
            if a == 0 and b == 0:
                continue
            fo, fi = lax.rem(o - a + no, no), lax.rem(i - b + ni, ni)
            k = a * ni + b - 1
            v = dst(fo, fi)
            rcopy(v, v, ss.at[k], rs.at[k], grp.dev(fo, fi)).wait_recv()
    for c in sent:
        c.wait_send()
    own.wait()


def exchange_sems(grp):
    n = grp.no * grp.ni - 1
    return [DMA((n,)), DMA((n,)), DMA((1,))]


def barrier(groups):
    sem = pltpu.get_barrier_semaphore()
    count = 0
    for grp in groups:
        o, i = grp.me()
        for a in range(grp.no):
            for b in range(grp.ni):
                if a == 0 and b == 0:
                    continue
                to, ti = lax.rem(o + a, grp.no), lax.rem(i + b, grp.ni)
                pl.semaphore_signal(sem, inc=1, device_id=grp.dev(to, ti), device_id_type=MESH)
                count += 1
    pl.semaphore_wait(sem, count)


def run_all(gens):
    live = list(gens)
    while live:
        left = []
        for g in live:
            try:
                next(g)
                left.append(g)
            except StopIteration:
                pass
        live = left


def comm(name, ident, groups, ops, ici=0):
    arrays, in_specs, out_shapes, out_specs, scratch, cuts = [], [], [], [], [], []
    for ins, outs, scr, steps in ops:
        cuts.append((len(ins), len(outs), len(scr), steps))
        for a, space in ins:
            arrays.append(a)
            in_specs.append(pl.BlockSpec(memory_space=space))
        for shape, dtype, space in outs:
            out_shapes.append(jax.ShapeDtypeStruct(shape, dtype))
            out_specs.append(pl.BlockSpec(memory_space=space))
        scratch.extend(scr)

    def kernel(*refs):
        barrier(groups)
        a, b, c = 0, len(arrays), len(arrays) + len(out_shapes)
        gens = []
        for ni, no, ns, steps in cuts:
            gens.append(steps(refs[a : a + ni], refs[b : b + no], refs[c : c + ns]))
            a, b, c = a + ni, b + no, c + ns
        run_all(gens)

    return pl.pallas_call(
        kernel,
        out_shape=out_shapes,
        in_specs=in_specs,
        out_specs=out_specs,
        scratch_shapes=scratch,
        compiler_params=pltpu.CompilerParams(
            collective_id=ident, has_side_effects=True, vmem_limit_bytes=63 * 1024 * 1024
        ),
        name=name,
    )(*arrays)


def op_gather(grp, x):
    shape = (grp.no * grp.ni,) + x.shape

    def steps(ins, outs, scr):
        return gather_steps(grp, ins[0], lambda o, i: outs[0].at[o * grp.ni + i], *scr)

    return ([(x, VMEM)], [(shape, x.dtype, ANY)], gather_sems(grp), steps)


def op_scatter(grp, x, dtype=F32):
    shape = x.shape[1:]

    def steps(ins, outs, scr):
        return scatter_steps(grp, lambda o, i: ins[0].at[o * grp.ni + i], outs[0], *scr)

    return ([(x, VMEM)], [(shape, dtype, VMEM)], scatter_scratch(grp, shape, x.dtype), steps)


def op_exchange(grp, x, space=ANY):
    def steps(ins, outs, scr):
        return exchange_steps(
            grp,
            lambda o, i: ins[0].at[o * grp.ni + i],
            lambda o, i: outs[0].at[o * grp.ni + i],
            *scr,
        )

    return ([(x, VMEM)], [(x.shape, x.dtype, space)], exchange_sems(grp), steps)


def layer_norm(values, gain_vec, shift_vec):
    center = jnp.mean(values, axis=-1, keepdims=True)
    centred = values - center
    spread = jnp.mean(centred * centred, axis=-1, keepdims=True)
    return centred * lax.rsqrt(spread + 1e-05) * gain_vec + shift_vec


def gelu_tanh(values):
    return (
        0.5
        * values
        * (
            1.0
            + jnp.tanh(math.sqrt(2.0 / math.pi) * (values + 0.044715 * values * values * values))
        )
    )


def allowed_mask(other_first, first_row, qblock, ctx_len, key_span):
    piece = jnp.broadcast_to(other_first, (qblock, ctx_len))
    query_pos = first_row + jnp.arange(qblock)[:, None]
    key_pos = jnp.arange(key_span)[None, :]
    return jnp.concatenate([piece, key_pos <= query_pos], axis=1)


def block_scores(block_queries, keyval, allowed):
    score_scale = 1.0 / math.sqrt(HD)
    raw_scores = jnp.einsum(
        "qhd,kd->hqk", block_queries, keyval[:, :HD], preferred_element_type=F32
    )
    return jnp.where(allowed[None], raw_scores * score_scale, -1e30)


def attention_forward(queries, own_rows, other_rows, other_first, qblock):
    ctx_len = own_rows.shape[0]
    outputs = []
    logsums = []
    for block_index in range(ctx_len // qblock):
        first_row = block_index * qblock
        key_span = first_row + qblock
        keyval = jnp.concatenate([other_rows, own_rows[:key_span]], axis=0)
        allowed = allowed_mask(other_first, first_row, qblock, ctx_len, key_span)
        masked = block_scores(queries[first_row:key_span], keyval, allowed)
        maxima = jnp.max(masked, axis=-1, keepdims=True)
        shifted = jnp.exp(masked - maxima)
        totals = jnp.sum(shifted, axis=-1, keepdims=True)
        weights = (shifted / totals).astype(BF)
        outputs.append(
            jnp.einsum("hqk,kd->qhd", weights, keyval[:, HD:], preferred_element_type=F32)
        )
        logsums.append(maxima + jnp.log(totals))
    return (jnp.concatenate(outputs, axis=0), logsums)


def attention_backward(queries, grad_out, own_rows, other_rows, other_first, qblock, logsums):
    ctx_len = own_rows.shape[0]
    score_scale = 1.0 / math.sqrt(HD)
    grad_others = jnp.zeros((ctx_len, 2 * HD), F32)
    grad_own = jnp.zeros((ctx_len, 2 * HD), F32)
    grad_queries = []
    for block_index in range(ctx_len // qblock):
        first_row = block_index * qblock
        key_span = first_row + qblock
        keyval = jnp.concatenate([other_rows, own_rows[:key_span]], axis=0)
        allowed = allowed_mask(other_first, first_row, qblock, ctx_len, key_span)
        block_queries = queries[first_row:key_span]
        block_grad = grad_out[first_row:key_span]
        masked = block_scores(block_queries, keyval, allowed)
        weights = jnp.exp(masked - logsums[block_index])
        grad_weights = jnp.einsum(
            "qhd,kd->hqk", block_grad, keyval[:, HD:], preferred_element_type=F32
        )
        inner_sum = jnp.sum(weights * grad_weights, axis=-1, keepdims=True)
        grad_scores = (weights * (grad_weights - inner_sum) * score_scale).astype(BF)
        grad_queries.append(
            jnp.einsum("hqk,kd->qhd", grad_scores, keyval[:, :HD], preferred_element_type=F32)
        )
        grad_keys = jnp.einsum(
            "hqk,qhd->kd", grad_scores, block_queries, preferred_element_type=F32
        )
        grad_values = jnp.einsum(
            "hqk,qhd->kd", weights.astype(BF), block_grad, preferred_element_type=F32
        )
        grad_keyval = jnp.concatenate([grad_keys, grad_values], axis=1)
        grad_others = grad_others + grad_keyval[:ctx_len]
        grad_own = grad_own + jnp.pad(grad_keyval[ctx_len:], ((0, ctx_len - key_span), (0, 0)))
    return (jnp.concatenate(grad_queries, axis=0), grad_others, grad_own)


def dot(a, b, dims=((1,), (0,))):
    return lax.dot_general(a, b, (dims, ((), ())), preferred_element_type=F32)


def make_body(mesh):
    zy, sq = ZY(mesh), SEQ(mesh)
    S = mesh.shape["seq"]
    G = mesh.shape["batch"] * mesh.shape["ctx"]
    W = D // G
    QC = (HEADS // S) * HD

    class CTX:
        no, ni = 1, 2

        def me(self):
            return 0, lax.axis_index("ctx")

        def dev(self, o, i):
            return {"ctx": i}

    yx = CTX()

    def op_pair(x):
        def steps(ins, outs, scr):
            def gen():
                o, i = yx.me()
                c = rcopy(ins[0], outs[0], scr[0].at[0], scr[1].at[0], yx.dev(o, 1 - i))
                c.start()
                yield
                c.wait()

            return gen()

        return ([(x, VMEM)], [(x.shape, x.dtype, VMEM)], [DMA((1,)), DMA((1,))], steps)

    def op_spread_fc(w):
        rows, cols = W // S, w.shape[1] // G

        def steps(ins, outs, scr):
            src, out = ins[0], outs[0]
            xs, gs = scr[:3], scr[3:]
            s = lax.axis_index("seq")

            def gen():
                yield from exchange_steps(
                    zy,
                    lambda o, i: src.at[
                        pl.ds(pl.multiple_of(s * rows, rows), rows),
                        pl.ds(pl.multiple_of((o * zy.ni + i) * cols, cols), cols),
                    ],
                    lambda o, i: out.at[o * zy.ni + i, s],
                    *xs,
                )
                yield from gather_steps_inplace(sq, lambda o, i: out.at[:, 2 * o + i], *gs)

            return gen()

        return (
            [(w, VMEM)],
            [((G, S, rows, cols), w.dtype, ANY)],
            exchange_sems(zy) + gather_sems(sq)[:2],
            steps,
        )

    def gather_steps_inplace(grp, view, ss, rs):
        o, i = grp.me()
        no = grp.no
        mate = grp.dev(o, 1 - i)
        sent = []
        for d in list(range(1, no)) + [0]:
            to = grp.dev(lax.rem(o + d, no), i) if d else mate
            c = rcopy(view(o, i), view(o, i), ss.at[d], rs.at[d], to)
            c.start()
            sent.append(c)
        yield
        for d in range(1, no):
            v = view(lax.rem(o - d + no, no), i)
            rcopy(v, v, ss.at[d], rs.at[d], mate).wait_recv()
            c = rcopy(v, v, ss.at[no + d - 1], rs.at[no + d - 1], mate)
            c.start()
            sent.append(c)
        yield
        v = view(o, 1 - i)
        rcopy(v, v, ss.at[0], rs.at[0], mate).wait_recv()
        for d in range(1, no):
            v = view(lax.rem(o - d + no, no), 1 - i)
            rcopy(v, v, ss.at[no + d - 1], rs.at[no + d - 1], mate).wait_recv()
        for c in sent:
            c.wait_send()

    def op_sum_all(grp, x):
        shape = x.shape[1:]

        def steps(ins, outs, scr):
            acc, sc, gs = scr[0], scr[1:6], scr[6:]

            def gen():
                yield from scatter_steps(
                    grp, lambda o, i: ins[0].at[o * grp.ni + i], acc, *sc
                )
                yield from gather_steps(
                    grp, acc, lambda o, i: outs[0].at[o * grp.ni + i], *gs
                )

            return gen()

        return (
            [(x, VMEM)],
            [(x.shape, x.dtype, ANY)],
            [VMEM(shape, x.dtype)] + scatter_scratch(grp, shape, x.dtype) + gather_sems(grp),
            steps,
        )

    def op_grad_fc(x):
        rows, cols = x.shape[2:]

        def steps(ins, outs, scr):
            acc, sc, line, xs, gs = scr[0], scr[1:6], scr[6], scr[7:10], scr[10:]

            def gen():
                near, mid, far, ss, rs = sc
                src = ins[0]
                yield from scatter_steps(
                    sq,
                    lambda o, i: src.at[2 * o + i],
                    acc,
                    near,
                    mid,
                    far,
                    ss,
                    rs,
                )
                yield from exchange_steps(
                    zy,
                    lambda o, i: acc.at[pl.ds(pl.multiple_of((o * zy.ni + i) * rows, rows), rows)],
                    lambda o, i: line.at[
                        :, pl.ds(pl.multiple_of((o * zy.ni + i) * cols, cols), cols)
                    ],
                    *xs,
                )
                yield from gather_steps(sq, line, lambda o, i: outs[0].at[2 * o + i], *gs)

            return gen()

        shape = (G * rows, cols)
        return (
            [(x.swapaxes(0, 1).reshape(S, G * rows, cols), VMEM)],
            [((S, rows, G * cols), x.dtype, ANY)],
            [VMEM(shape, x.dtype)]
            + scatter_scratch(sq, shape, x.dtype)
            + [VMEM((rows, G * cols), x.dtype)]
            + exchange_sems(zy)
            + gather_sems(sq),
            steps,
        )

    def op_scatter_gather(x):
        shape = x.shape[1:]

        def steps(ins, outs, scr):
            acc, sc, gs = scr[0], scr[1:6], scr[6:]

            def gen():
                yield from scatter_steps(zy, lambda o, i: ins[0].at[o * zy.ni + i], acc, *sc)
                yield from gather_steps(sq, acc, lambda o, i: outs[0].at[2 * o + i], *gs)

            return gen()

        return (
            [(x, VMEM)],
            [((S,) + shape, x.dtype, ANY)],
            [VMEM(shape, x.dtype)] + scatter_scratch(zy, shape, x.dtype) + gather_sems(sq),
            steps,
        )

    def op_small(x, own):
        r, q = x.shape[1], own.shape[0]

        def steps(ins, outs, scr):
            got, line = scr[0], scr[1]
            xs, gs = scr[2:5], scr[5:]

            def gen():
                yield from exchange_steps(
                    zy,
                    lambda o, i: ins[0].at[o * zy.ni + i],
                    lambda o, i: got.at[o * zy.ni + i],
                    *xs,
                )
                total = got[0]
                for k in range(1, G):
                    total = total + got[k]
                line[:r] = total
                line[r:] = ins[1][...]
                yield from gather_steps(sq, line, lambda o, i: outs[0].at[2 * o + i], *gs)

            return gen()

        return (
            [(x, VMEM), (own, VMEM)],
            [((S, r + q, 128), F32, ANY)],
            [VMEM(x.shape, F32), VMEM((r + q, 128), F32)] + exchange_sems(zy) + gather_sems(sq),
            steps,
        )

    def body(
        inputs,
        w_qkv,
        q_bias,
        v_bias,
        w_out,
        out_bias,
        gain_attn,
        shift_attn,
        w_fc,
        fc_bias,
        w_proj,
        proj_bias,
        gain_mlp,
        shift_mlp,
        cotangent,
    ):
        s = lax.axis_index("seq")
        place = lax.axis_index("ctx")
        rows_in = inputs[0]
        R = rows_in.shape[0]
        g_out = cotangent[0]
        vb = v_bias.shape[0]
        small = jnp.concatenate(
            [gain_attn, shift_attn, q_bias, out_bias, proj_bias, gain_mlp, shift_mlp]
            + [v_bias, jnp.zeros((256 - vb,), BF)]
        ).reshape(-1, 128)
        w_cols = jnp.concatenate(
            [
                lax.dynamic_slice_in_dim(w_qkv, s * QC, QC, 1),
                w_qkv[:, D:],
                lax.dynamic_slice_in_dim(w_out, s * QC, QC, 1),
            ],
            axis=1,
        )
        span, small_all, w_att, fc_cols, g_all = comm(
            "comm_entry",
            1,
            [zy, sq],
            [
                op_gather(sq, rows_in),
                op_gather(zy, small),
                op_gather(zy, w_cols),
                op_spread_fc(w_fc),
                op_gather(zy, g_out),
            ],
        )
        vecs = small_all[:, :14].reshape(G, 7, W).swapaxes(0, 1).reshape(7, D).astype(F32)
        gain_one, shift_one, qb, ob, pb, gain_two, shift_two = [vecs[k] for k in range(7)]
        vb_full = small_all[:, 14, :vb].reshape(-1).astype(F32)
        w_att = w_att.reshape(D, 2 * QC + 2 * HD)
        w_in = w_att[:, : QC + 2 * HD]
        w_back = w_att[:, QC + 2 * HD :]

        tokens = rows_in.astype(F32)
        _, norm_back = jax.vjp(layer_norm, tokens, gain_one, shift_one)
        span_rows = span.reshape(S * R, D).astype(F32)
        normed = layer_norm(span_rows, gain_one, shift_one).astype(BF)
        mixed = dot(normed, w_in)
        queries = (mixed[:, :QC] + lax.dynamic_slice_in_dim(qb, s * QC, QC, 0)).astype(BF)
        keyval = jnp.concatenate(
            [mixed[:, QC : QC + HD].astype(BF), (mixed[:, QC + HD :] + vb_full).astype(BF)], axis=1
        )
        (other,) = comm("comm_kv", 2, [yx], [op_pair(keyval)])
        other_first = place == 1
        T = S * R
        qblock = min(512, T)
        q3 = queries.reshape(T, QC // HD, HD)
        attended, logsums = attention_forward(q3, keyval, other, other_first, qblock)
        attended = attended.astype(BF).reshape(T, QC)
        (att_all,) = comm("comm_att", 3, [sq], [op_gather(sq, attended)])
        att_rows = att_all.swapaxes(0, 1).reshape(T, D)
        branch_cols = dot(att_rows, w_back).astype(BF)
        (branch_in,) = comm(
            "comm_branch", 4, [sq], [op_exchange(sq, branch_cols.reshape(S, R, QC))]
        )
        branch = branch_in.swapaxes(0, 1).reshape(R, D).astype(F32) + ob
        residual = tokens + branch
        normed_mlp, norm_back_mlp = jax.vjp(layer_norm, residual, gain_two, shift_two)
        (x_all,) = comm("comm_mlp", 5, [zy], [op_gather(zy, normed_mlp.astype(BF))])
        x_all = x_all.reshape(G * R, D)
        g_rows = g_all.reshape(G * R, D)
        fc = fc_cols.reshape(D, -1)
        ffl = fc.shape[1]
        hidden = dot(x_all, fc) + fc_bias.astype(F32)
        active, gelu_back = jax.vjp(gelu_tanh, hidden)
        active_low = active.astype(BF)
        y_part = dot(active_low, w_proj).astype(BF)
        grad_active = dot(g_rows, w_proj, ((1,), (1,)))
        grad_hidden = gelu_back(grad_active)[0].astype(BF)
        grad_fc_bias = jnp.sum(grad_hidden.astype(F32), axis=0)
        gx_part = dot(grad_hidden, fc, ((1,), (1,))).astype(BF)
        d_proj = dot(active_low, g_rows, ((0,), (0,))).astype(BF)
        d_fc = dot(x_all, grad_hidden, ((0,), (0,))).astype(BF)
        gx_sum, y_sum, d_proj_all, d_fc_all = comm(
            "comm_mlp_back",
            6,
            [zy, sq],
            [
                op_scatter(zy, gx_part.reshape(G, R, D)),
                op_scatter(zy, y_part.reshape(G, R, D)),
                op_sum_all(sq, d_proj.reshape(S, ffl // S, D)),
                op_grad_fc(d_fc.reshape(G, S, W // S, ffl)),
            ],
        )
        output = residual + y_sum + pb
        grad_output = g_out.astype(F32)
        grad_resid_part, grad_gain_mlp, grad_shift_mlp = norm_back_mlp(gx_sum)
        grad_residual = grad_output + grad_resid_part
        grad_branch = grad_residual.astype(BF)
        (gb_in,) = comm(
            "comm_gbranch",
            7,
            [sq],
            [op_exchange(sq, grad_branch.reshape(R, S, QC).swapaxes(0, 1))],
        )
        gb = gb_in.reshape(T, QC)
        ga_part = dot(gb, w_back, ((1,), (1,))).astype(BF)
        d_out = dot(att_rows, gb, ((0,), (0,)))
        (g_att,) = comm(
            "comm_gatt",
            8,
            [sq],
            [op_scatter(sq, ga_part.reshape(T, S, QC).swapaxes(0, 1))],
        )
        g_att = g_att.astype(BF).reshape(T, QC // HD, HD)
        grad_q, grad_other, grad_own = attention_backward(
            q3, g_att, keyval, other, other_first, qblock, logsums
        )
        (grad_in,) = comm("comm_gkv", 9, [yx], [op_pair(grad_other.astype(BF))])
        grad_kv = (grad_own + grad_in.astype(F32)).astype(BF)
        grad_q = grad_q.astype(BF).reshape(T, QC)
        grad_mixed = jnp.concatenate([grad_q, grad_kv], axis=1)
        gn_part = dot(grad_mixed, w_in, ((1,), (1,))).astype(BF)
        d_in = dot(normed, grad_mixed, ((0,), (0,)))
        d_att = jnp.concatenate([d_in, d_out], axis=1).astype(BF)
        gn_sum, d_att_all = comm(
            "comm_attn_back",
            10,
            [zy, sq],
            [
                op_scatter(sq, gn_part.reshape(S, R, D)),
                op_scatter_gather(d_att.reshape(G, W, 2 * QC + 2 * HD)),
            ],
        )
        grad_token_part, grad_gain_attn, grad_shift_attn = norm_back(gn_sum)
        input_grad = grad_residual + grad_token_part
        grad_qb = lax.dynamic_update_slice_in_dim(
            jnp.zeros((D,), F32), jnp.sum(grad_q.astype(F32), axis=0), s * QC, 0
        )
        grad_vb = jnp.sum(grad_kv[:, HD:].astype(F32), axis=0)
        terms = jnp.stack(
            [
                grad_qb,
                jnp.sum(grad_residual, axis=0),
                grad_gain_attn,
                grad_shift_attn,
                jnp.sum(grad_output, axis=0),
                grad_gain_mlp,
                grad_shift_mlp,
            ]
        )
        terms = terms.reshape(7, G, W).swapaxes(0, 1).reshape(G, 7 * W)
        tail = jnp.pad(grad_vb.reshape(G, vb), ((0, 0), (0, 256 - vb)))
        terms = jnp.concatenate([terms, tail], axis=1).reshape(G, -1, 128)
        (small_sum,) = comm(
            "comm_small", 11, [zy, sq], [op_small(terms, grad_fc_bias.reshape(-1, 128))]
        )
        sums = jnp.sum(small_sum, axis=0)
        v7 = sums[:14].reshape(7, W)
        d_att_f = d_att_all.astype(F32)
        grad_w_qkv = jnp.concatenate(
            [
                d_att_f[:, :, :QC].swapaxes(0, 1).reshape(W, D),
                jnp.sum(d_att_f[:, :, QC : QC + 2 * HD], axis=0),
            ],
            axis=1,
        )
        grad_w_out = d_att_f[:, :, QC + 2 * HD :].swapaxes(0, 1).reshape(W, D)
        return (
            output.astype(BF)[None],
            input_grad[None],
            grad_w_qkv,
            v7[0],
            sums[14, :vb],
            grad_w_out,
            v7[1],
            v7[2],
            v7[3],
            d_fc_all.reshape(W, -1).astype(F32),
            sums[16:].reshape(-1),
            d_proj_all.reshape(-1, D).astype(F32),
            v7[4],
            v7[5],
            v7[6],
        )

    return body


def solution(mesh):
    rows = P("batch", ("ctx", "seq"), None)
    mat = P(("batch", "ctx"), None)
    vec = P(("batch", "ctx"))
    in_specs = (rows, mat, vec, vec, mat, vec, vec, vec, mat, vec, mat, vec, vec, vec, rows)
    out_specs = (rows, rows, mat, vec, vec, mat, vec, vec, vec, mat, vec, mat, vec, vec, vec)
    return jax.shard_map(
        make_body(mesh), mesh=mesh, in_specs=in_specs, out_specs=out_specs, check_vma=False
    )
```

```python
import functools
import math

import jax
import jax.numpy as jnp
from jax import lax
from jax.experimental import pallas as pl
from jax.experimental.pallas import tpu as pltpu
from jax.sharding import PartitionSpec as P

D = 2048
HEADS = 16
HD = 128
MESH = pl.DeviceIdType.MESH
BF = jnp.bfloat16
F32 = jnp.float32
ANY = pl.ANY
VMEM = pltpu.VMEM
DMA = pltpu.SemaphoreType.DMA


class ZY:
    line = True

    def __init__(self, mesh):
        self.no, self.ni = mesh.shape["batch"], mesh.shape["ctx"]

    def me(self):
        return lax.axis_index("batch"), lax.axis_index("ctx")

    def dev(self, o, i):
        return {"batch": o, "ctx": i}


class SEQ:
    line = False

    def __init__(self, mesh):
        self.no, self.ni = mesh.shape["seq"] // 2, 2

    def me(self):
        s = lax.axis_index("seq")
        return s // 2, lax.rem(s, 2)

    def dev(self, o, i):
        return {"seq": 2 * o + i}


def rcopy(src, dst, ss, rs, dev):
    return pltpu.make_async_remote_copy(
        src_ref=src, dst_ref=dst, send_sem=ss, recv_sem=rs, device_id=dev, device_id_type=MESH
    )


def gather_steps(grp, src, view, ss, rs, ls):
    if grp.line:
        return line_gather_steps(grp, src, view, ss, rs, ls)
    return star_gather_steps(grp, src, view, ss, rs, ls)


def star_gather_steps(grp, src, view, ss, rs, ls):
    o, i = grp.me()
    no = grp.no
    mate = grp.dev(o, 1 - i)
    own = pltpu.make_async_copy(src, view(o, i), ls.at[0])
    own.start()
    sent = []
    for d in range(1, no):
        c = rcopy(src, view(o, i), ss.at[d], rs.at[d], grp.dev(lax.rem(o + d, no), i))
        c.start()
        sent.append(c)
    c = rcopy(src, view(o, i), ss.at[0], rs.at[0], mate)
    c.start()
    sent.append(c)
    yield
    for d in range(1, no):
        f = lax.rem(o - d + no, no)
        rcopy(view(f, i), view(f, i), ss.at[d], rs.at[d], mate).wait_recv()
        c = rcopy(view(f, i), view(f, i), ss.at[no + d - 1], rs.at[no + d - 1], mate)
        c.start()
        sent.append(c)
        yield
    rcopy(view(o, 1 - i), view(o, 1 - i), ss.at[0], rs.at[0], mate).wait_recv()
    for d in range(1, no):
        f = lax.rem(o - d + no, no)
        v = view(f, 1 - i)
        rcopy(v, v, ss.at[no + d - 1], rs.at[no + d - 1], mate).wait_recv()
    for c in sent:
        c.wait_send()
    own.wait()


def gather_sems(grp):
    if grp.line:
        return line_gather_sems(grp)
    n = 2 * grp.no - 1
    return [DMA((n,)), DMA((n,)), DMA((1,))]


def add_all(dst, refs, rows, step=16):
    def one(r, _):
        at = pl.ds(pl.multiple_of(r * step, step), step)
        total = refs[0][at].astype(F32)
        for ref in refs[1:]:
            total = total + ref[at].astype(F32)
        dst[at] = total.astype(dst.dtype)
        return 0

    lax.fori_loop(0, rows // step, one, 0)


def scatter_steps(grp, part, out, *scr):
    if grp.line:
        return line_scatter_steps(grp, part, out, *scr)
    return star_scatter_steps(grp, part, out, *scr)


def star_scatter_steps(grp, part, out, near, mid, far, ss, rs, ls):
    o, i = grp.me()
    no = grp.no
    mate = grp.dev(o, 1 - i)
    sent, own = [], []
    order = list(range(1, no)) + [0]
    rows = out.shape[0]
    for d in order:
        t = lax.rem(o + d, no)
        c = rcopy(part(t, 1 - i), near.at[d], ss.at[d], rs.at[d], mate)
        c.start()
        sent.append(c)
        c = pltpu.make_async_copy(part(t, i), mid.at[d], ls.at[d])
        c.start()
        own.append(c)
    yield
    for c, d in zip(own, order):
        t = lax.rem(o + d, no)
        c.wait()
        rcopy(near.at[d], near.at[d], ss.at[d], rs.at[d], mate).wait_recv()
        if d == 0:
            add_all(out, [mid.at[d], near.at[d]], rows)
        else:
            add_all(mid.at[d], [mid.at[d], near.at[d]], rows)
            c = rcopy(
                mid.at[d], far.at[d - 1], ss.at[no + d - 1], rs.at[no + d - 1], grp.dev(t, i)
            )
            c.start()
            sent.append(c)
            yield
    yield
    for d in range(1, no):
        v = far.at[d - 1]
        rcopy(v, v, ss.at[no + d - 1], rs.at[no + d - 1], mate).wait_recv()
        add_all(out, [out, v], rows)
    for c in sent:
        c.wait_send()


def scatter_scratch(grp, shape, dtype):
    no = grp.no
    if grp.line:
        return [
            VMEM((no,) + shape, dtype),
            VMEM((no,) + shape, dtype),
            VMEM((no + 1,) + shape, dtype),
            DMA((2 * no - 1,)),
            DMA((2 * no + 1,)),
            DMA((no,)),
        ]
    n = 2 * no - 1
    return [
        VMEM((no,) + shape, dtype),
        VMEM((no,) + shape, dtype),
        VMEM((no - 1,) + shape, dtype),
        DMA((n,)),
        DMA((n,)),
        DMA((no,)),
    ]


def line_gather_steps(grp, src, view, ss, rs, ls):
    o, i = grp.me()
    n = grp.no
    mate, right, left = grp.dev(o, 1 - i), grp.dev(o + 1, i), grp.dev(o - 1, i)
    own = pltpu.make_async_copy(src, view(o, i), ls.at[0])
    own.start()
    sent = []

    def send(pred, ref, dst, k, to):
        def copy():
            return rcopy(ref, dst, ss.at[k], rs.at[k], to)

        pl.when(pred)(lambda: copy().start())
        sent.append((pred, copy))

    def got(v, k):
        rcopy(v, v, ss.at[k], rs.at[k], mate).wait_recv()

    R, L, Y = -1, n - 2, 2 * n - 2
    send(o < n - 1, src, view(o, i), R + 1, right)
    send(o > 0, src, view(o, i), L + 1, left)
    c = rcopy(src, view(o, i), ss.at[Y], rs.at[Y], mate)
    c.start()
    yield
    for k in range(1, n):
        a, b = lax.max(o - k, 0), lax.min(o + k, n - 1)
        from_left, from_right = o >= k, o + k <= n - 1
        pl.when(from_left)(lambda: got(view(a, i), R + k))
        if k < n - 1:
            send(from_left & (o < n - 1), view(a, i), view(a, i), R + k + 1, right)
        send(from_left, view(a, i), view(a, i), Y + k, mate)
        pl.when(from_right)(lambda: got(view(b, i), L + k))
        if k < n - 1:
            send(from_right & (o > 0), view(b, i), view(b, i), L + k + 1, left)
        send(from_right, view(b, i), view(b, i), Y + n - 1 + k, mate)
        yield
    got(view(o, 1 - i), Y)
    for k in range(1, n):
        a, b = lax.max(o - k, 0), lax.min(o + k, n - 1)
        pl.when(o >= k)(lambda: got(view(a, 1 - i), Y + k))
        pl.when(o + k <= n - 1)(lambda: got(view(b, 1 - i), Y + n - 1 + k))
    for pred, copy in sent:
        pl.when(pred)(lambda: copy().wait_send())
    c.wait_send()
    own.wait()


def line_gather_sems(grp):
    n = 4 * grp.no - 3
    return [DMA((n,)), DMA((n,)), DMA((1,))]


def line_scatter_steps(grp, part, out, near, mid, far, ss, rs, ls):
    o, i = grp.me()
    n = grp.no
    mate = grp.dev(o, 1 - i)
    rows = out.shape[0]
    low = o < n // 2

    def target(j):
        if j == n - 1:
            return o
        down = jnp.where(n - 1 - j > o, n - 1 - j, n - 2 - j)
        up = jnp.where(j < o, j, j + 1)
        return jnp.where(low, down, up)

    sent, own = [], []
    for j in range(n):
        c = rcopy(part(target(j), 1 - i), near.at[j], ss.at[j], rs.at[j], mate)
        c.start()
        sent.append(c)
        c = pltpu.make_async_copy(part(target(j), i), mid.at[j], ls.at[j])
        c.start()
        own.append(c)
    yield
    moved = []
    for j in range(n - 1):
        t = target(j)
        own[j].wait()
        rcopy(near.at[j], near.at[j], ss.at[j], rs.at[j], mate).wait_recv()
        for right in (True, False):
            towards = (t > o) if right else (t < o)
            inner = (o > 0) if right else (o < n - 1)
            slot = t if right else jnp.where(t == o - 1, n, t)
            to = grp.dev(o + 1, i) if right else grp.dev(o - 1, i)

            def copy(j=j, slot=slot, to=to):
                return rcopy(mid.at[j], far.at[slot], ss.at[n + j], rs.at[n + slot], to)

            @pl.when(towards & inner)
            def _():
                rcopy(far.at[t], far.at[t], ss.at[n + j], rs.at[n + t], mate).wait_recv()
                add_all(mid.at[j], [mid.at[j], near.at[j], far.at[t]], rows)

            @pl.when(towards & jnp.logical_not(inner))
            def _():
                add_all(mid.at[j], [mid.at[j], near.at[j]], rows)

            pl.when(towards)(lambda: copy().start())
            moved.append((towards, copy))
        yield
    j = n - 1
    own[j].wait()
    rcopy(near.at[j], near.at[j], ss.at[j], rs.at[j], mate).wait_recv()

    def arrived(k):
        rcopy(far.at[k], far.at[k], ss.at[j], rs.at[n + k], mate).wait_recv()

    pl.when(o > 0)(lambda: arrived(o))
    pl.when(o < n - 1)(lambda: arrived(n))
    mine = [mid.at[j], near.at[j]]
    inside = (o > 0) & (o < n - 1)
    pl.when(inside)(lambda: add_all(out, mine + [far.at[o], far.at[n]], rows))
    pl.when(o == 0)(lambda: add_all(out, mine + [far.at[n]], rows))
    pl.when(o == n - 1)(lambda: add_all(out, mine + [far.at[o]], rows))
    for c in sent:
        c.wait_send()
    for pred, copy in moved:
        pl.when(pred)(lambda: copy().wait_send())


def exchange_steps(grp, src, dst, ss, rs, ls):
    o, i = grp.me()
    no, ni = grp.no, grp.ni
    sent = []
    own = pltpu.make_async_copy(src(o, i), dst(o, i), ls.at[0])
    own.start()
    for a in range(no):
        for b in range(ni):
            if a == 0 and b == 0:
                continue
            to, ti = lax.rem(o + a, no), lax.rem(i + b, ni)
            k = a * ni + b - 1
            c = rcopy(src(to, ti), dst(o, i), ss.at[k], rs.at[k], grp.dev(to, ti))
            c.start()
            sent.append(c)
    yield
    for a in range(no):
        for b in range(ni):
            if a == 0 and b == 0:
                continue
            fo, fi = lax.rem(o - a + no, no), lax.rem(i - b + ni, ni)
            k = a * ni + b - 1
            v = dst(fo, fi)
            rcopy(v, v, ss.at[k], rs.at[k], grp.dev(fo, fi)).wait_recv()
    for c in sent:
        c.wait_send()
    own.wait()


def exchange_sems(grp):
    n = grp.no * grp.ni - 1
    return [DMA((n,)), DMA((n,)), DMA((1,))]


def barrier(groups):
    sem = pltpu.get_barrier_semaphore()
    count = 0
    for grp in groups:
        o, i = grp.me()
        for a in range(grp.no):
            for b in range(grp.ni):
                if a == 0 and b == 0:
                    continue
                to, ti = lax.rem(o + a, grp.no), lax.rem(i + b, grp.ni)
                pl.semaphore_signal(sem, inc=1, device_id=grp.dev(to, ti), device_id_type=MESH)
                count += 1
    pl.semaphore_wait(sem, count)


def run_all(gens):
    live = list(gens)
    while live:
        left = []
        for g in live:
            try:
                next(g)
                left.append(g)
            except StopIteration:
                pass
        live = left


def comm(name, ident, groups, ops, ici=0):
    arrays, in_specs, out_shapes, out_specs, scratch, cuts = [], [], [], [], [], []
    for ins, outs, scr, steps in ops:
        cuts.append((len(ins), len(outs), len(scr), steps))
        for a, space in ins:
            arrays.append(a)
            in_specs.append(pl.BlockSpec(memory_space=space))
        for shape, dtype, space in outs:
            out_shapes.append(jax.ShapeDtypeStruct(shape, dtype))
            out_specs.append(pl.BlockSpec(memory_space=space))
        scratch.extend(scr)

    def kernel(*refs):
        barrier(groups)
        a, b, c = 0, len(arrays), len(arrays) + len(out_shapes)
        gens = []
        for ni, no, ns, steps in cuts:
            gens.append(steps(refs[a : a + ni], refs[b : b + no], refs[c : c + ns]))
            a, b, c = a + ni, b + no, c + ns
        run_all(gens)

    return pl.pallas_call(
        kernel,
        out_shape=out_shapes,
        in_specs=in_specs,
        out_specs=out_specs,
        scratch_shapes=scratch,
        compiler_params=pltpu.CompilerParams(
            collective_id=ident, has_side_effects=True, vmem_limit_bytes=63 * 1024 * 1024
        ),
        name=name,
    )(*arrays)


def fused(name, ident, groups, ins, outs, scratch, main):
    keys = list(ins) + list(outs)
    in_specs = [pl.BlockSpec(memory_space=space) for _, space in ins.values()]
    out_specs = [pl.BlockSpec(memory_space=space) for _, _, space in outs.values()]
    out_shapes = [jax.ShapeDtypeStruct(shape, dtype) for shape, dtype, _ in outs.values()]
    flat = [x for group in scratch.values() for x in group]

    def kernel(*refs):
        named = dict(zip(keys, refs))
        at = len(keys)
        for key, group in scratch.items():
            named[key] = refs[at : at + len(group)]
            at += len(group)
        barrier(groups)
        main(named)

    got = pl.pallas_call(
        kernel,
        out_shape=out_shapes,
        in_specs=in_specs,
        out_specs=out_specs,
        scratch_shapes=flat,
        compiler_params=pltpu.CompilerParams(
            collective_id=ident, has_side_effects=True, vmem_limit_bytes=63 * 1024 * 1024
        ),
        name=name,
    )(*[a for a, _ in ins.values()])
    return dict(zip(outs, got))


def step(gen):
    next(gen, None)


def finish(*gens):
    run_all(gens)


def row_loop(rows, fn, size=16):
    def one(r, _):
        fn(pl.ds(pl.multiple_of(r * size, size), size))
        return 0

    lax.fori_loop(0, rows // size, one, 0)


def cols(k, width):
    return pl.ds(pl.multiple_of(k * width, width), width)


def op_gather(grp, x):
    shape = (grp.no * grp.ni,) + x.shape

    def steps(ins, outs, scr):
        return gather_steps(grp, ins[0], lambda o, i: outs[0].at[o * grp.ni + i], *scr)

    return ([(x, VMEM)], [(shape, x.dtype, ANY)], gather_sems(grp), steps)


def op_scatter(grp, x, dtype=F32):
    shape = x.shape[1:]

    def steps(ins, outs, scr):
        return scatter_steps(grp, lambda o, i: ins[0].at[o * grp.ni + i], outs[0], *scr)

    return ([(x, VMEM)], [(shape, dtype, VMEM)], scatter_scratch(grp, shape, x.dtype), steps)


def op_exchange(grp, x, space=ANY):
    def steps(ins, outs, scr):
        return exchange_steps(
            grp,
            lambda o, i: ins[0].at[o * grp.ni + i],
            lambda o, i: outs[0].at[o * grp.ni + i],
            *scr,
        )

    return ([(x, VMEM)], [(x.shape, x.dtype, space)], exchange_sems(grp), steps)


def layer_norm(values, gain_vec, shift_vec):
    center = jnp.mean(values, axis=-1, keepdims=True)
    centred = values - center
    spread = jnp.mean(centred * centred, axis=-1, keepdims=True)
    return centred * lax.rsqrt(spread + 1e-05) * gain_vec + shift_vec


def gelu_tanh(values):
    return (
        0.5
        * values
        * (
            1.0
            + jnp.tanh(math.sqrt(2.0 / math.pi) * (values + 0.044715 * values * values * values))
        )
    )


def allowed_mask(other_first, first_row, qblock, ctx_len, key_span):
    piece = jnp.broadcast_to(other_first, (qblock, ctx_len))
    query_pos = first_row + jnp.arange(qblock)[:, None]
    key_pos = jnp.arange(key_span)[None, :]
    return jnp.concatenate([piece, key_pos <= query_pos], axis=1)


def block_scores(block_queries, keyval, allowed):
    score_scale = 1.0 / math.sqrt(HD)
    raw_scores = jnp.einsum(
        "qhd,kd->hqk", block_queries, keyval[:, :HD], preferred_element_type=F32
    )
    return jnp.where(allowed[None], raw_scores * score_scale, -1e30)


def attention_forward(queries, own_rows, other_rows, other_first, qblock):
    ctx_len = own_rows.shape[0]
    outputs = []
    logsums = []
    for block_index in range(ctx_len // qblock):
        first_row = block_index * qblock
        key_span = first_row + qblock
        keyval = jnp.concatenate([other_rows, own_rows[:key_span]], axis=0)
        allowed = allowed_mask(other_first, first_row, qblock, ctx_len, key_span)
        masked = block_scores(queries[first_row:key_span], keyval, allowed)
        maxima = jnp.max(masked, axis=-1, keepdims=True)
        shifted = jnp.exp(masked - maxima)
        totals = jnp.sum(shifted, axis=-1, keepdims=True)
        weights = (shifted / totals).astype(BF)
        outputs.append(
            jnp.einsum("hqk,kd->qhd", weights, keyval[:, HD:], preferred_element_type=F32)
        )
        logsums.append(maxima + jnp.log(totals))
    return (jnp.concatenate(outputs, axis=0), logsums)


def attention_backward(queries, grad_out, own_rows, other_rows, other_first, qblock, logsums):
    ctx_len = own_rows.shape[0]
    score_scale = 1.0 / math.sqrt(HD)
    grad_others = jnp.zeros((ctx_len, 2 * HD), F32)
    grad_own = jnp.zeros((ctx_len, 2 * HD), F32)
    grad_queries = []
    for block_index in range(ctx_len // qblock):
        first_row = block_index * qblock
        key_span = first_row + qblock
        keyval = jnp.concatenate([other_rows, own_rows[:key_span]], axis=0)
        allowed = allowed_mask(other_first, first_row, qblock, ctx_len, key_span)
        block_queries = queries[first_row:key_span]
        block_grad = grad_out[first_row:key_span]
        masked = block_scores(block_queries, keyval, allowed)
        weights = jnp.exp(masked - logsums[block_index])
        grad_weights = jnp.einsum(
            "qhd,kd->hqk", block_grad, keyval[:, HD:], preferred_element_type=F32
        )
        inner_sum = jnp.sum(weights * grad_weights, axis=-1, keepdims=True)
        grad_scores = (weights * (grad_weights - inner_sum) * score_scale).astype(BF)
        grad_queries.append(
            jnp.einsum("hqk,kd->qhd", grad_scores, keyval[:, :HD], preferred_element_type=F32)
        )
        grad_keys = jnp.einsum(
            "hqk,qhd->kd", grad_scores, block_queries, preferred_element_type=F32
        )
        grad_values = jnp.einsum(
            "hqk,qhd->kd", weights.astype(BF), block_grad, preferred_element_type=F32
        )
        grad_keyval = jnp.concatenate([grad_keys, grad_values], axis=1)
        grad_others = grad_others + grad_keyval[:ctx_len]
        grad_own = grad_own + jnp.pad(grad_keyval[ctx_len:], ((0, ctx_len - key_span), (0, 0)))
    return (jnp.concatenate(grad_queries, axis=0), grad_others, grad_own)


def dot(a, b, dims=((1,), (0,))):
    return lax.dot_general(a, b, (dims, ((), ())), preferred_element_type=F32)


def make_body(mesh):
    zy, sq = ZY(mesh), SEQ(mesh)
    S = mesh.shape["seq"]
    G = mesh.shape["batch"] * mesh.shape["ctx"]
    W = D // G
    QC = (HEADS // S) * HD

    class CTX:
        no, ni = 1, 2

        def me(self):
            return 0, lax.axis_index("ctx")

        def dev(self, o, i):
            return {"ctx": i}

    yx = CTX()

    def op_pair(x):
        def steps(ins, outs, scr):
            def gen():
                o, i = yx.me()
                c = rcopy(ins[0], outs[0], scr[0].at[0], scr[1].at[0], yx.dev(o, 1 - i))
                c.start()
                yield
                c.wait()

            return gen()

        return ([(x, VMEM)], [(x.shape, x.dtype, VMEM)], [DMA((1,)), DMA((1,))], steps)

    def op_spread_fc(w):
        rows, cols = W // S, w.shape[1] // G

        def steps(ins, outs, scr):
            src, out = ins[0], outs[0]
            xs, gs = scr[:3], scr[3:]
            s = lax.axis_index("seq")

            def gen():
                yield from exchange_steps(
                    zy,
                    lambda o, i: src.at[
                        pl.ds(pl.multiple_of(s * rows, rows), rows),
                        pl.ds(pl.multiple_of((o * zy.ni + i) * cols, cols), cols),
                    ],
                    lambda o, i: out.at[o * zy.ni + i, s],
                    *xs,
                )
                yield from gather_steps_inplace(sq, lambda o, i: out.at[:, 2 * o + i], *gs)

            return gen()

        return (
            [(w, VMEM)],
            [((G, S, rows, cols), w.dtype, ANY)],
            exchange_sems(zy) + gather_sems(sq)[:2],
            steps,
        )

    def gather_steps_inplace(grp, view, ss, rs):
        o, i = grp.me()
        no = grp.no
        mate = grp.dev(o, 1 - i)
        sent = []
        for d in list(range(1, no)) + [0]:
            to = grp.dev(lax.rem(o + d, no), i) if d else mate
            c = rcopy(view(o, i), view(o, i), ss.at[d], rs.at[d], to)
            c.start()
            sent.append(c)
        yield
        for d in range(1, no):
            v = view(lax.rem(o - d + no, no), i)
            rcopy(v, v, ss.at[d], rs.at[d], mate).wait_recv()
            c = rcopy(v, v, ss.at[no + d - 1], rs.at[no + d - 1], mate)
            c.start()
            sent.append(c)
        yield
        v = view(o, 1 - i)
        rcopy(v, v, ss.at[0], rs.at[0], mate).wait_recv()
        for d in range(1, no):
            v = view(lax.rem(o - d + no, no), 1 - i)
            rcopy(v, v, ss.at[no + d - 1], rs.at[no + d - 1], mate).wait_recv()
        for c in sent:
            c.wait_send()

    def op_sum_all(grp, x):
        shape = x.shape[1:]

        def steps(ins, outs, scr):
            acc, sc, gs = scr[0], scr[1:7], scr[7:]

            def gen():
                yield from scatter_steps(
                    grp, lambda o, i: ins[0].at[o * grp.ni + i], acc, *sc
                )
                yield from gather_steps(
                    grp, acc, lambda o, i: outs[0].at[o * grp.ni + i], *gs
                )

            return gen()

        return (
            [(x, VMEM)],
            [(x.shape, x.dtype, ANY)],
            [VMEM(shape, x.dtype)] + scatter_scratch(grp, shape, x.dtype) + gather_sems(grp),
            steps,
        )

    def op_grad_fc(x):
        rows, cols = x.shape[2:]

        def steps(ins, outs, scr):
            acc, sc, line, xs, gs = scr[0], scr[1:7], scr[7], scr[8:11], scr[11:]

            def gen():
                src = ins[0]
                yield from scatter_steps(
                    sq,
                    lambda o, i: src.at[2 * o + i],
                    acc,
                    *sc,
                )
                yield from exchange_steps(
                    zy,
                    lambda o, i: acc.at[pl.ds(pl.multiple_of((o * zy.ni + i) * rows, rows), rows)],
                    lambda o, i: line.at[
                        :, pl.ds(pl.multiple_of((o * zy.ni + i) * cols, cols), cols)
                    ],
                    *xs,
                )
                yield from gather_steps(sq, line, lambda o, i: outs[0].at[2 * o + i], *gs)

            return gen()

        shape = (G * rows, cols)
        return (
            [(x.swapaxes(0, 1).reshape(S, G * rows, cols), VMEM)],
            [((S, rows, G * cols), x.dtype, ANY)],
            [VMEM(shape, x.dtype)]
            + scatter_scratch(sq, shape, x.dtype)
            + [VMEM((rows, G * cols), x.dtype)]
            + exchange_sems(zy)
            + gather_sems(sq),
            steps,
        )

    def op_scatter_gather(x):
        shape = x.shape[1:]

        def steps(ins, outs, scr):
            acc, sc, gs = scr[0], scr[1:7], scr[7:]

            def gen():
                yield from scatter_steps(zy, lambda o, i: ins[0].at[o * zy.ni + i], acc, *sc)
                yield from gather_steps(sq, acc, lambda o, i: outs[0].at[2 * o + i], *gs)

            return gen()

        return (
            [(x, VMEM)],
            [((S,) + shape, x.dtype, ANY)],
            [VMEM(shape, x.dtype)] + scatter_scratch(zy, shape, x.dtype) + gather_sems(sq),
            steps,
        )

    def op_small(x, own):
        r, q = x.shape[1], own.shape[0]

        def steps(ins, outs, scr):
            got, line = scr[0], scr[1]
            xs, gs = scr[2:5], scr[5:]

            def gen():
                yield from exchange_steps(
                    zy,
                    lambda o, i: ins[0].at[o * zy.ni + i],
                    lambda o, i: got.at[o * zy.ni + i],
                    *xs,
                )
                total = got[0]
                for k in range(1, G):
                    total = total + got[k]
                line[:r] = total
                line[r:] = ins[1][...]
                yield from gather_steps(sq, line, lambda o, i: outs[0].at[2 * o + i], *gs)

            return gen()

        return (
            [(x, VMEM), (own, VMEM)],
            [((S, r + q, 128), F32, ANY)],
            [VMEM(x.shape, F32), VMEM((r + q, 128), F32)] + exchange_sems(zy) + gather_sems(sq),
            steps,
        )

    def body(
        inputs,
        w_qkv,
        q_bias,
        v_bias,
        w_out,
        out_bias,
        gain_attn,
        shift_attn,
        w_fc,
        fc_bias,
        w_proj,
        proj_bias,
        gain_mlp,
        shift_mlp,
        cotangent,
    ):
        s = lax.axis_index("seq")
        place = lax.axis_index("ctx")
        rows_in = inputs[0]
        R = rows_in.shape[0]
        g_out = cotangent[0]
        vb = v_bias.shape[0]
        small = jnp.concatenate(
            [gain_attn, shift_attn, q_bias, out_bias, proj_bias, gain_mlp, shift_mlp]
            + [v_bias, jnp.zeros((256 - vb,), BF)]
        ).reshape(-1, 128)
        w_cols = jnp.concatenate(
            [
                lax.dynamic_slice_in_dim(w_qkv, s * QC, QC, 1),
                w_qkv[:, D:],
                lax.dynamic_slice_in_dim(w_out, s * QC, QC, 1),
            ],
            axis=1,
        )
        span, small_all, w_att, fc_cols, g_all = comm(
            "comm_entry",
            1,
            [zy, sq],
            [
                op_gather(sq, rows_in),
                op_gather(zy, small),
                op_gather(zy, w_cols),
                op_spread_fc(w_fc),
                op_gather(zy, g_out),
            ],
        )
        vecs = small_all[:, :14].reshape(G, 7, W).swapaxes(0, 1).reshape(7, D).astype(F32)
        gain_one, shift_one, qb, ob, pb, gain_two, shift_two = [vecs[k] for k in range(7)]
        vb_full = small_all[:, 14, :vb].reshape(-1).astype(F32)
        w_att = w_att.reshape(D, 2 * QC + 2 * HD)
        w_in = w_att[:, : QC + 2 * HD]
        w_back = w_att[:, QC + 2 * HD :]

        tokens = rows_in.astype(F32)
        _, norm_back = jax.vjp(layer_norm, tokens, gain_one, shift_one)
        span_rows = span.reshape(S * R, D).astype(F32)
        normed = layer_norm(span_rows, gain_one, shift_one).astype(BF)
        mixed = dot(normed, w_in)
        queries = (mixed[:, :QC] + lax.dynamic_slice_in_dim(qb, s * QC, QC, 0)).astype(BF)
        keyval = jnp.concatenate(
            [mixed[:, QC : QC + HD].astype(BF), (mixed[:, QC + HD :] + vb_full).astype(BF)], axis=1
        )
        (other,) = comm("comm_kv", 2, [yx], [op_pair(keyval)])
        other_first = place == 1
        T = S * R
        qblock = min(512, T)
        q3 = queries.reshape(T, QC // HD, HD)
        attended, logsums = attention_forward(q3, keyval, other, other_first, qblock)
        attended = attended.astype(BF).reshape(T, QC)
        (att_all,) = comm("comm_att", 3, [sq], [op_gather(sq, attended)])
        att_rows = att_all.swapaxes(0, 1).reshape(T, D)
        branch_cols = dot(att_rows, w_back).astype(BF)
        (branch_in,) = comm(
            "comm_branch", 4, [sq], [op_exchange(sq, branch_cols.reshape(S, R, QC))]
        )
        branch = branch_in.swapaxes(0, 1).reshape(R, D).astype(F32) + ob
        residual = tokens + branch
        normed_mlp = layer_norm(residual, gain_two, shift_two)
        (x_all,) = comm("comm_mlp", 5, [zy], [op_gather(zy, normed_mlp.astype(BF))])
        x_all = x_all.reshape(G * R, D)
        g_rows = g_all.reshape(G * R, D)
        fc = fc_cols.reshape(D, -1)
        ffl = fc.shape[1]
        hidden = dot(x_all, fc) + fc_bias.astype(F32)
        active, gelu_back = jax.vjp(gelu_tanh, hidden)
        active_low = active.astype(BF)
        y_part = dot(active_low, w_proj).astype(BF)
        grad_active = dot(g_rows, w_proj, ((1,), (1,)))
        grad_hidden = gelu_back(grad_active)[0].astype(BF)
        grad_fc_bias = jnp.sum(grad_hidden.astype(F32), axis=0)
        gx_part = dot(grad_hidden, fc, ((1,), (1,))).astype(BF)
        d_proj = dot(active_low, g_rows, ((0,), (0,))).astype(BF)
        d_fc = dot(x_all, grad_hidden, ((0,), (0,))).astype(BF)
        rows_d = (R, D)
        far_out = (ffl // S, D)

        def back_main(k):
            gx = scatter_steps(
                zy, lambda o, i: k["gx"].at[o * zy.ni + i], k["gx_sum"][0], *k["gx_s"]
            )
            yy = scatter_steps(zy, lambda o, i: k["y"].at[o * zy.ni + i], k["y_sum"], *k["y_s"])

            def sum_proj():
                acc = k["pj_acc"][0]
                yield from scatter_steps(
                    sq, lambda o, i: k["d_proj"].at[2 * o + i], acc, *k["pj_s"]
                )
                yield from gather_steps(
                    sq, acc, lambda o, i: k["d_proj_all"].at[2 * o + i], *k["pj_g"]
                )

            pj = sum_proj()
            step(gx)
            step(pj)
            step(yy)
            step(gx)
            step(pj)
            step(gx)
            step(pj)
            finish(gx)
            gain = k["vec"][0:1]
            stat = k["stat"]
            stat[...] = jnp.zeros(stat.shape, F32)

            def norm_back_rows(at):
                v = k["residual"][at]
                center = jnp.mean(v, axis=-1, keepdims=True)
                v = v - center
                scale = lax.rsqrt(jnp.mean(v * v, axis=-1, keepdims=True) + 1e-05)
                v = v * scale
                dn = k["gx_sum"][0][at]
                stat[0:1] += jnp.sum(dn * v, axis=0, keepdims=True)
                stat[1:2] += jnp.sum(dn, axis=0, keepdims=True)
                dn = dn * gain
                c1 = jnp.mean(dn, axis=-1, keepdims=True)
                c2 = jnp.mean(dn * v, axis=-1, keepdims=True)
                total = k["cot"][at].astype(F32) + scale * (dn - c1 - v * c2)
                stat[2:3] += jnp.sum(total, axis=0, keepdims=True)
                k["g_res"][at] = total
                k["gb"][0][at] = total.astype(BF)

            row_loop(R, norm_back_rows)
            gb = exchange_steps(
                sq,
                lambda o, i: k["gb"][0].at[:, cols(2 * o + i, QC)],
                lambda o, i: k["gbs"].at[cols(2 * o + i, R)],
                *k["gb_x"],
            )
            step(gb)
            step(pj)
            step(yy)
            finish(gb)
            ga = k["ga"][0]

            def back_cols(b, _):
                at = cols(b, QC)
                ga[b] = dot(k["gbs"][...], k["w_back"][at, :], ((1,), (1,))).astype(BF)
                return 0

            lax.fori_loop(0, S, back_cols, 0)
            at_ = scatter_steps(sq, lambda o, i: ga.at[2 * o + i], k["g_att"], *k["ga_s"])
            step(at_)
            step(yy)
            finish(at_)
            finish(yy, pj)

        b1 = fused(
            "back_one",
            6,
            [zy, sq],
            dict(
                gx=(gx_part.reshape(G, R, D), ANY),
                y=(y_part.reshape(G, R, D), ANY),
                d_proj=(d_proj.reshape((S,) + far_out), ANY),
                cot=(g_out, VMEM),
                residual=(residual, VMEM),
                vec=(gain_two[None], VMEM),
                w_back=(w_back, VMEM),
            ),
            dict(
                y_sum=(rows_d, F32, VMEM),
                d_proj_all=((S,) + far_out, BF, ANY),
                g_res=(rows_d, F32, VMEM),
                stat=((8, D), F32, VMEM),
                gbs=((T, QC), BF, VMEM),
                g_att=((T, QC), BF, VMEM),
            ),
            dict(
                gx_sum=[VMEM(rows_d, F32)],
                gx_s=scatter_scratch(zy, rows_d, BF),
                y_s=scatter_scratch(zy, rows_d, BF),
                pj_acc=[VMEM(far_out, BF)],
                pj_s=scatter_scratch(sq, far_out, BF),
                pj_g=gather_sems(sq),
                gb=[VMEM(rows_d, BF)],
                gb_x=exchange_sems(sq),
                ga=[VMEM((S, T, QC), BF)],
                ga_s=scatter_scratch(sq, (T, QC), BF),
            ),
            back_main,
        )
        d_proj_all = b1["d_proj_all"]
        output = residual + b1["y_sum"] + pb
        grad_output = g_out.astype(F32)
        grad_residual = b1["g_res"]
        grad_gain_mlp, grad_shift_mlp, grad_ob = [b1["stat"][r] for r in range(3)]
        gb = b1["gbs"]
        d_out = dot(att_rows, gb, ((0,), (0,)))
        g_att = b1["g_att"]
        g_att = g_att.reshape(T, QC // HD, HD)
        grad_q, grad_other, grad_own = attention_backward(
            q3, g_att, keyval, other, other_first, qblock, logsums
        )
        (grad_in,) = comm("comm_gkv", 9, [yx], [op_pair(grad_other.astype(BF))])
        grad_kv = (grad_own + grad_in.astype(F32)).astype(BF)
        grad_q = grad_q.astype(BF).reshape(T, QC)
        grad_mixed = jnp.concatenate([grad_q, grad_kv], axis=1)
        gn_part = dot(grad_mixed, w_in, ((1,), (1,))).astype(BF)
        d_in = dot(normed, grad_mixed, ((0,), (0,)))
        d_att = jnp.concatenate([d_in, d_out], axis=1).astype(BF)
        gn_sum, d_att_all, d_fc_all = comm(
            "comm_attn_back",
            10,
            [zy, sq],
            [
                op_scatter(sq, gn_part.reshape(S, R, D)),
                op_scatter_gather(d_att.reshape(G, W, 2 * QC + 2 * HD)),
                op_grad_fc(d_fc.reshape(G, S, W // S, ffl)),
            ],
        )
        grad_token_part, grad_gain_attn, grad_shift_attn = norm_back(gn_sum)
        input_grad = grad_residual + grad_token_part
        grad_qb = lax.dynamic_update_slice_in_dim(
            jnp.zeros((D,), F32), jnp.sum(grad_q.astype(F32), axis=0), s * QC, 0
        )
        grad_vb = jnp.sum(grad_kv[:, HD:].astype(F32), axis=0)
        terms = jnp.stack(
            [
                grad_qb,
                grad_ob,
                grad_gain_attn,
                grad_shift_attn,
                jnp.sum(grad_output, axis=0),
                grad_gain_mlp,
                grad_shift_mlp,
            ]
        )
        terms = terms.reshape(7, G, W).swapaxes(0, 1).reshape(G, 7 * W)
        tail = jnp.pad(grad_vb.reshape(G, vb), ((0, 0), (0, 256 - vb)))
        terms = jnp.concatenate([terms, tail], axis=1).reshape(G, -1, 128)
        (small_sum,) = comm(
            "comm_small", 11, [zy, sq], [op_small(terms, grad_fc_bias.reshape(-1, 128))]
        )
        sums = jnp.sum(small_sum, axis=0)
        v7 = sums[:14].reshape(7, W)
        d_att_f = d_att_all.astype(F32)
        grad_w_qkv = jnp.concatenate(
            [
                d_att_f[:, :, :QC].swapaxes(0, 1).reshape(W, D),
                jnp.sum(d_att_f[:, :, QC : QC + 2 * HD], axis=0),
            ],
            axis=1,
        )
        grad_w_out = d_att_f[:, :, QC + 2 * HD :].swapaxes(0, 1).reshape(W, D)
        return (
            output.astype(BF)[None],
            input_grad[None],
            grad_w_qkv,
            v7[0],
            sums[14, :vb],
            grad_w_out,
            v7[1],
            v7[2],
            v7[3],
            d_fc_all.reshape(W, -1).astype(F32),
            sums[16:].reshape(-1),
            d_proj_all.reshape(-1, D).astype(F32),
            v7[4],
            v7[5],
            v7[6],
        )

    return body


def solution(mesh):
    rows = P("batch", ("ctx", "seq"), None)
    mat = P(("batch", "ctx"), None)
    vec = P(("batch", "ctx"))
    in_specs = (rows, mat, vec, vec, mat, vec, vec, vec, mat, vec, mat, vec, vec, vec, rows)
    out_specs = (rows, rows, mat, vec, vec, mat, vec, vec, vec, mat, vec, mat, vec, vec, vec)
    return jax.shard_map(
        make_body(mesh), mesh=mesh, in_specs=in_specs, out_specs=out_specs, check_vma=False
    )
```

```python
import functools
import math

import jax
import jax.numpy as jnp
from jax import lax
from jax.experimental import pallas as pl
from jax.experimental.pallas import tpu as pltpu
from jax.sharding import PartitionSpec as P

D = 2048
HEADS = 16
HD = 128
MESH = pl.DeviceIdType.MESH
BF = jnp.bfloat16
F32 = jnp.float32
ANY = pl.ANY
VMEM = pltpu.VMEM
DMA = pltpu.SemaphoreType.DMA


class ZY:
    line = True

    def __init__(self, mesh):
        self.no, self.ni = mesh.shape["batch"], mesh.shape["ctx"]

    def me(self):
        return lax.axis_index("batch"), lax.axis_index("ctx")

    def dev(self, o, i):
        return {"batch": o, "ctx": i}


class SEQ:
    line = False

    def __init__(self, mesh):
        self.no, self.ni = mesh.shape["seq"] // 2, 2

    def me(self):
        s = lax.axis_index("seq")
        return s // 2, lax.rem(s, 2)

    def dev(self, o, i):
        return {"seq": 2 * o + i}


def rcopy(src, dst, ss, rs, dev):
    return pltpu.make_async_remote_copy(
        src_ref=src, dst_ref=dst, send_sem=ss, recv_sem=rs, device_id=dev, device_id_type=MESH
    )


def gather_steps(grp, src, view, ss, rs, ls):
    if grp.line:
        return line_gather_steps(grp, src, view, ss, rs, ls)
    return star_gather_steps(grp, src, view, ss, rs, ls)


def star_gather_steps(grp, src, view, ss, rs, ls):
    o, i = grp.me()
    no = grp.no
    mate = grp.dev(o, 1 - i)
    own = pltpu.make_async_copy(src, view(o, i), ls.at[0])
    own.start()
    sent = []
    for d in range(1, no):
        c = rcopy(src, view(o, i), ss.at[d], rs.at[d], grp.dev(lax.rem(o + d, no), i))
        c.start()
        sent.append(c)
    c = rcopy(src, view(o, i), ss.at[0], rs.at[0], mate)
    c.start()
    sent.append(c)
    yield
    for d in range(1, no):
        f = lax.rem(o - d + no, no)
        rcopy(view(f, i), view(f, i), ss.at[d], rs.at[d], mate).wait_recv()
        c = rcopy(view(f, i), view(f, i), ss.at[no + d - 1], rs.at[no + d - 1], mate)
        c.start()
        sent.append(c)
        yield
    rcopy(view(o, 1 - i), view(o, 1 - i), ss.at[0], rs.at[0], mate).wait_recv()
    for d in range(1, no):
        f = lax.rem(o - d + no, no)
        v = view(f, 1 - i)
        rcopy(v, v, ss.at[no + d - 1], rs.at[no + d - 1], mate).wait_recv()
    for c in sent:
        c.wait_send()
    own.wait()


def gather_sems(grp):
    if grp.line:
        return line_gather_sems(grp)
    n = 2 * grp.no - 1
    return [DMA((n,)), DMA((n,)), DMA((1,))]


def add_all(dst, refs, rows, step=16):
    if len(dst.shape) == 3:
        for b in range(dst.shape[0]):
            add_all(dst.at[b], [ref.at[b] for ref in refs], dst.shape[1], step)
        return

    def one(r, _):
        at = pl.ds(pl.multiple_of(r * step, step), step)
        total = refs[0][at].astype(F32)
        for ref in refs[1:]:
            total = total + ref[at].astype(F32)
        dst[at] = total.astype(dst.dtype)
        return 0

    lax.fori_loop(0, rows // step, one, 0)


def scatter_steps(grp, part, out, *scr):
    if grp.line:
        return line_scatter_steps(grp, part, out, *scr)
    return star_scatter_steps(grp, part, out, *scr)


def star_scatter_steps(grp, part, out, near, mid, far, ss, rs, ls):
    o, i = grp.me()
    no = grp.no
    mate = grp.dev(o, 1 - i)
    sent, own = [], []
    order = list(range(1, no)) + [0]
    rows = out.shape[0]
    for d in order:
        t = lax.rem(o + d, no)
        c = rcopy(part(t, 1 - i), near.at[d], ss.at[d], rs.at[d], mate)
        c.start()
        sent.append(c)
        c = pltpu.make_async_copy(part(t, i), mid.at[d], ls.at[d])
        c.start()
        own.append(c)
    yield
    for c, d in zip(own, order):
        t = lax.rem(o + d, no)
        c.wait()
        rcopy(near.at[d], near.at[d], ss.at[d], rs.at[d], mate).wait_recv()
        if d == 0:
            add_all(out, [mid.at[d], near.at[d]], rows)
        else:
            add_all(mid.at[d], [mid.at[d], near.at[d]], rows)
            c = rcopy(
                mid.at[d], far.at[d - 1], ss.at[no + d - 1], rs.at[no + d - 1], grp.dev(t, i)
            )
            c.start()
            sent.append(c)
            yield
    yield
    for d in range(1, no):
        v = far.at[d - 1]
        rcopy(v, v, ss.at[no + d - 1], rs.at[no + d - 1], mate).wait_recv()
        add_all(out, [out, v], rows)
    for c in sent:
        c.wait_send()


def scatter_scratch(grp, shape, dtype):
    no = grp.no
    if grp.line:
        return [
            VMEM((no,) + shape, dtype),
            VMEM((no,) + shape, dtype),
            VMEM((no + 1,) + shape, dtype),
            DMA((2 * no - 1,)),
            DMA((2 * no + 1,)),
            DMA((no,)),
        ]
    n = 2 * no - 1
    return [
        VMEM((no,) + shape, dtype),
        VMEM((no,) + shape, dtype),
        VMEM((no - 1,) + shape, dtype),
        DMA((n,)),
        DMA((n,)),
        DMA((no,)),
    ]


def line_gather_steps(grp, src, view, ss, rs, ls):
    o, i = grp.me()
    n = grp.no
    mate, right, left = grp.dev(o, 1 - i), grp.dev(o + 1, i), grp.dev(o - 1, i)
    own = pltpu.make_async_copy(src, view(o, i), ls.at[0])
    own.start()
    sent = []

    def send(pred, ref, dst, k, to):
        def copy():
            return rcopy(ref, dst, ss.at[k], rs.at[k], to)

        pl.when(pred)(lambda: copy().start())
        sent.append((pred, copy))

    def got(v, k):
        rcopy(v, v, ss.at[k], rs.at[k], mate).wait_recv()

    R, L, Y = -1, n - 2, 2 * n - 2
    send(o < n - 1, src, view(o, i), R + 1, right)
    send(o > 0, src, view(o, i), L + 1, left)
    c = rcopy(src, view(o, i), ss.at[Y], rs.at[Y], mate)
    c.start()
    yield
    for k in range(1, n):
        a, b = lax.max(o - k, 0), lax.min(o + k, n - 1)
        from_left, from_right = o >= k, o + k <= n - 1
        pl.when(from_left)(lambda: got(view(a, i), R + k))
        if k < n - 1:
            send(from_left & (o < n - 1), view(a, i), view(a, i), R + k + 1, right)
        send(from_left, view(a, i), view(a, i), Y + k, mate)
        pl.when(from_right)(lambda: got(view(b, i), L + k))
        if k < n - 1:
            send(from_right & (o > 0), view(b, i), view(b, i), L + k + 1, left)
        send(from_right, view(b, i), view(b, i), Y + n - 1 + k, mate)
        yield
    got(view(o, 1 - i), Y)
    for k in range(1, n):
        a, b = lax.max(o - k, 0), lax.min(o + k, n - 1)
        pl.when(o >= k)(lambda: got(view(a, 1 - i), Y + k))
        pl.when(o + k <= n - 1)(lambda: got(view(b, 1 - i), Y + n - 1 + k))
    for pred, copy in sent:
        pl.when(pred)(lambda: copy().wait_send())
    c.wait_send()
    own.wait()


def line_gather_sems(grp):
    n = 4 * grp.no - 3
    return [DMA((n,)), DMA((n,)), DMA((1,))]


def line_scatter_steps(grp, part, out, near, mid, far, ss, rs, ls):
    o, i = grp.me()
    n = grp.no
    mate = grp.dev(o, 1 - i)
    rows = out.shape[0]
    low = o < n // 2

    def target(j):
        if j == n - 1:
            return o
        down = jnp.where(n - 1 - j > o, n - 1 - j, n - 2 - j)
        up = jnp.where(j < o, j, j + 1)
        return jnp.where(low, down, up)

    sent, own = [], []
    for j in range(n):
        c = rcopy(part(target(j), 1 - i), near.at[j], ss.at[j], rs.at[j], mate)
        c.start()
        sent.append(c)
        c = pltpu.make_async_copy(part(target(j), i), mid.at[j], ls.at[j])
        c.start()
        own.append(c)
    yield
    moved = []
    for j in range(n - 1):
        t = target(j)
        own[j].wait()
        rcopy(near.at[j], near.at[j], ss.at[j], rs.at[j], mate).wait_recv()
        for right in (True, False):
            towards = (t > o) if right else (t < o)
            inner = (o > 0) if right else (o < n - 1)
            slot = t if right else jnp.where(t == o - 1, n, t)
            to = grp.dev(o + 1, i) if right else grp.dev(o - 1, i)

            def copy(j=j, slot=slot, to=to):
                return rcopy(mid.at[j], far.at[slot], ss.at[n + j], rs.at[n + slot], to)

            @pl.when(towards & inner)
            def _():
                rcopy(far.at[t], far.at[t], ss.at[n + j], rs.at[n + t], mate).wait_recv()
                add_all(mid.at[j], [mid.at[j], near.at[j], far.at[t]], rows)

            @pl.when(towards & jnp.logical_not(inner))
            def _():
                add_all(mid.at[j], [mid.at[j], near.at[j]], rows)

            pl.when(towards)(lambda: copy().start())
            moved.append((towards, copy))
        yield
    j = n - 1
    own[j].wait()
    rcopy(near.at[j], near.at[j], ss.at[j], rs.at[j], mate).wait_recv()

    def arrived(k):
        rcopy(far.at[k], far.at[k], ss.at[j], rs.at[n + k], mate).wait_recv()

    pl.when(o > 0)(lambda: arrived(o))
    pl.when(o < n - 1)(lambda: arrived(n))
    mine = [mid.at[j], near.at[j]]
    inside = (o > 0) & (o < n - 1)
    pl.when(inside)(lambda: add_all(out, mine + [far.at[o], far.at[n]], rows))
    pl.when(o == 0)(lambda: add_all(out, mine + [far.at[n]], rows))
    pl.when(o == n - 1)(lambda: add_all(out, mine + [far.at[o]], rows))
    for c in sent:
        c.wait_send()
    for pred, copy in moved:
        pl.when(pred)(lambda: copy().wait_send())


def exchange_steps(grp, src, dst, ss, rs, ls):
    o, i = grp.me()
    no, ni = grp.no, grp.ni
    sent = []
    own = pltpu.make_async_copy(src(o, i), dst(o, i), ls.at[0])
    own.start()
    for a in range(no):
        for b in range(ni):
            if a == 0 and b == 0:
                continue
            to, ti = lax.rem(o + a, no), lax.rem(i + b, ni)
            k = a * ni + b - 1
            c = rcopy(src(to, ti), dst(o, i), ss.at[k], rs.at[k], grp.dev(to, ti))
            c.start()
            sent.append(c)
    yield
    for a in range(no):
        for b in range(ni):
            if a == 0 and b == 0:
                continue
            fo, fi = lax.rem(o - a + no, no), lax.rem(i - b + ni, ni)
            k = a * ni + b - 1
            v = dst(fo, fi)
            rcopy(v, v, ss.at[k], rs.at[k], grp.dev(fo, fi)).wait_recv()
    for c in sent:
        c.wait_send()
    own.wait()


def exchange_sems(grp):
    n = grp.no * grp.ni - 1
    return [DMA((n,)), DMA((n,)), DMA((1,))]


def barrier(groups):
    sem = pltpu.get_barrier_semaphore()
    count = 0
    for grp in groups:
        o, i = grp.me()
        for a in range(grp.no):
            for b in range(grp.ni):
                if a == 0 and b == 0:
                    continue
                to, ti = lax.rem(o + a, grp.no), lax.rem(i + b, grp.ni)
                pl.semaphore_signal(sem, inc=1, device_id=grp.dev(to, ti), device_id_type=MESH)
                count += 1
    pl.semaphore_wait(sem, count)


def run_all(gens):
    live = list(gens)
    while live:
        left = []
        for g in live:
            try:
                next(g)
                left.append(g)
            except StopIteration:
                pass
        live = left


def comm(name, ident, groups, ops, ici=0):
    arrays, in_specs, out_shapes, out_specs, scratch, cuts = [], [], [], [], [], []
    for ins, outs, scr, steps in ops:
        cuts.append((len(ins), len(outs), len(scr), steps))
        for a, space in ins:
            arrays.append(a)
            in_specs.append(pl.BlockSpec(memory_space=space))
        for shape, dtype, space in outs:
            out_shapes.append(jax.ShapeDtypeStruct(shape, dtype))
            out_specs.append(pl.BlockSpec(memory_space=space))
        scratch.extend(scr)

    def kernel(*refs):
        barrier(groups)
        a, b, c = 0, len(arrays), len(arrays) + len(out_shapes)
        gens = []
        for ni, no, ns, steps in cuts:
            gens.append(steps(refs[a : a + ni], refs[b : b + no], refs[c : c + ns]))
            a, b, c = a + ni, b + no, c + ns
        run_all(gens)

    return pl.pallas_call(
        kernel,
        out_shape=out_shapes,
        in_specs=in_specs,
        out_specs=out_specs,
        scratch_shapes=scratch,
        compiler_params=pltpu.CompilerParams(
            collective_id=ident, has_side_effects=True, vmem_limit_bytes=63 * 1024 * 1024
        ),
        name=name,
    )(*arrays)


def fused(name, ident, groups, ins, outs, scratch, main):
    keys = list(ins) + list(outs)
    in_specs = [pl.BlockSpec(memory_space=space) for _, space in ins.values()]
    out_specs = [pl.BlockSpec(memory_space=space) for _, _, space in outs.values()]
    out_shapes = [jax.ShapeDtypeStruct(shape, dtype) for shape, dtype, _ in outs.values()]
    flat = [x for group in scratch.values() for x in group]

    def kernel(*refs):
        named = dict(zip(keys, refs))
        at = len(keys)
        for key, group in scratch.items():
            named[key] = refs[at : at + len(group)]
            at += len(group)
        barrier(groups)
        main(named)

    got = pl.pallas_call(
        kernel,
        out_shape=out_shapes,
        in_specs=in_specs,
        out_specs=out_specs,
        scratch_shapes=flat,
        compiler_params=pltpu.CompilerParams(
            collective_id=ident, has_side_effects=True, vmem_limit_bytes=63 * 1024 * 1024
        ),
        name=name,
    )(*[a for a, _ in ins.values()])
    return dict(zip(outs, got))


def step(gen):
    next(gen, None)


def finish(*gens):
    run_all(gens)


def row_loop(rows, fn, size=16):
    def one(r, _):
        fn(pl.ds(pl.multiple_of(r * size, size), size))
        return 0

    lax.fori_loop(0, rows // size, one, 0)


def cols(k, width):
    return pl.ds(pl.multiple_of(k * width, width), width)


def op_gather(grp, x):
    shape = (grp.no * grp.ni,) + x.shape

    def steps(ins, outs, scr):
        return gather_steps(grp, ins[0], lambda o, i: outs[0].at[o * grp.ni + i], *scr)

    return ([(x, VMEM)], [(shape, x.dtype, ANY)], gather_sems(grp), steps)


def op_scatter(grp, x, dtype=F32):
    shape = x.shape[1:]

    def steps(ins, outs, scr):
        return scatter_steps(grp, lambda o, i: ins[0].at[o * grp.ni + i], outs[0], *scr)

    return ([(x, VMEM)], [(shape, dtype, VMEM)], scatter_scratch(grp, shape, x.dtype), steps)


def op_exchange(grp, x, space=ANY):
    def steps(ins, outs, scr):
        return exchange_steps(
            grp,
            lambda o, i: ins[0].at[o * grp.ni + i],
            lambda o, i: outs[0].at[o * grp.ni + i],
            *scr,
        )

    return ([(x, VMEM)], [(x.shape, x.dtype, space)], exchange_sems(grp), steps)


def layer_norm(values, gain_vec, shift_vec):
    center = jnp.mean(values, axis=-1, keepdims=True)
    centred = values - center
    spread = jnp.mean(centred * centred, axis=-1, keepdims=True)
    return centred * lax.rsqrt(spread + 1e-05) * gain_vec + shift_vec


def gelu_tanh(values):
    return (
        0.5
        * values
        * (
            1.0
            + jnp.tanh(math.sqrt(2.0 / math.pi) * (values + 0.044715 * values * values * values))
        )
    )


def allowed_mask(other_first, first_row, qblock, ctx_len, key_span):
    piece = jnp.broadcast_to(other_first, (qblock, ctx_len))
    query_pos = first_row + jnp.arange(qblock)[:, None]
    key_pos = jnp.arange(key_span)[None, :]
    return jnp.concatenate([piece, key_pos <= query_pos], axis=1)


def block_scores(block_queries, keyval, allowed):
    score_scale = 1.0 / math.sqrt(HD)
    raw_scores = jnp.einsum(
        "qhd,kd->hqk", block_queries, keyval[:, :HD], preferred_element_type=F32
    )
    return jnp.where(allowed[None], raw_scores * score_scale, -1e30)


def attention_forward(queries, own_rows, other_rows, other_first, qblock):
    ctx_len = own_rows.shape[0]
    outputs = []
    logsums = []
    for block_index in range(ctx_len // qblock):
        first_row = block_index * qblock
        key_span = first_row + qblock
        keyval = jnp.concatenate([other_rows, own_rows[:key_span]], axis=0)
        allowed = allowed_mask(other_first, first_row, qblock, ctx_len, key_span)
        masked = block_scores(queries[first_row:key_span], keyval, allowed)
        maxima = jnp.max(masked, axis=-1, keepdims=True)
        shifted = jnp.exp(masked - maxima)
        totals = jnp.sum(shifted, axis=-1, keepdims=True)
        weights = (shifted / totals).astype(BF)
        outputs.append(
            jnp.einsum("hqk,kd->qhd", weights, keyval[:, HD:], preferred_element_type=F32)
        )
        logsums.append(maxima + jnp.log(totals))
    return (jnp.concatenate(outputs, axis=0), logsums)


def dot(a, b, dims=((1,), (0,))):
    return lax.dot_general(a, b, (dims, ((), ())), preferred_element_type=F32)


def make_body(mesh):
    zy, sq = ZY(mesh), SEQ(mesh)
    S = mesh.shape["seq"]
    G = mesh.shape["batch"] * mesh.shape["ctx"]
    W = D // G
    QC = (HEADS // S) * HD

    class CTX:
        no, ni = 1, 2

        def me(self):
            return 0, lax.axis_index("ctx")

        def dev(self, o, i):
            return {"ctx": i}

    yx = CTX()

    def op_pair(x):
        def steps(ins, outs, scr):
            def gen():
                o, i = yx.me()
                c = rcopy(ins[0], outs[0], scr[0].at[0], scr[1].at[0], yx.dev(o, 1 - i))
                c.start()
                yield
                c.wait()

            return gen()

        return ([(x, VMEM)], [(x.shape, x.dtype, VMEM)], [DMA((1,)), DMA((1,))], steps)

    def op_spread_fc(w):
        rows, cols = W // S, w.shape[1] // G

        def steps(ins, outs, scr):
            src, out = ins[0], outs[0]
            xs, gs = scr[:3], scr[3:]
            s = lax.axis_index("seq")

            def gen():
                yield from exchange_steps(
                    zy,
                    lambda o, i: src.at[
                        pl.ds(pl.multiple_of(s * rows, rows), rows),
                        pl.ds(pl.multiple_of((o * zy.ni + i) * cols, cols), cols),
                    ],
                    lambda o, i: out.at[o * zy.ni + i, s],
                    *xs,
                )
                yield from gather_steps_inplace(sq, lambda o, i: out.at[:, 2 * o + i], *gs)

            return gen()

        return (
            [(w, VMEM)],
            [((G, S, rows, cols), w.dtype, ANY)],
            exchange_sems(zy) + gather_sems(sq)[:2],
            steps,
        )

    def gather_steps_inplace(grp, view, ss, rs):
        o, i = grp.me()
        no = grp.no
        mate = grp.dev(o, 1 - i)
        sent = []
        for d in list(range(1, no)) + [0]:
            to = grp.dev(lax.rem(o + d, no), i) if d else mate
            c = rcopy(view(o, i), view(o, i), ss.at[d], rs.at[d], to)
            c.start()
            sent.append(c)
        yield
        for d in range(1, no):
            v = view(lax.rem(o - d + no, no), i)
            rcopy(v, v, ss.at[d], rs.at[d], mate).wait_recv()
            c = rcopy(v, v, ss.at[no + d - 1], rs.at[no + d - 1], mate)
            c.start()
            sent.append(c)
        yield
        v = view(o, 1 - i)
        rcopy(v, v, ss.at[0], rs.at[0], mate).wait_recv()
        for d in range(1, no):
            v = view(lax.rem(o - d + no, no), 1 - i)
            rcopy(v, v, ss.at[no + d - 1], rs.at[no + d - 1], mate).wait_recv()
        for c in sent:
            c.wait_send()

    def op_sum_all(grp, x):
        shape = x.shape[1:]

        def steps(ins, outs, scr):
            acc, sc, gs = scr[0], scr[1:7], scr[7:]

            def gen():
                yield from scatter_steps(
                    grp, lambda o, i: ins[0].at[o * grp.ni + i], acc, *sc
                )
                yield from gather_steps(
                    grp, acc, lambda o, i: outs[0].at[o * grp.ni + i], *gs
                )

            return gen()

        return (
            [(x, VMEM)],
            [(x.shape, x.dtype, ANY)],
            [VMEM(shape, x.dtype)] + scatter_scratch(grp, shape, x.dtype) + gather_sems(grp),
            steps,
        )

    def op_grad_fc(x):
        rows, cols = x.shape[2:]

        def steps(ins, outs, scr):
            acc, sc, line, xs, gs = scr[0], scr[1:7], scr[7], scr[8:11], scr[11:]

            def gen():
                src = ins[0]
                yield from scatter_steps(
                    sq,
                    lambda o, i: src.at[2 * o + i],
                    acc,
                    *sc,
                )
                yield from exchange_steps(
                    zy,
                    lambda o, i: acc.at[pl.ds(pl.multiple_of((o * zy.ni + i) * rows, rows), rows)],
                    lambda o, i: line.at[
                        :, pl.ds(pl.multiple_of((o * zy.ni + i) * cols, cols), cols)
                    ],
                    *xs,
                )
                yield from gather_steps(sq, line, lambda o, i: outs[0].at[2 * o + i], *gs)

            return gen()

        shape = (G * rows, cols)
        return (
            [(x.swapaxes(0, 1).reshape(S, G * rows, cols), VMEM)],
            [((S, rows, G * cols), x.dtype, ANY)],
            [VMEM(shape, x.dtype)]
            + scatter_scratch(sq, shape, x.dtype)
            + [VMEM((rows, G * cols), x.dtype)]
            + exchange_sems(zy)
            + gather_sems(sq),
            steps,
        )

    def op_scatter_gather(x):
        shape = x.shape[1:]

        def steps(ins, outs, scr):
            acc, sc, gs = scr[0], scr[1:7], scr[7:]

            def gen():
                yield from scatter_steps(zy, lambda o, i: ins[0].at[o * zy.ni + i], acc, *sc)
                yield from gather_steps(sq, acc, lambda o, i: outs[0].at[2 * o + i], *gs)

            return gen()

        return (
            [(x, VMEM)],
            [((S,) + shape, x.dtype, ANY)],
            [VMEM(shape, x.dtype)] + scatter_scratch(zy, shape, x.dtype) + gather_sems(sq),
            steps,
        )

    def op_small(x, own):
        r, q = x.shape[1], own.shape[0]

        def steps(ins, outs, scr):
            got, line = scr[0], scr[1]
            xs, gs = scr[2:5], scr[5:]

            def gen():
                yield from exchange_steps(
                    zy,
                    lambda o, i: ins[0].at[o * zy.ni + i],
                    lambda o, i: got.at[o * zy.ni + i],
                    *xs,
                )
                total = got[0]
                for k in range(1, G):
                    total = total + got[k]
                line[:r] = total
                line[r:] = ins[1][...]
                yield from gather_steps(sq, line, lambda o, i: outs[0].at[2 * o + i], *gs)

            return gen()

        return (
            [(x, VMEM), (own, VMEM)],
            [((S, r + q, 128), F32, ANY)],
            [VMEM(x.shape, F32), VMEM((r + q, 128), F32)] + exchange_sems(zy) + gather_sems(sq),
            steps,
        )

    def body(
        inputs,
        w_qkv,
        q_bias,
        v_bias,
        w_out,
        out_bias,
        gain_attn,
        shift_attn,
        w_fc,
        fc_bias,
        w_proj,
        proj_bias,
        gain_mlp,
        shift_mlp,
        cotangent,
    ):
        s = lax.axis_index("seq")
        place = lax.axis_index("ctx")
        rows_in = inputs[0]
        R = rows_in.shape[0]
        g_out = cotangent[0]
        vb = v_bias.shape[0]
        small = jnp.concatenate(
            [gain_attn, shift_attn, q_bias, out_bias, proj_bias, gain_mlp, shift_mlp]
            + [v_bias, jnp.zeros((256 - vb,), BF)]
        ).reshape(-1, 128)
        w_cols = jnp.concatenate(
            [
                lax.dynamic_slice_in_dim(w_qkv, s * QC, QC, 1),
                w_qkv[:, D:],
                lax.dynamic_slice_in_dim(w_out, s * QC, QC, 1),
            ],
            axis=1,
        )
        span, small_all, w_att, fc_cols, g_all = comm(
            "comm_entry",
            1,
            [zy, sq],
            [
                op_gather(sq, rows_in),
                op_gather(zy, small),
                op_gather(zy, w_cols),
                op_spread_fc(w_fc),
                op_gather(zy, g_out),
            ],
        )
        vecs = small_all[:, :14].reshape(G, 7, W).swapaxes(0, 1).reshape(7, D).astype(F32)
        gain_one, shift_one, qb, ob, pb, gain_two, shift_two = [vecs[k] for k in range(7)]
        vb_full = small_all[:, 14, :vb].reshape(-1).astype(F32)
        w_att = w_att.reshape(D, 2 * QC + 2 * HD)
        w_in = w_att[:, : QC + 2 * HD]
        w_back = w_att[:, QC + 2 * HD :]

        tokens = rows_in.astype(F32)
        span_rows = span.reshape(S * R, D).astype(F32)
        normed = layer_norm(span_rows, gain_one, shift_one).astype(BF)
        mixed = dot(normed, w_in)
        queries = (mixed[:, :QC] + lax.dynamic_slice_in_dim(qb, s * QC, QC, 0)).astype(BF)
        keyval = jnp.concatenate(
            [mixed[:, QC : QC + HD].astype(BF), (mixed[:, QC + HD :] + vb_full).astype(BF)], axis=1
        )
        (other,) = comm("comm_kv", 2, [yx], [op_pair(keyval)])
        other_first = place == 1
        T = S * R
        qblock = min(512, T)
        q3 = queries.reshape(T, QC // HD, HD)
        attended, logsums = attention_forward(q3, keyval, other, other_first, qblock)
        attended = attended.astype(BF).reshape(T, QC)
        (att_all,) = comm("comm_att", 3, [sq], [op_gather(sq, attended)])
        att_rows = att_all.swapaxes(0, 1).reshape(T, D)
        branch_cols = dot(att_rows, w_back).astype(BF)
        (branch_in,) = comm(
            "comm_branch", 4, [sq], [op_exchange(sq, branch_cols.reshape(S, R, QC))]
        )
        branch = branch_in.swapaxes(0, 1).reshape(R, D).astype(F32) + ob
        residual = tokens + branch
        normed_mlp = layer_norm(residual, gain_two, shift_two)
        (x_all,) = comm("comm_mlp", 5, [zy], [op_gather(zy, normed_mlp.astype(BF))])
        x_all = x_all.reshape(G * R, D)
        g_rows = g_all.reshape(G * R, D)
        fc = fc_cols.reshape(D, -1)
        ffl = fc.shape[1]
        hidden = dot(x_all, fc) + fc_bias.astype(F32)
        active, gelu_back = jax.vjp(gelu_tanh, hidden)
        active_low = active.astype(BF)
        y_part = dot(active_low, w_proj).astype(BF)
        grad_active = dot(g_rows, w_proj, ((1,), (1,)))
        grad_hidden = gelu_back(grad_active)[0].astype(BF)
        grad_fc_bias = jnp.sum(grad_hidden.astype(F32), axis=0)
        gx_part = dot(grad_hidden, fc, ((1,), (1,))).astype(BF)
        d_proj = dot(active_low, g_rows, ((0,), (0,))).astype(BF)
        d_fc = dot(x_all, grad_hidden, ((0,), (0,))).astype(BF)
        rows_d = (R, D)
        far_out = (ffl // S, D)

        def back_main(k):
            gx = scatter_steps(
                zy, lambda o, i: k["gx"].at[o * zy.ni + i], k["gx_sum"][0], *k["gx_s"]
            )
            yy = scatter_steps(zy, lambda o, i: k["y"].at[o * zy.ni + i], k["y_sum"], *k["y_s"])

            def sum_proj():
                acc = k["pj_acc"][0]
                yield from scatter_steps(
                    sq, lambda o, i: k["d_proj"].at[2 * o + i], acc, *k["pj_s"]
                )
                yield from gather_steps(
                    sq, acc, lambda o, i: k["d_proj_all"].at[2 * o + i], *k["pj_g"]
                )

            pj = sum_proj()
            step(gx)
            step(pj)
            step(yy)
            step(gx)
            step(pj)
            step(gx)
            step(pj)
            finish(gx)
            gain = k["vec"][0:1]
            stat = k["stat"]
            stat[...] = jnp.zeros(stat.shape, F32)

            def norm_back_rows(at):
                v = k["residual"][at]
                center = jnp.mean(v, axis=-1, keepdims=True)
                v = v - center
                scale = lax.rsqrt(jnp.mean(v * v, axis=-1, keepdims=True) + 1e-05)
                v = v * scale
                dn = k["gx_sum"][0][at]
                stat[0:1] += jnp.sum(dn * v, axis=0, keepdims=True)
                stat[1:2] += jnp.sum(dn, axis=0, keepdims=True)
                dn = dn * gain
                c1 = jnp.mean(dn, axis=-1, keepdims=True)
                c2 = jnp.mean(dn * v, axis=-1, keepdims=True)
                total = k["cot"][at].astype(F32) + scale * (dn - c1 - v * c2)
                stat[2:3] += jnp.sum(total, axis=0, keepdims=True)
                k["g_res"][at] = total
                k["gb"][0][at] = total.astype(BF)

            row_loop(R, norm_back_rows)
            gb = exchange_steps(
                sq,
                lambda o, i: k["gb"][0].at[:, cols(2 * o + i, QC)],
                lambda o, i: k["gbs"].at[cols(2 * o + i, R)],
                *k["gb_x"],
            )
            step(gb)
            step(pj)
            step(yy)
            finish(gb)
            ga = k["ga"][0]

            def back_cols(b, _):
                at = cols(b, QC)
                ga[b] = dot(k["gbs"][...], k["w_back"][at, :], ((1,), (1,))).astype(BF)
                return 0

            lax.fori_loop(0, S, back_cols, 0)
            at_ = scatter_steps(sq, lambda o, i: ga.at[2 * o + i], k["g_att"], *k["ga_s"])
            step(at_)
            step(yy)
            finish(at_)
            finish(yy, pj)

        b1 = fused(
            "back_one",
            6,
            [zy, sq],
            dict(
                gx=(gx_part.reshape(G, R, D), ANY),
                y=(y_part.reshape(G, R, D), ANY),
                d_proj=(d_proj.reshape((S,) + far_out), ANY),
                cot=(g_out, VMEM),
                residual=(residual, VMEM),
                vec=(gain_two[None], VMEM),
                w_back=(w_back, VMEM),
            ),
            dict(
                y_sum=(rows_d, F32, VMEM),
                d_proj_all=((S,) + far_out, BF, ANY),
                g_res=(rows_d, F32, VMEM),
                stat=((8, D), F32, VMEM),
                gbs=((T, QC), BF, VMEM),
                g_att=((T, QC), BF, VMEM),
            ),
            dict(
                gx_sum=[VMEM(rows_d, F32)],
                gx_s=scatter_scratch(zy, rows_d, BF),
                y_s=scatter_scratch(zy, rows_d, BF),
                pj_acc=[VMEM(far_out, BF)],
                pj_s=scatter_scratch(sq, far_out, BF),
                pj_g=gather_sems(sq),
                gb=[VMEM(rows_d, BF)],
                gb_x=exchange_sems(sq),
                ga=[VMEM((S, T, QC), BF)],
                ga_s=scatter_scratch(sq, (T, QC), BF),
            ),
            back_main,
        )
        d_proj_all = b1["d_proj_all"]
        output = residual + b1["y_sum"] + pb
        grad_output = g_out.astype(F32)
        grad_residual = b1["g_res"]
        gb = b1["gbs"]
        d_out = dot(att_rows, gb, ((0,), (0,))).astype(BF)
        NQ = min(256, T)
        NB = (QC // HD) * (T // NQ)
        score_scale = 1.0 / math.sqrt(HD)

        def back_two_main(k):
            fcg = grad_fc(k)
            og = scatter_steps(zy, lambda o, i: k["d_out"].at[o * zy.ni + i], k["o_acc"][0], *k["o_s"])
            step(og)
            step(fcg)
            own, oth = k["dkv_own"][0], k["dkv_oth"][0]
            own[...] = jnp.zeros(own.shape, F32)
            oth[...] = jnp.zeros(oth.shape, F32)
            far_bias = (1 - lax.axis_index("ctx")).astype(F32) * -1e30

            def attend_back(n, _):
                h, first = n // (T // NQ), lax.rem(n, T // NQ) * NQ
                at = pl.ds(pl.multiple_of(first, NQ), NQ)
                hc = cols(h, HD)
                q, g = k["q"][at, hc], k["g_att"][at, hc]
                kv0, kv1 = k["kv"], k["other"]
                s0 = dot(q, kv0[:, :HD], ((1,), (1,))) * score_scale
                s1 = dot(q, kv1[:, :HD], ((1,), (1,))) * score_scale + far_bias
                qpos = first + lax.broadcasted_iota(jnp.int32, s0.shape, 0)
                kpos = lax.broadcasted_iota(jnp.int32, s0.shape, 1)
                s0 = jnp.where(kpos <= qpos, s0, -1e30)
                top = jnp.maximum(
                    jnp.max(s0, axis=-1, keepdims=True), jnp.max(s1, axis=-1, keepdims=True)
                )
                p0, p1 = jnp.exp(s0 - top), jnp.exp(s1 - top)
                total = jnp.sum(p0, axis=-1, keepdims=True) + jnp.sum(p1, axis=-1, keepdims=True)
                inv = 1.0 / total
                p0, p1 = p0 * inv, p1 * inv
                own[:, HD:] += dot(p0.astype(BF), g, ((0,), (0,)))
                oth[:, HD:] += dot(p1.astype(BF), g, ((0,), (0,)))
                e0 = dot(g, kv0[:, HD:], ((1,), (1,)))
                e1 = dot(g, kv1[:, HD:], ((1,), (1,)))
                inner = jnp.sum(p0 * e0, axis=-1, keepdims=True) + jnp.sum(
                    p1 * e1, axis=-1, keepdims=True
                )
                d0 = (p0 * (e0 - inner) * score_scale).astype(BF)
                d1 = (p1 * (e1 - inner) * score_scale).astype(BF)
                own[:, :HD] += dot(d0, q, ((0,), (0,)))
                oth[:, :HD] += dot(d1, q, ((0,), (0,)))
                k["gq"][0][at, hc] = (dot(d0, kv0[:, :HD]) + dot(d1, kv1[:, :HD])).astype(BF)
                return 0

            cuts = [0, NB // 2, NB]
            for lo, hi in zip(cuts[:-1], cuts[1:]):
                lax.fori_loop(lo, hi, attend_back, 0)
                step(og)
                step(fcg)
            c = lax.axis_index("ctx")
            k["gkv_out"][0][...] = oth[...].astype(BF)
            swap = rcopy(
                k["gkv_out"][0],
                k["gkv_in"][0],
                k["swap"][0].at[0],
                k["swap"][1].at[0],
                {"ctx": 1 - c},
            )
            swap.start()
            gq, dq = k["gq"][0], k["dq"][0]

            def weight_q(b, _):
                dq[b] = dot(k["normed"][:, cols(b, W)], gq[...], ((0,), (0,))).astype(BF)
                return 0

            lax.fori_loop(0, G, weight_q, 0)
            qg = scatter_steps(zy, lambda o, i: dq.at[o * zy.ni + i], k["q_acc"][0], *k["q_s"])
            step(og)
            step(qg)
            swap.wait()
            gkv = k["gkv"][0]
            gkv[...] = (own[...] + k["gkv_in"][0][...].astype(F32)).astype(BF)
            gn = k["gn"][0]

            def back_in(b, _):
                at = cols(b, R)
                gn[b] = (
                    dot(gq[at], k["w_in"][:, :QC], ((1,), (1,)))
                    + dot(gkv[at], k["w_in"][:, QC:], ((1,), (1,)))
                ).astype(BF)
                return 0

            lax.fori_loop(0, S, back_in, 0)
            gng = scatter_steps(sq, lambda o, i: gn.at[2 * o + i], k["gn_sum"][0], *k["gn_s"])
            step(gng)
            dkv = k["dkv"][0]

            def weight_kv(b, _):
                dkv[b] = dot(k["normed"][:, cols(b, W)], gkv[...], ((0,), (0,))).astype(BF)
                return 0

            lax.fori_loop(0, G, weight_kv, 0)
            vg = scatter_steps(zy, lambda o, i: dkv.at[o * zy.ni + i], k["v_acc"][0], *k["v_s"])
            step(gng)
            step(vg)
            finish(og)
            step(qg)
            step(fcg)
            finish(gng)
            small = k["small"][0]
            small[...] = k["terms"][...]
            gain = k["vec"][0:1]

            def norm_back_rows(at):
                v = k["rows"][at].astype(F32)
                center = jnp.mean(v, axis=-1, keepdims=True)
                v = v - center
                scale = lax.rsqrt(jnp.mean(v * v, axis=-1, keepdims=True) + 1e-05)
                v = v * scale
                dn = k["gn_sum"][0][at]
                small[2:3] += jnp.sum(dn * v, axis=0, keepdims=True)
                small[3:4] += jnp.sum(dn, axis=0, keepdims=True)
                dn = dn * gain
                c1 = jnp.mean(dn, axis=-1, keepdims=True)
                c2 = jnp.mean(dn * v, axis=-1, keepdims=True)
                k["input_grad"][at] = k["g_res"][at] + scale * (dn - c1 - v * c2)

            row_loop(R, norm_back_rows)
            small[0:1, cols(lax.axis_index("seq"), QC)] = jnp.sum(
                gq[...].astype(F32), axis=0, keepdims=True
            )
            v_sum = jnp.sum(gkv[:, HD:].astype(F32), axis=0, keepdims=True)
            for b in range(G):
                small[7:8, b * W : b * W + HD] = v_sum

            def small_sums():
                got, line = k["s_got"][0], k["s_line"][0]
                yield from exchange_steps(
                    zy,
                    lambda o, i: small.at[:, cols(o * zy.ni + i, W)],
                    lambda o, i: got.at[o * zy.ni + i],
                    *k["s_x"],
                )
                line[:, :W] = sum([got[b] for b in range(1, G)], got[0])
                line[:, W:] = k["fc_terms"][...]
                yield
                yield from gather_steps(
                    sq, line, lambda o, i: k["s_all"][0].at[2 * o + i], *k["s_g"]
                )

            sg = small_sums()
            step(sg)
            step(qg)
            step(vg)
            step(fcg)
            step(sg)
            step(qg)
            step(vg)
            step(fcg)
            step(sg)
            finish(qg, vg)
            tails = [
                gather_steps(
                    sq, k["o_acc"][0], lambda o, i: k["o_all"].at[:, cols(2 * o + i, QC)], *k["o_g"]
                ),
                gather_steps(
                    sq, k["q_acc"][0], lambda o, i: k["q_all"].at[:, cols(2 * o + i, QC)], *k["q_g"]
                ),
                gather_steps(sq, k["v_acc"][0], lambda o, i: k["v_all"].at[2 * o + i], *k["v_g"]),
            ]
            finish(sg, *tails, fcg)
            tot = k["s_all"][0][0]
            for b in range(1, S):
                tot = tot + k["s_all"][0][b]
            k["s_sum"][...] = tot

        fc_rows = W // S

        def grad_fc(k):
            acc, line = k["fc_acc"][0], k["fc_line"][0]
            yield from scatter_steps(sq, lambda o, i: k["d_fc"].at[:, 2 * o + i], acc, *k["fc_s"])
            yield from exchange_steps(
                zy,
                lambda o, i: acc.at[o * zy.ni + i],
                lambda o, i: line.at[:, cols(o * zy.ni + i, ffl)],
                *k["fc_x"],
            )
            yield from gather_steps(
                sq, line, lambda o, i: k["fc_all"].at[cols(2 * o + i, fc_rows)], *k["fc_g"]
            )

        zero = jnp.zeros((D,), F32)
        terms = jnp.stack(
            [zero, b1["stat"][2], zero, zero, jnp.sum(grad_output, axis=0)]
            + [b1["stat"][0], b1["stat"][1], zero]
        )
        fc_shape = (G, fc_rows, ffl)
        b2 = fused(
            "back_two",
            7,
            [zy, sq],
            dict(
                q=(queries, VMEM),
                g_att=(b1["g_att"], VMEM),
                kv=(keyval, VMEM),
                other=(other, VMEM),
                normed=(normed, VMEM),
                w_in=(w_in, VMEM),
                d_out=(d_out.reshape(G, W, QC), ANY),
                d_fc=(d_fc.reshape(G, S, fc_rows, ffl), ANY),
                rows=(rows_in, VMEM),
                g_res=(grad_residual, VMEM),
                vec=(gain_one[None], VMEM),
                terms=(terms, VMEM),
                fc_terms=(grad_fc_bias.reshape(8, -1), VMEM),
            ),
            dict(
                input_grad=((R, D), F32, VMEM),
                o_all=((W, D), BF, ANY),
                q_all=((W, D), BF, ANY),
                v_all=((S, W, 2 * HD), BF, ANY),
                fc_all=((W, G * ffl), BF, ANY),
                s_sum=((8, W + ffl // 8), F32, VMEM),
            ),
            dict(
                dkv_own=[VMEM((T, 2 * HD), F32)],
                dkv_oth=[VMEM((T, 2 * HD), F32)],
                gkv_out=[VMEM((T, 2 * HD), BF)],
                gkv_in=[VMEM((T, 2 * HD), BF)],
                gkv=[VMEM((T, 2 * HD), BF)],
                swap=[DMA((1,)), DMA((1,))],
                gq=[VMEM((T, QC), BF)],
                dq=[VMEM((G, W, QC), BF)],
                dkv=[VMEM((G, W, 2 * HD), BF)],
                gn=[VMEM((S, R, D), BF)],
                gn_sum=[VMEM((R, D), F32)],
                gn_s=scatter_scratch(sq, (R, D), BF),
                o_acc=[VMEM((W, QC), BF)],
                q_acc=[VMEM((W, QC), BF)],
                v_acc=[VMEM((W, 2 * HD), BF)],
                o_s=scatter_scratch(zy, (W, QC), BF),
                q_s=scatter_scratch(zy, (W, QC), BF),
                v_s=scatter_scratch(zy, (W, 2 * HD), BF),
                o_g=gather_sems(sq),
                q_g=gather_sems(sq),
                v_g=gather_sems(sq),
                fc_acc=[VMEM(fc_shape, BF)],
                fc_line=[VMEM((fc_rows, G * ffl), BF)],
                fc_s=scatter_scratch(sq, fc_shape, BF),
                fc_x=exchange_sems(zy),
                fc_g=gather_sems(sq),
                small=[VMEM((8, D), F32)],
                s_got=[VMEM((G, 8, W), F32)],
                s_line=[VMEM((8, W + ffl // 8), F32)],
                s_all=[VMEM((S, 8, W + ffl // 8), F32)],
                s_x=exchange_sems(zy),
                s_g=gather_sems(sq),
            ),
            back_two_main,
        )
        sums = b2["s_sum"]
        place_zy = lax.axis_index(("batch", "ctx"))
        grad_w_qkv = jnp.concatenate(
            [b2["q_all"].astype(F32), jnp.sum(b2["v_all"].astype(F32), axis=0)], axis=1
        )
        return (
            output.astype(BF)[None],
            b2["input_grad"][None],
            grad_w_qkv,
            sums[0, :W],
            lax.dynamic_slice_in_dim(sums[7, :HD], place_zy * vb, vb, 0),
            b2["o_all"].astype(F32),
            sums[1, :W],
            sums[2, :W],
            sums[3, :W],
            b2["fc_all"].astype(F32),
            sums[:, W:].reshape(-1),
            d_proj_all.reshape(-1, D).astype(F32),
            sums[4, :W],
            sums[5, :W],
            sums[6, :W],
        )

    return body


def solution(mesh):
    rows = P("batch", ("ctx", "seq"), None)
    mat = P(("batch", "ctx"), None)
    vec = P(("batch", "ctx"))
    in_specs = (rows, mat, vec, vec, mat, vec, vec, vec, mat, vec, mat, vec, vec, vec, rows)
    out_specs = (rows, rows, mat, vec, vec, mat, vec, vec, vec, mat, vec, mat, vec, vec, vec)
    return jax.shard_map(
        make_body(mesh), mesh=mesh, in_specs=in_specs, out_specs=out_specs, check_vma=False
    )
```

```python
import functools
import math

import jax
import jax.numpy as jnp
from jax import lax
from jax.experimental import pallas as pl
from jax.experimental.pallas import tpu as pltpu
from jax.sharding import PartitionSpec as P

D = 2048
HEADS = 16
HD = 128
MESH = pl.DeviceIdType.MESH
BF = jnp.bfloat16
F32 = jnp.float32
ANY = pl.ANY
VMEM = pltpu.VMEM
DMA = pltpu.SemaphoreType.DMA


class ZY:
    line = True

    def __init__(self, mesh):
        self.no, self.ni = mesh.shape["batch"], mesh.shape["ctx"]

    def me(self):
        return lax.axis_index("batch"), lax.axis_index("ctx")

    def dev(self, o, i):
        return {"batch": o, "ctx": i}


class SEQ:
    line = False

    def __init__(self, mesh):
        self.no, self.ni = mesh.shape["seq"] // 2, 2

    def me(self):
        s = lax.axis_index("seq")
        return s // 2, lax.rem(s, 2)

    def dev(self, o, i):
        return {"seq": 2 * o + i}


def rcopy(src, dst, ss, rs, dev):
    return pltpu.make_async_remote_copy(
        src_ref=src, dst_ref=dst, send_sem=ss, recv_sem=rs, device_id=dev, device_id_type=MESH
    )


def gather_steps(grp, src, view, ss, rs, ls):
    if grp.line:
        return line_gather_steps(grp, src, view, ss, rs, ls)
    return star_gather_steps(grp, src, view, ss, rs, ls)


def star_gather_steps(grp, src, view, ss, rs, ls):
    o, i = grp.me()
    no = grp.no
    mate = grp.dev(o, 1 - i)
    own = pltpu.make_async_copy(src, view(o, i), ls.at[0])
    own.start()
    sent = []
    for d in range(1, no):
        c = rcopy(src, view(o, i), ss.at[d], rs.at[d], grp.dev(lax.rem(o + d, no), i))
        c.start()
        sent.append(c)
    c = rcopy(src, view(o, i), ss.at[0], rs.at[0], mate)
    c.start()
    sent.append(c)
    yield
    for d in range(1, no):
        f = lax.rem(o - d + no, no)
        rcopy(view(f, i), view(f, i), ss.at[d], rs.at[d], mate).wait_recv()
        c = rcopy(view(f, i), view(f, i), ss.at[no + d - 1], rs.at[no + d - 1], mate)
        c.start()
        sent.append(c)
        yield
    rcopy(view(o, 1 - i), view(o, 1 - i), ss.at[0], rs.at[0], mate).wait_recv()
    for d in range(1, no):
        f = lax.rem(o - d + no, no)
        v = view(f, 1 - i)
        rcopy(v, v, ss.at[no + d - 1], rs.at[no + d - 1], mate).wait_recv()
    for c in sent:
        c.wait_send()
    own.wait()


def gather_sems(grp):
    if grp.line:
        return line_gather_sems(grp)
    n = 2 * grp.no - 1
    return [DMA((n,)), DMA((n,)), DMA((1,))]


def add_all(dst, refs, rows, step=16):
    if len(dst.shape) == 3:
        for b in range(dst.shape[0]):
            add_all(dst.at[b], [ref.at[b] for ref in refs], dst.shape[1], step)
        return

    def one(r, _):
        at = pl.ds(pl.multiple_of(r * step, step), step)
        total = refs[0][at].astype(F32)
        for ref in refs[1:]:
            total = total + ref[at].astype(F32)
        dst[at] = total.astype(dst.dtype)
        return 0

    lax.fori_loop(0, rows // step, one, 0)


def scatter_steps(grp, part, out, *scr):
    if grp.line:
        return line_scatter_steps(grp, part, out, *scr)
    return star_scatter_steps(grp, part, out, *scr)


def star_scatter_steps(grp, part, out, near, mid, far, ss, rs, ls):
    o, i = grp.me()
    no = grp.no
    mate = grp.dev(o, 1 - i)
    sent, own = [], []
    order = list(range(1, no)) + [0]
    rows = out.shape[0]
    for d in order:
        t = lax.rem(o + d, no)
        c = rcopy(part(t, 1 - i), near.at[d], ss.at[d], rs.at[d], mate)
        c.start()
        sent.append(c)
        c = pltpu.make_async_copy(part(t, i), mid.at[d], ls.at[d])
        c.start()
        own.append(c)
    yield
    for c, d in zip(own, order):
        t = lax.rem(o + d, no)
        c.wait()
        rcopy(near.at[d], near.at[d], ss.at[d], rs.at[d], mate).wait_recv()
        if d == 0:
            add_all(out, [mid.at[d], near.at[d]], rows)
        else:
            add_all(mid.at[d], [mid.at[d], near.at[d]], rows)
            c = rcopy(
                mid.at[d], far.at[d - 1], ss.at[no + d - 1], rs.at[no + d - 1], grp.dev(t, i)
            )
            c.start()
            sent.append(c)
            yield
    yield
    for d in range(1, no):
        v = far.at[d - 1]
        rcopy(v, v, ss.at[no + d - 1], rs.at[no + d - 1], mate).wait_recv()
        add_all(out, [out, v], rows)
    for c in sent:
        c.wait_send()


def scatter_scratch(grp, shape, dtype):
    no = grp.no
    if grp.line:
        return [
            VMEM((no,) + shape, dtype),
            VMEM((no,) + shape, dtype),
            VMEM((no + 1,) + shape, dtype),
            DMA((2 * no - 1,)),
            DMA((2 * no + 1,)),
            DMA((no,)),
        ]
    n = 2 * no - 1
    return [
        VMEM((no,) + shape, dtype),
        VMEM((no,) + shape, dtype),
        VMEM((no - 1,) + shape, dtype),
        DMA((n,)),
        DMA((n,)),
        DMA((no,)),
    ]


def line_gather_steps(grp, src, view, ss, rs, ls):
    o, i = grp.me()
    n = grp.no
    mate, right, left = grp.dev(o, 1 - i), grp.dev(o + 1, i), grp.dev(o - 1, i)
    own = pltpu.make_async_copy(src, view(o, i), ls.at[0])
    own.start()
    sent = []

    def send(pred, ref, dst, k, to):
        def copy():
            return rcopy(ref, dst, ss.at[k], rs.at[k], to)

        pl.when(pred)(lambda: copy().start())
        sent.append((pred, copy))

    def got(v, k):
        rcopy(v, v, ss.at[k], rs.at[k], mate).wait_recv()

    R, L, Y = -1, n - 2, 2 * n - 2
    send(o < n - 1, src, view(o, i), R + 1, right)
    send(o > 0, src, view(o, i), L + 1, left)
    c = rcopy(src, view(o, i), ss.at[Y], rs.at[Y], mate)
    c.start()
    yield
    for k in range(1, n):
        a, b = lax.max(o - k, 0), lax.min(o + k, n - 1)
        from_left, from_right = o >= k, o + k <= n - 1
        pl.when(from_left)(lambda: got(view(a, i), R + k))
        if k < n - 1:
            send(from_left & (o < n - 1), view(a, i), view(a, i), R + k + 1, right)
        send(from_left, view(a, i), view(a, i), Y + k, mate)
        pl.when(from_right)(lambda: got(view(b, i), L + k))
        if k < n - 1:
            send(from_right & (o > 0), view(b, i), view(b, i), L + k + 1, left)
        send(from_right, view(b, i), view(b, i), Y + n - 1 + k, mate)
        yield
    got(view(o, 1 - i), Y)
    for k in range(1, n):
        a, b = lax.max(o - k, 0), lax.min(o + k, n - 1)
        pl.when(o >= k)(lambda: got(view(a, 1 - i), Y + k))
        pl.when(o + k <= n - 1)(lambda: got(view(b, 1 - i), Y + n - 1 + k))
    for pred, copy in sent:
        pl.when(pred)(lambda: copy().wait_send())
    c.wait_send()
    own.wait()


def line_gather_sems(grp):
    n = 4 * grp.no - 3
    return [DMA((n,)), DMA((n,)), DMA((1,))]


def line_scatter_steps(grp, part, out, near, mid, far, ss, rs, ls):
    o, i = grp.me()
    n = grp.no
    mate = grp.dev(o, 1 - i)
    rows = out.shape[0]
    low = o < n // 2

    def target(j):
        if j == n - 1:
            return o
        down = jnp.where(n - 1 - j > o, n - 1 - j, n - 2 - j)
        up = jnp.where(j < o, j, j + 1)
        return jnp.where(low, down, up)

    sent, own = [], []
    for j in range(n):
        c = rcopy(part(target(j), 1 - i), near.at[j], ss.at[j], rs.at[j], mate)
        c.start()
        sent.append(c)
        c = pltpu.make_async_copy(part(target(j), i), mid.at[j], ls.at[j])
        c.start()
        own.append(c)
    yield
    moved = []
    for j in range(n - 1):
        t = target(j)
        own[j].wait()
        rcopy(near.at[j], near.at[j], ss.at[j], rs.at[j], mate).wait_recv()
        for right in (True, False):
            towards = (t > o) if right else (t < o)
            inner = (o > 0) if right else (o < n - 1)
            slot = t if right else jnp.where(t == o - 1, n, t)
            to = grp.dev(o + 1, i) if right else grp.dev(o - 1, i)

            def copy(j=j, slot=slot, to=to):
                return rcopy(mid.at[j], far.at[slot], ss.at[n + j], rs.at[n + slot], to)

            @pl.when(towards & inner)
            def _():
                rcopy(far.at[t], far.at[t], ss.at[n + j], rs.at[n + t], mate).wait_recv()
                add_all(mid.at[j], [mid.at[j], near.at[j], far.at[t]], rows)

            @pl.when(towards & jnp.logical_not(inner))
            def _():
                add_all(mid.at[j], [mid.at[j], near.at[j]], rows)

            pl.when(towards)(lambda: copy().start())
            moved.append((towards, copy))
        yield
    j = n - 1
    own[j].wait()
    rcopy(near.at[j], near.at[j], ss.at[j], rs.at[j], mate).wait_recv()

    def arrived(k):
        rcopy(far.at[k], far.at[k], ss.at[j], rs.at[n + k], mate).wait_recv()

    pl.when(o > 0)(lambda: arrived(o))
    pl.when(o < n - 1)(lambda: arrived(n))
    mine = [mid.at[j], near.at[j]]
    inside = (o > 0) & (o < n - 1)
    pl.when(inside)(lambda: add_all(out, mine + [far.at[o], far.at[n]], rows))
    pl.when(o == 0)(lambda: add_all(out, mine + [far.at[n]], rows))
    pl.when(o == n - 1)(lambda: add_all(out, mine + [far.at[o]], rows))
    for c in sent:
        c.wait_send()
    for pred, copy in moved:
        pl.when(pred)(lambda: copy().wait_send())


def exchange_steps(grp, src, dst, ss, rs, ls):
    o, i = grp.me()
    no, ni = grp.no, grp.ni
    sent = []
    own = pltpu.make_async_copy(src(o, i), dst(o, i), ls.at[0])
    own.start()
    for a in range(no):
        for b in range(ni):
            if a == 0 and b == 0:
                continue
            to, ti = lax.rem(o + a, no), lax.rem(i + b, ni)
            k = a * ni + b - 1
            c = rcopy(src(to, ti), dst(o, i), ss.at[k], rs.at[k], grp.dev(to, ti))
            c.start()
            sent.append(c)
    yield
    for a in range(no):
        for b in range(ni):
            if a == 0 and b == 0:
                continue
            fo, fi = lax.rem(o - a + no, no), lax.rem(i - b + ni, ni)
            k = a * ni + b - 1
            v = dst(fo, fi)
            rcopy(v, v, ss.at[k], rs.at[k], grp.dev(fo, fi)).wait_recv()
    for c in sent:
        c.wait_send()
    own.wait()


def exchange_sems(grp):
    n = grp.no * grp.ni - 1
    return [DMA((n,)), DMA((n,)), DMA((1,))]


def barrier(groups):
    sem = pltpu.get_barrier_semaphore()
    count = 0
    for grp in groups:
        o, i = grp.me()
        for a in range(grp.no):
            for b in range(grp.ni):
                if a == 0 and b == 0:
                    continue
                to, ti = lax.rem(o + a, grp.no), lax.rem(i + b, grp.ni)
                pl.semaphore_signal(sem, inc=1, device_id=grp.dev(to, ti), device_id_type=MESH)
                count += 1
    pl.semaphore_wait(sem, count)


def run_all(gens):
    live = list(gens)
    while live:
        left = []
        for g in live:
            try:
                next(g)
                left.append(g)
            except StopIteration:
                pass
        live = left


def fused(name, ident, groups, ins, outs, scratch, main):
    keys = list(ins) + list(outs)
    in_specs = [pl.BlockSpec(memory_space=space) for _, space in ins.values()]
    out_specs = [pl.BlockSpec(memory_space=space) for _, _, space in outs.values()]
    out_shapes = [jax.ShapeDtypeStruct(shape, dtype) for shape, dtype, _ in outs.values()]
    flat = [x for group in scratch.values() for x in group]

    def kernel(*refs):
        named = dict(zip(keys, refs))
        at = len(keys)
        for key, group in scratch.items():
            named[key] = refs[at : at + len(group)]
            at += len(group)
        barrier(groups)
        main(named)

    got = pl.pallas_call(
        kernel,
        out_shape=out_shapes,
        in_specs=in_specs,
        out_specs=out_specs,
        scratch_shapes=flat,
        compiler_params=pltpu.CompilerParams(
            collective_id=ident, has_side_effects=True, vmem_limit_bytes=63 * 1024 * 1024
        ),
        name=name,
    )(*[a for a, _ in ins.values()])
    return dict(zip(outs, got))


def step(gen):
    next(gen, None)


def finish(*gens):
    run_all(gens)


def row_loop(rows, fn, size=16):
    def one(r, _):
        fn(pl.ds(pl.multiple_of(r * size, size), size))
        return 0

    lax.fori_loop(0, rows // size, one, 0)


def cols(k, width):
    return pl.ds(pl.multiple_of(k * width, width), width)


def gelu_tanh(values):
    return (
        0.5
        * values
        * (
            1.0
            + jnp.tanh(math.sqrt(2.0 / math.pi) * (values + 0.044715 * values * values * values))
        )
    )


def dot(a, b, dims=((1,), (0,))):
    return lax.dot_general(a, b, (dims, ((), ())), preferred_element_type=F32)


def make_body(mesh):
    zy, sq = ZY(mesh), SEQ(mesh)
    S = mesh.shape["seq"]
    G = mesh.shape["batch"] * mesh.shape["ctx"]
    W = D // G
    QC = (HEADS // S) * HD

    def gather_steps_inplace(grp, view, ss, rs):
        o, i = grp.me()
        no = grp.no
        mate = grp.dev(o, 1 - i)
        sent = []
        for d in list(range(1, no)) + [0]:
            to = grp.dev(lax.rem(o + d, no), i) if d else mate
            c = rcopy(view(o, i), view(o, i), ss.at[d], rs.at[d], to)
            c.start()
            sent.append(c)
        yield
        for d in range(1, no):
            v = view(lax.rem(o - d + no, no), i)
            rcopy(v, v, ss.at[d], rs.at[d], mate).wait_recv()
            c = rcopy(v, v, ss.at[no + d - 1], rs.at[no + d - 1], mate)
            c.start()
            sent.append(c)
        yield
        v = view(o, 1 - i)
        rcopy(v, v, ss.at[0], rs.at[0], mate).wait_recv()
        for d in range(1, no):
            v = view(lax.rem(o - d + no, no), 1 - i)
            rcopy(v, v, ss.at[no + d - 1], rs.at[no + d - 1], mate).wait_recv()
        for c in sent:
            c.wait_send()

    def body(
        inputs,
        w_qkv,
        q_bias,
        v_bias,
        w_out,
        out_bias,
        gain_attn,
        shift_attn,
        w_fc,
        fc_bias,
        w_proj,
        proj_bias,
        gain_mlp,
        shift_mlp,
        cotangent,
    ):
        rows_in = inputs[0]
        R = rows_in.shape[0]
        g_out = cotangent[0]
        vb = v_bias.shape[0]
        place_zy = lax.axis_index(("batch", "ctx"))
        lift = lambda v: v.astype(F32)
        small = jnp.stack(
            [lift(v) for v in (gain_attn, shift_attn, q_bias, out_bias, proj_bias, gain_mlp)]
            + [
                lift(shift_mlp),
                lax.dynamic_update_slice_in_dim(jnp.zeros((W,), F32), lift(v_bias), place_zy * vb, 0),
            ]
        )
        T = S * R
        NQ = min(256, T)
        HL = QC // HD
        NB = HL * (T // NQ)
        HALF = T // 2
        score_scale = 1.0 / math.sqrt(HD)
        ffl = w_fc.shape[1] // G
        fc_rows = W // S

        def front_main(k):
            c, sid = lax.axis_index("ctx"), lax.axis_index("seq")
            vec, span, normed = k["vec"], k["span"][0], k["normed_s"][0]
            w_in, w_back = k["w_in_s"][0], k["w_back_s"][0]
            row_of = lambda o, i: cols(o * zy.ni + i, W)
            sm = gather_steps(zy, k["small"], lambda o, i: vec.at[:, row_of(o, i)], *k["sm_g"])
            sp = gather_steps(sq, k["rows"], lambda o, i: span.at[cols(2 * o + i, R)], *k["sp_g"])
            wk = gather_steps(
                zy,
                k["w_qkv"].at[:, D : D + 2 * HD],
                lambda o, i: w_in.at[row_of(o, i), QC : QC + 2 * HD],
                *k["wk_g"],
            )
            wq = gather_steps(
                zy,
                k["w_qkv"].at[:, cols(sid, QC)],
                lambda o, i: w_in.at[row_of(o, i), :QC],
                *k["wq_g"],
            )
            wb = gather_steps(
                zy, k["w_out"].at[:, cols(sid, QC)], lambda o, i: w_back.at[row_of(o, i)], *k["wb_g"]
            )
            gg = gather_steps(
                zy, k["cot"], lambda o, i: k["g_all"].at[o * zy.ni + i], *k["gg_g"]
            )

            def spread_fc():
                yield from exchange_steps(
                    zy,
                    lambda o, i: k["w_fc"].at[cols(sid, fc_rows), cols(o * zy.ni + i, ffl)],
                    lambda o, i: k["fc"].at[o * zy.ni + i, sid],
                    *k["fc_x"],
                )
                yield from gather_steps_inplace(sq, lambda o, i: k["fc"].at[:, 2 * o + i], *k["fc_g"])

            fc = spread_fc()
            step(sm)
            step(sp)
            step(wk)
            step(wq)
            for _ in range(zy.no - 1):
                step(sm)
                step(wk)
            finish(sm)
            step(wq)
            finish(sp)
            gain, shift = vec[0:1], vec[1:2]

            def norm_rows(at):
                v = span[at].astype(F32)
                v = v - jnp.mean(v, axis=-1, keepdims=True)
                v = v * lax.rsqrt(jnp.mean(v * v, axis=-1, keepdims=True) + 1e-05)
                normed[at] = (v * gain + shift).astype(BF)

            row_loop(T, norm_rows)
            step(wq)
            finish(wk)
            v_bias_row = sum([vec[7:8, b * W : b * W + HD] for b in range(1, G)], vec[7:8, :HD])

            def key_rows(b, _):
                at = cols(b, NQ)
                mixed = dot(normed[at], w_in[:, QC:])
                k["kv"][at, :HD] = mixed[:, :HD].astype(BF)
                k["kv"][at, HD:] = (mixed[:, HD:] + v_bias_row).astype(BF)
                return 0

            lax.fori_loop(0, T // NQ, key_rows, 0)
            swap = rcopy(
                k["kv"], k["other"], k["swap"][0].at[0], k["swap"][1].at[0], {"ctx": 1 - c}
            )
            swap.start()
            step(wq)
            saves = [
                pltpu.make_async_copy(normed, k["normed"], k["save"][0].at[0]),
                pltpu.make_async_copy(w_in, k["w_in"], k["save"][0].at[1]),
                pltpu.make_async_copy(w_back, k["w_back"], k["save"][0].at[2]),
                pltpu.make_async_copy(k["att_s"][0], k["att_rows"], k["save"][0].at[3]),
            ]
            saves[0].start()
            step(fc)
            step(wb)
            finish(wq)
            saves[1].start()
            q_bias_row = vec[2:3, cols(sid, QC)]

            def query_rows(b, _):
                at = cols(b, NQ)
                k["q"][at] = (dot(normed[at], w_in[:, :QC]) + q_bias_row).astype(BF)
                return 0

            lax.fori_loop(0, T // NQ, query_rows, 0)
            swap.wait()
            step(wb)
            step(gg)
            far_bias = (1 - c).astype(F32) * -1e30
            att = k["att"][0]

            def attend(n, _):
                h, first = lax.rem(n, HL), (n // HL) * NQ
                at = pl.ds(pl.multiple_of(first, NQ), NQ)
                hc = cols(h, HD)
                q = k["q"][at, hc]
                s0 = dot(q, k["kv"][:, :HD], ((1,), (1,))) * score_scale
                s1 = dot(q, k["other"][:, :HD], ((1,), (1,))) * score_scale + far_bias
                qpos = first + lax.broadcasted_iota(jnp.int32, s0.shape, 0)
                kpos = lax.broadcasted_iota(jnp.int32, s0.shape, 1)
                s0 = jnp.where(kpos <= qpos, s0, -1e30)
                top = jnp.maximum(
                    jnp.max(s0, axis=-1, keepdims=True), jnp.max(s1, axis=-1, keepdims=True)
                )
                p0, p1 = jnp.exp(s0 - top), jnp.exp(s1 - top)
                total = jnp.sum(p0, axis=-1, keepdims=True) + jnp.sum(p1, axis=-1, keepdims=True)
                inv = 1.0 / total
                att[at, hc] = (
                    dot((p0 * inv).astype(BF), k["kv"][:, HD:])
                    + dot((p1 * inv).astype(BF), k["other"][:, HD:])
                ).astype(BF)
                return 0

            att_s = k["att_s"][0]
            ag = []
            for half in range(2):
                lax.fori_loop(half * NB // 2, (half + 1) * NB // 2, attend, 0)
                lines = pl.ds(half * HALF, HALF)
                g = gather_steps(
                    sq,
                    att.at[lines],
                    lambda o, i, lines=lines: att_s.at[lines, cols(2 * o + i, QC)],
                    *k["at_g%d" % half],
                )
                step(g)
                ag.append(g)
                step(wb)
                step(fc)
            finish(wb)
            saves[2].start()
            br, brn = k["br"][0], k["brn"][0]
            for half in range(2):
                step(gg)
                finish(ag[half])

                def branch_rows(b, _):
                    at = cols(half * (S // 2) + b, R)
                    br[at] = dot(att_s[at], w_back[...]).astype(BF)
                    return 0

                lax.fori_loop(0, S // 2, branch_rows, 0)
            saves[3].start()
            bx = exchange_steps(
                sq,
                lambda o, i: br.at[cols(2 * o + i, R)],
                lambda o, i: brn.at[:, cols(2 * o + i, QC)],
                *k["br_x"],
            )
            step(bx)
            step(fc)
            finish(bx)
            ob, gain2, shift2 = vec[3:4], vec[5:6], vec[6:7]
            nm = k["nm"][0]

            def norm_rows_two(at):
                v = k["rows"][at].astype(F32) + brn[at].astype(F32) + ob
                k["residual"][at] = v
                v = v - jnp.mean(v, axis=-1, keepdims=True)
                v = v * lax.rsqrt(jnp.mean(v * v, axis=-1, keepdims=True) + 1e-05)
                nm[at] = (v * gain2 + shift2).astype(BF)

            row_loop(R, norm_rows_two)
            xg = gather_steps(zy, nm, lambda o, i: k["x_all"].at[o * zy.ni + i], *k["xg_g"])
            step(xg)
            finish(gg, xg, fc)
            for c_ in saves:
                c_.wait()

        f = fused(
            "front",
            1,
            [zy, sq],
            dict(
                small=(small, VMEM),
                rows=(rows_in, VMEM),
                w_qkv=(w_qkv, VMEM),
                w_out=(w_out, VMEM),
                w_fc=(w_fc, VMEM),
                cot=(g_out, VMEM),
            ),
            dict(
                vec=((8, D), F32, VMEM),
                normed=((T, D), BF, ANY),
                w_in=((D, QC + 2 * HD), BF, ANY),
                w_back=((D, QC), BF, ANY),
                q=((T, QC), BF, VMEM),
                kv=((T, 2 * HD), BF, VMEM),
                other=((T, 2 * HD), BF, VMEM),
                att_rows=((T, D), BF, ANY),
                residual=((R, D), F32, VMEM),
                fc=((G, S, fc_rows, ffl), BF, ANY),
                g_all=((G, R, D), BF, ANY),
                x_all=((G, R, D), BF, ANY),
            ),
            dict(
                span=[VMEM((T, D), BF)],
                normed_s=[VMEM((T, D), BF)],
                w_in_s=[VMEM((D, QC + 2 * HD), BF)],
                w_back_s=[VMEM((D, QC), BF)],
                att=[VMEM((T, QC), BF)],
                att_s=[VMEM((T, D), BF)],
                br=[VMEM((T, QC), BF)],
                brn=[VMEM((R, D), BF)],
                nm=[VMEM((R, D), BF)],
                sm_g=gather_sems(zy),
                sp_g=gather_sems(sq),
                wk_g=gather_sems(zy),
                wq_g=gather_sems(zy),
                wb_g=gather_sems(zy),
                gg_g=gather_sems(zy),
                xg_g=gather_sems(zy),
                fc_x=exchange_sems(zy),
                fc_g=gather_sems(sq)[:2],
                at_g0=gather_sems(sq),
                at_g1=gather_sems(sq),
                br_x=exchange_sems(sq),
                swap=[DMA((1,)), DMA((1,))],
                save=[DMA((4,))],
            ),
            front_main,
        )
        vec = f["vec"]
        gain_one, gain_two, pb = vec[0], vec[5], vec[4]
        normed, w_in, w_back, att_rows = f["normed"], f["w_in"], f["w_back"], f["att_rows"]
        queries, keyval, other, residual = f["q"], f["kv"], f["other"], f["residual"]
        x_all, g_all, fc_cols = f["x_all"], f["g_all"], f["fc"]
        x_all = x_all.reshape(G * R, D)
        g_rows = g_all.reshape(G * R, D)
        fc = fc_cols.reshape(D, ffl)
        hidden = dot(x_all, fc) + fc_bias.astype(F32)
        active, gelu_back = jax.vjp(gelu_tanh, hidden)
        active_low = active.astype(BF)
        y_part = dot(active_low, w_proj).astype(BF)
        grad_active = dot(g_rows, w_proj, ((1,), (1,)))
        grad_hidden = gelu_back(grad_active)[0].astype(BF)
        grad_fc_bias = jnp.sum(grad_hidden.astype(F32), axis=0)
        gx_part = dot(grad_hidden, fc, ((1,), (1,))).astype(BF)
        d_proj = dot(active_low, g_rows, ((0,), (0,))).astype(BF)
        d_fc = dot(x_all, grad_hidden, ((0,), (0,))).astype(BF)
        rows_d = (R, D)
        far_out = (ffl // S, D)

        def back_main(k):
            gx = scatter_steps(
                zy, lambda o, i: k["gx"].at[o * zy.ni + i], k["gx_sum"][0], *k["gx_s"]
            )
            yy = scatter_steps(zy, lambda o, i: k["y"].at[o * zy.ni + i], k["y_sum"], *k["y_s"])

            def sum_proj():
                acc = k["pj_acc"][0]
                yield from scatter_steps(
                    sq, lambda o, i: k["d_proj"].at[2 * o + i], acc, *k["pj_s"]
                )
                yield from gather_steps(
                    sq, acc, lambda o, i: k["d_proj_all"].at[2 * o + i], *k["pj_g"]
                )

            pj = sum_proj()
            step(gx)
            step(pj)
            step(yy)
            step(gx)
            step(pj)
            step(gx)
            step(pj)
            finish(gx)
            gain = k["vec"][0:1]
            stat = k["stat"]
            stat[...] = jnp.zeros(stat.shape, F32)

            def norm_back_rows(at):
                v = k["residual"][at]
                center = jnp.mean(v, axis=-1, keepdims=True)
                v = v - center
                scale = lax.rsqrt(jnp.mean(v * v, axis=-1, keepdims=True) + 1e-05)
                v = v * scale
                dn = k["gx_sum"][0][at]
                stat[0:1] += jnp.sum(dn * v, axis=0, keepdims=True)
                stat[1:2] += jnp.sum(dn, axis=0, keepdims=True)
                dn = dn * gain
                c1 = jnp.mean(dn, axis=-1, keepdims=True)
                c2 = jnp.mean(dn * v, axis=-1, keepdims=True)
                total = k["cot"][at].astype(F32) + scale * (dn - c1 - v * c2)
                stat[2:3] += jnp.sum(total, axis=0, keepdims=True)
                k["g_res"][at] = total
                k["gb"][0][at] = total.astype(BF)

            row_loop(R, norm_back_rows)
            gb = exchange_steps(
                sq,
                lambda o, i: k["gb"][0].at[:, cols(2 * o + i, QC)],
                lambda o, i: k["gbs"].at[cols(2 * o + i, R)],
                *k["gb_x"],
            )
            step(gb)
            step(pj)
            step(yy)
            finish(gb)
            ga = k["ga"][0]

            def back_cols(b, _):
                at = cols(b, QC)
                ga[b] = dot(k["gbs"][...], k["w_back"][at, :], ((1,), (1,))).astype(BF)
                return 0

            lax.fori_loop(0, S, back_cols, 0)
            at_ = scatter_steps(sq, lambda o, i: ga.at[2 * o + i], k["g_att"], *k["ga_s"])
            step(at_)
            step(yy)
            finish(at_)
            finish(yy, pj)

        b1 = fused(
            "back_one",
            6,
            [zy, sq],
            dict(
                gx=(gx_part.reshape(G, R, D), ANY),
                y=(y_part.reshape(G, R, D), ANY),
                d_proj=(d_proj.reshape((S,) + far_out), ANY),
                cot=(g_out, VMEM),
                residual=(residual, VMEM),
                vec=(gain_two[None], VMEM),
                w_back=(w_back, VMEM),
            ),
            dict(
                y_sum=(rows_d, F32, VMEM),
                d_proj_all=((S,) + far_out, BF, ANY),
                g_res=(rows_d, F32, VMEM),
                stat=((8, D), F32, VMEM),
                gbs=((T, QC), BF, VMEM),
                g_att=((T, QC), BF, VMEM),
            ),
            dict(
                gx_sum=[VMEM(rows_d, F32)],
                gx_s=scatter_scratch(zy, rows_d, BF),
                y_s=scatter_scratch(zy, rows_d, BF),
                pj_acc=[VMEM(far_out, BF)],
                pj_s=scatter_scratch(sq, far_out, BF),
                pj_g=gather_sems(sq),
                gb=[VMEM(rows_d, BF)],
                gb_x=exchange_sems(sq),
                ga=[VMEM((S, T, QC), BF)],
                ga_s=scatter_scratch(sq, (T, QC), BF),
            ),
            back_main,
        )
        d_proj_all = b1["d_proj_all"]
        output = residual + b1["y_sum"] + pb
        grad_output = g_out.astype(F32)
        grad_residual = b1["g_res"]
        gb = b1["gbs"]
        d_out = dot(att_rows, gb, ((0,), (0,))).astype(BF)

        def back_two_main(k):
            fcg = grad_fc(k)
            og = scatter_steps(zy, lambda o, i: k["d_out"].at[o * zy.ni + i], k["o_acc"][0], *k["o_s"])
            step(og)
            step(fcg)
            own, oth = k["dkv_own"][0], k["dkv_oth"][0]
            own[...] = jnp.zeros(own.shape, F32)
            oth[...] = jnp.zeros(oth.shape, F32)
            far_bias = (1 - lax.axis_index("ctx")).astype(F32) * -1e30

            def attend_back(n, _):
                h, first = n // (T // NQ), lax.rem(n, T // NQ) * NQ
                at = pl.ds(pl.multiple_of(first, NQ), NQ)
                hc = cols(h, HD)
                q, g = k["q"][at, hc], k["g_att"][at, hc]
                kv0, kv1 = k["kv"], k["other"]
                s0 = dot(q, kv0[:, :HD], ((1,), (1,))) * score_scale
                s1 = dot(q, kv1[:, :HD], ((1,), (1,))) * score_scale + far_bias
                qpos = first + lax.broadcasted_iota(jnp.int32, s0.shape, 0)
                kpos = lax.broadcasted_iota(jnp.int32, s0.shape, 1)
                s0 = jnp.where(kpos <= qpos, s0, -1e30)
                top = jnp.maximum(
                    jnp.max(s0, axis=-1, keepdims=True), jnp.max(s1, axis=-1, keepdims=True)
                )
                p0, p1 = jnp.exp(s0 - top), jnp.exp(s1 - top)
                total = jnp.sum(p0, axis=-1, keepdims=True) + jnp.sum(p1, axis=-1, keepdims=True)
                inv = 1.0 / total
                p0, p1 = p0 * inv, p1 * inv
                own[:, HD:] += dot(p0.astype(BF), g, ((0,), (0,)))
                oth[:, HD:] += dot(p1.astype(BF), g, ((0,), (0,)))
                e0 = dot(g, kv0[:, HD:], ((1,), (1,)))
                e1 = dot(g, kv1[:, HD:], ((1,), (1,)))
                inner = jnp.sum(p0 * e0, axis=-1, keepdims=True) + jnp.sum(
                    p1 * e1, axis=-1, keepdims=True
                )
                d0 = (p0 * (e0 - inner) * score_scale).astype(BF)
                d1 = (p1 * (e1 - inner) * score_scale).astype(BF)
                own[:, :HD] += dot(d0, q, ((0,), (0,)))
                oth[:, :HD] += dot(d1, q, ((0,), (0,)))
                k["gq"][0][at, hc] = (dot(d0, kv0[:, :HD]) + dot(d1, kv1[:, :HD])).astype(BF)
                return 0

            cuts = [0, NB // 2, NB]
            for lo, hi in zip(cuts[:-1], cuts[1:]):
                lax.fori_loop(lo, hi, attend_back, 0)
                step(og)
                step(fcg)
            c = lax.axis_index("ctx")
            k["gkv_out"][0][...] = oth[...].astype(BF)
            swap = rcopy(
                k["gkv_out"][0],
                k["gkv_in"][0],
                k["swap"][0].at[0],
                k["swap"][1].at[0],
                {"ctx": 1 - c},
            )
            swap.start()
            gq, dq = k["gq"][0], k["dq"][0]

            def weight_q(b, _):
                dq[b] = dot(k["normed"][:, cols(b, W)], gq[...], ((0,), (0,))).astype(BF)
                return 0

            lax.fori_loop(0, G, weight_q, 0)
            qg = scatter_steps(zy, lambda o, i: dq.at[o * zy.ni + i], k["q_acc"][0], *k["q_s"])
            step(og)
            step(qg)
            swap.wait()
            gkv = k["gkv"][0]
            gkv[...] = (own[...] + k["gkv_in"][0][...].astype(F32)).astype(BF)
            gn = k["gn"][0]

            def back_in(b, _):
                at = cols(b, R)
                gn[b] = (
                    dot(gq[at], k["w_in"][:, :QC], ((1,), (1,)))
                    + dot(gkv[at], k["w_in"][:, QC:], ((1,), (1,)))
                ).astype(BF)
                return 0

            lax.fori_loop(0, S, back_in, 0)
            gng = scatter_steps(sq, lambda o, i: gn.at[2 * o + i], k["gn_sum"][0], *k["gn_s"])
            step(gng)
            dkv = k["dkv"][0]

            def weight_kv(b, _):
                dkv[b] = dot(k["normed"][:, cols(b, W)], gkv[...], ((0,), (0,))).astype(BF)
                return 0

            lax.fori_loop(0, G, weight_kv, 0)
            vg = scatter_steps(zy, lambda o, i: dkv.at[o * zy.ni + i], k["v_acc"][0], *k["v_s"])
            step(gng)
            step(vg)
            finish(og)
            step(qg)
            step(fcg)
            finish(gng)
            small = k["small"][0]
            small[...] = k["terms"][...]
            gain = k["vec"][0:1]

            def norm_back_rows(at):
                v = k["rows"][at].astype(F32)
                center = jnp.mean(v, axis=-1, keepdims=True)
                v = v - center
                scale = lax.rsqrt(jnp.mean(v * v, axis=-1, keepdims=True) + 1e-05)
                v = v * scale
                dn = k["gn_sum"][0][at]
                small[2:3] += jnp.sum(dn * v, axis=0, keepdims=True)
                small[3:4] += jnp.sum(dn, axis=0, keepdims=True)
                dn = dn * gain
                c1 = jnp.mean(dn, axis=-1, keepdims=True)
                c2 = jnp.mean(dn * v, axis=-1, keepdims=True)
                k["input_grad"][at] = k["g_res"][at] + scale * (dn - c1 - v * c2)

            row_loop(R, norm_back_rows)
            small[0:1, cols(lax.axis_index("seq"), QC)] = jnp.sum(
                gq[...].astype(F32), axis=0, keepdims=True
            )
            v_sum = jnp.sum(gkv[:, HD:].astype(F32), axis=0, keepdims=True)
            for b in range(G):
                small[7:8, b * W : b * W + HD] = v_sum

            def small_sums():
                got, line = k["s_got"][0], k["s_line"][0]
                yield from exchange_steps(
                    zy,
                    lambda o, i: small.at[:, cols(o * zy.ni + i, W)],
                    lambda o, i: got.at[o * zy.ni + i],
                    *k["s_x"],
                )
                line[:, :W] = sum([got[b] for b in range(1, G)], got[0])
                line[:, W:] = k["fc_terms"][...]
                yield
                yield from gather_steps(
                    sq, line, lambda o, i: k["s_all"][0].at[2 * o + i], *k["s_g"]
                )

            sg = small_sums()
            step(sg)
            step(qg)
            step(vg)
            step(fcg)
            step(sg)
            step(qg)
            step(vg)
            step(fcg)
            step(sg)
            finish(qg, vg)
            tails = [
                gather_steps(
                    sq, k["o_acc"][0], lambda o, i: k["o_all"].at[:, cols(2 * o + i, QC)], *k["o_g"]
                ),
                gather_steps(
                    sq, k["q_acc"][0], lambda o, i: k["q_all"].at[:, cols(2 * o + i, QC)], *k["q_g"]
                ),
                gather_steps(sq, k["v_acc"][0], lambda o, i: k["v_all"].at[2 * o + i], *k["v_g"]),
            ]
            finish(sg, *tails, fcg)
            tot = k["s_all"][0][0]
            for b in range(1, S):
                tot = tot + k["s_all"][0][b]
            k["s_sum"][...] = tot

        def grad_fc(k):
            acc, line = k["fc_acc"][0], k["fc_line"][0]
            yield from scatter_steps(sq, lambda o, i: k["d_fc"].at[:, 2 * o + i], acc, *k["fc_s"])
            yield from exchange_steps(
                zy,
                lambda o, i: acc.at[o * zy.ni + i],
                lambda o, i: line.at[:, cols(o * zy.ni + i, ffl)],
                *k["fc_x"],
            )
            yield from gather_steps(
                sq, line, lambda o, i: k["fc_all"].at[cols(2 * o + i, fc_rows)], *k["fc_g"]
            )

        zero = jnp.zeros((D,), F32)
        terms = jnp.stack(
            [zero, b1["stat"][2], zero, zero, jnp.sum(grad_output, axis=0)]
            + [b1["stat"][0], b1["stat"][1], zero]
        )
        fc_shape = (G, fc_rows, ffl)
        b2 = fused(
            "back_two",
            7,
            [zy, sq],
            dict(
                q=(queries, VMEM),
                g_att=(b1["g_att"], VMEM),
                kv=(keyval, VMEM),
                other=(other, VMEM),
                normed=(normed, VMEM),
                w_in=(w_in, VMEM),
                d_out=(d_out.reshape(G, W, QC), ANY),
                d_fc=(d_fc.reshape(G, S, fc_rows, ffl), ANY),
                rows=(rows_in, VMEM),
                g_res=(grad_residual, VMEM),
                vec=(gain_one[None], VMEM),
                terms=(terms, VMEM),
                fc_terms=(grad_fc_bias.reshape(8, -1), VMEM),
            ),
            dict(
                input_grad=((R, D), F32, VMEM),
                o_all=((W, D), BF, ANY),
                q_all=((W, D), BF, ANY),
                v_all=((S, W, 2 * HD), BF, ANY),
                fc_all=((W, G * ffl), BF, ANY),
                s_sum=((8, W + ffl // 8), F32, VMEM),
            ),
            dict(
                dkv_own=[VMEM((T, 2 * HD), F32)],
                dkv_oth=[VMEM((T, 2 * HD), F32)],
                gkv_out=[VMEM((T, 2 * HD), BF)],
                gkv_in=[VMEM((T, 2 * HD), BF)],
                gkv=[VMEM((T, 2 * HD), BF)],
                swap=[DMA((1,)), DMA((1,))],
                gq=[VMEM((T, QC), BF)],
                dq=[VMEM((G, W, QC), BF)],
                dkv=[VMEM((G, W, 2 * HD), BF)],
                gn=[VMEM((S, R, D), BF)],
                gn_sum=[VMEM((R, D), F32)],
                gn_s=scatter_scratch(sq, (R, D), BF),
                o_acc=[VMEM((W, QC), BF)],
                q_acc=[VMEM((W, QC), BF)],
                v_acc=[VMEM((W, 2 * HD), BF)],
                o_s=scatter_scratch(zy, (W, QC), BF),
                q_s=scatter_scratch(zy, (W, QC), BF),
                v_s=scatter_scratch(zy, (W, 2 * HD), BF),
                o_g=gather_sems(sq),
                q_g=gather_sems(sq),
                v_g=gather_sems(sq),
                fc_acc=[VMEM(fc_shape, BF)],
                fc_line=[VMEM((fc_rows, G * ffl), BF)],
                fc_s=scatter_scratch(sq, fc_shape, BF),
                fc_x=exchange_sems(zy),
                fc_g=gather_sems(sq),
                small=[VMEM((8, D), F32)],
                s_got=[VMEM((G, 8, W), F32)],
                s_line=[VMEM((8, W + ffl // 8), F32)],
                s_all=[VMEM((S, 8, W + ffl // 8), F32)],
                s_x=exchange_sems(zy),
                s_g=gather_sems(sq),
            ),
            back_two_main,
        )
        sums = b2["s_sum"]
        grad_w_qkv = jnp.concatenate(
            [b2["q_all"].astype(F32), jnp.sum(b2["v_all"].astype(F32), axis=0)], axis=1
        )
        return (
            output.astype(BF)[None],
            b2["input_grad"][None],
            grad_w_qkv,
            sums[0, :W],
            lax.dynamic_slice_in_dim(sums[7, :HD], place_zy * vb, vb, 0),
            b2["o_all"].astype(F32),
            sums[1, :W],
            sums[2, :W],
            sums[3, :W],
            b2["fc_all"].astype(F32),
            sums[:, W:].reshape(-1),
            d_proj_all.reshape(-1, D).astype(F32),
            sums[4, :W],
            sums[5, :W],
            sums[6, :W],
        )

    return body


def solution(mesh):
    rows = P("batch", ("ctx", "seq"), None)
    mat = P(("batch", "ctx"), None)
    vec = P(("batch", "ctx"))
    in_specs = (rows, mat, vec, vec, mat, vec, vec, vec, mat, vec, mat, vec, vec, vec, rows)
    out_specs = (rows, rows, mat, vec, vec, mat, vec, vec, vec, mat, vec, mat, vec, vec, vec)
    return jax.shard_map(
        make_body(mesh), mesh=mesh, in_specs=in_specs, out_specs=out_specs, check_vma=False
    )
```

```python
import functools
import math

import jax
import jax.numpy as jnp
from jax import lax
from jax.experimental import pallas as pl
from jax.experimental.pallas import tpu as pltpu
from jax.sharding import PartitionSpec as P

D = 2048
HEADS = 16
HD = 128
MESH = pl.DeviceIdType.MESH
BF = jnp.bfloat16
F32 = jnp.float32
ANY = pl.ANY
VMEM = pltpu.VMEM
DMA = pltpu.SemaphoreType.DMA


class ZY:
    line = True

    def __init__(self, mesh):
        self.no, self.ni = mesh.shape["batch"], mesh.shape["ctx"]

    def me(self):
        return lax.axis_index("batch"), lax.axis_index("ctx")

    def dev(self, o, i):
        return {"batch": o, "ctx": i}


class SEQ:
    line = False

    def __init__(self, mesh):
        self.no, self.ni = mesh.shape["seq"] // 2, 2

    def me(self):
        s = lax.axis_index("seq")
        return s // 2, lax.rem(s, 2)

    def dev(self, o, i):
        return {"seq": 2 * o + i}


def rcopy(src, dst, ss, rs, dev):
    return pltpu.make_async_remote_copy(
        src_ref=src, dst_ref=dst, send_sem=ss, recv_sem=rs, device_id=dev, device_id_type=MESH
    )


def gather_steps(grp, src, view, ss, rs, ls):
    if grp.line:
        return line_gather_steps(grp, src, view, ss, rs, ls)
    return star_gather_steps(grp, src, view, ss, rs, ls)


def star_gather_steps(grp, src, view, ss, rs, ls):
    o, i = grp.me()
    no = grp.no
    mate = grp.dev(o, 1 - i)
    own = pltpu.make_async_copy(src, view(o, i), ls.at[0])
    own.start()
    sent = []
    for d in range(1, no):
        c = rcopy(src, view(o, i), ss.at[d], rs.at[d], grp.dev(lax.rem(o + d, no), i))
        c.start()
        sent.append(c)
    c = rcopy(src, view(o, i), ss.at[0], rs.at[0], mate)
    c.start()
    sent.append(c)
    yield
    for d in range(1, no):
        f = lax.rem(o - d + no, no)
        rcopy(view(f, i), view(f, i), ss.at[d], rs.at[d], mate).wait_recv()
        c = rcopy(view(f, i), view(f, i), ss.at[no + d - 1], rs.at[no + d - 1], mate)
        c.start()
        sent.append(c)
        yield
    rcopy(view(o, 1 - i), view(o, 1 - i), ss.at[0], rs.at[0], mate).wait_recv()
    for d in range(1, no):
        f = lax.rem(o - d + no, no)
        v = view(f, 1 - i)
        rcopy(v, v, ss.at[no + d - 1], rs.at[no + d - 1], mate).wait_recv()
    for c in sent:
        c.wait_send()
    own.wait()


def gather_sems(grp):
    if grp.line:
        return line_gather_sems(grp)
    n = 2 * grp.no - 1
    return [DMA((n,)), DMA((n,)), DMA((1,))]


def add_all(dst, refs, rows, step=16):
    if len(dst.shape) == 3:
        for b in range(dst.shape[0]):
            add_all(dst.at[b], [ref.at[b] for ref in refs], dst.shape[1], step)
        return

    def one(r, _):
        at = pl.ds(pl.multiple_of(r * step, step), step)
        total = refs[0][at].astype(F32)
        for ref in refs[1:]:
            total = total + ref[at].astype(F32)
        dst[at] = total.astype(dst.dtype)
        return 0

    lax.fori_loop(0, rows // step, one, 0)


def scatter_steps(grp, part, out, *scr, inplace=False):
    if grp.line:
        return line_scatter_steps(grp, part, out, *scr, inplace=inplace)
    return star_scatter_steps(grp, part, out, *scr, inplace=inplace)


def star_scatter_steps(grp, part, out, near, mid, far, ss, rs, ls, inplace):
    o, i = grp.me()
    no = grp.no
    mate = grp.dev(o, 1 - i)
    sent, own = [], []
    order = list(range(1, no)) + [0]
    rows = out.shape[0]
    for d in order:
        t = lax.rem(o + d, no)
        c = rcopy(part(t, 1 - i), near.at[d], ss.at[d], rs.at[d], mate)
        c.start()
        sent.append(c)
        if not inplace:
            c = pltpu.make_async_copy(part(t, i), mid.at[d], ls.at[d])
            c.start()
            own.append(c)
    yield
    for n, d in enumerate(order):
        t = lax.rem(o + d, no)
        held = part(t, i) if inplace else mid.at[d]
        if not inplace:
            own[n].wait()
        rcopy(near.at[d], near.at[d], ss.at[d], rs.at[d], mate).wait_recv()
        if d == 0:
            add_all(out, [held, near.at[d]], rows)
        else:
            add_all(held, [held, near.at[d]], rows)
            c = rcopy(
                held, far.at[d - 1], ss.at[no + d - 1], rs.at[no + d - 1], grp.dev(t, i)
            )
            c.start()
            sent.append(c)
            yield
    yield
    for d in range(1, no):
        v = far.at[d - 1]
        rcopy(v, v, ss.at[no + d - 1], rs.at[no + d - 1], mate).wait_recv()
        add_all(out, [out, v], rows)
    for c in sent:
        c.wait_send()


def scatter_scratch(grp, shape, dtype, mid=True):
    no = grp.no
    held = (no,) + shape if mid else (1, 8, 128)
    if grp.line:
        return [
            VMEM((no,) + shape, dtype),
            VMEM(held, dtype),
            VMEM((no + 1,) + shape, dtype),
            DMA((2 * no - 1,)),
            DMA((2 * no + 1,)),
            DMA((no,)),
        ]
    n = 2 * no - 1
    return [
        VMEM((no,) + shape, dtype),
        VMEM(held, dtype),
        VMEM((no - 1,) + shape, dtype),
        DMA((n,)),
        DMA((n,)),
        DMA((no,)),
    ]


def line_gather_steps(grp, src, view, ss, rs, ls):
    o, i = grp.me()
    n = grp.no
    mate, right, left = grp.dev(o, 1 - i), grp.dev(o + 1, i), grp.dev(o - 1, i)
    own = pltpu.make_async_copy(src, view(o, i), ls.at[0])
    own.start()
    sent = []

    def send(pred, ref, dst, k, to):
        def copy():
            return rcopy(ref, dst, ss.at[k], rs.at[k], to)

        pl.when(pred)(lambda: copy().start())
        sent.append((pred, copy))

    def got(v, k):
        rcopy(v, v, ss.at[k], rs.at[k], mate).wait_recv()

    R, L, Y = -1, n - 2, 2 * n - 2
    send(o < n - 1, src, view(o, i), R + 1, right)
    send(o > 0, src, view(o, i), L + 1, left)
    c = rcopy(src, view(o, i), ss.at[Y], rs.at[Y], mate)
    c.start()
    yield
    for k in range(1, n):
        a, b = lax.max(o - k, 0), lax.min(o + k, n - 1)
        from_left, from_right = o >= k, o + k <= n - 1
        pl.when(from_left)(lambda: got(view(a, i), R + k))
        if k < n - 1:
            send(from_left & (o < n - 1), view(a, i), view(a, i), R + k + 1, right)
        send(from_left, view(a, i), view(a, i), Y + k, mate)
        pl.when(from_right)(lambda: got(view(b, i), L + k))
        if k < n - 1:
            send(from_right & (o > 0), view(b, i), view(b, i), L + k + 1, left)
        send(from_right, view(b, i), view(b, i), Y + n - 1 + k, mate)
        yield
    got(view(o, 1 - i), Y)
    for k in range(1, n):
        a, b = lax.max(o - k, 0), lax.min(o + k, n - 1)
        pl.when(o >= k)(lambda: got(view(a, 1 - i), Y + k))
        pl.when(o + k <= n - 1)(lambda: got(view(b, 1 - i), Y + n - 1 + k))
    for pred, copy in sent:
        pl.when(pred)(lambda: copy().wait_send())
    c.wait_send()
    own.wait()


def line_gather_sems(grp):
    n = 4 * grp.no - 3
    return [DMA((n,)), DMA((n,)), DMA((1,))]


def line_scatter_steps(grp, part, out, near, mid, far, ss, rs, ls, inplace):
    o, i = grp.me()
    n = grp.no
    mate = grp.dev(o, 1 - i)
    rows = out.shape[0]
    low = o < n // 2

    def target(j):
        if j == n - 1:
            return o
        down = jnp.where(n - 1 - j > o, n - 1 - j, n - 2 - j)
        up = jnp.where(j < o, j, j + 1)
        return jnp.where(low, down, up)

    sent, own = [], []
    for j in range(n):
        c = rcopy(part(target(j), 1 - i), near.at[j], ss.at[j], rs.at[j], mate)
        c.start()
        sent.append(c)
        if not inplace:
            c = pltpu.make_async_copy(part(target(j), i), mid.at[j], ls.at[j])
            c.start()
            own.append(c)
    yield
    moved = []
    for j in range(n - 1):
        t = target(j)
        held = part(t, i) if inplace else mid.at[j]
        if not inplace:
            own[j].wait()
        rcopy(near.at[j], near.at[j], ss.at[j], rs.at[j], mate).wait_recv()
        for right in (True, False):
            towards = (t > o) if right else (t < o)
            inner = (o > 0) if right else (o < n - 1)
            slot = t if right else jnp.where(t == o - 1, n, t)
            to = grp.dev(o + 1, i) if right else grp.dev(o - 1, i)

            def copy(j=j, slot=slot, to=to, held=held):
                return rcopy(held, far.at[slot], ss.at[n + j], rs.at[n + slot], to)

            @pl.when(towards & inner)
            def _():
                rcopy(far.at[t], far.at[t], ss.at[n + j], rs.at[n + t], mate).wait_recv()
                add_all(held, [held, near.at[j], far.at[t]], rows)

            @pl.when(towards & jnp.logical_not(inner))
            def _():
                add_all(held, [held, near.at[j]], rows)

            pl.when(towards)(lambda: copy().start())
            moved.append((towards, copy))
        yield
    j = n - 1
    held = part(o, i) if inplace else mid.at[j]
    if not inplace:
        own[j].wait()
    rcopy(near.at[j], near.at[j], ss.at[j], rs.at[j], mate).wait_recv()

    def arrived(k):
        rcopy(far.at[k], far.at[k], ss.at[j], rs.at[n + k], mate).wait_recv()

    pl.when(o > 0)(lambda: arrived(o))
    pl.when(o < n - 1)(lambda: arrived(n))
    mine = [held, near.at[j]]
    inside = (o > 0) & (o < n - 1)
    pl.when(inside)(lambda: add_all(out, mine + [far.at[o], far.at[n]], rows))
    pl.when(o == 0)(lambda: add_all(out, mine + [far.at[n]], rows))
    pl.when(o == n - 1)(lambda: add_all(out, mine + [far.at[o]], rows))
    for c in sent:
        c.wait_send()
    for pred, copy in moved:
        pl.when(pred)(lambda: copy().wait_send())


def exchange_steps(grp, src, dst, ss, rs, ls):
    o, i = grp.me()
    no, ni = grp.no, grp.ni
    sent = []
    own = pltpu.make_async_copy(src(o, i), dst(o, i), ls.at[0])
    own.start()
    for a in range(no):
        for b in range(ni):
            if a == 0 and b == 0:
                continue
            to, ti = lax.rem(o + a, no), lax.rem(i + b, ni)
            k = a * ni + b - 1
            c = rcopy(src(to, ti), dst(o, i), ss.at[k], rs.at[k], grp.dev(to, ti))
            c.start()
            sent.append(c)
    yield
    for a in range(no):
        for b in range(ni):
            if a == 0 and b == 0:
                continue
            fo, fi = lax.rem(o - a + no, no), lax.rem(i - b + ni, ni)
            k = a * ni + b - 1
            v = dst(fo, fi)
            rcopy(v, v, ss.at[k], rs.at[k], grp.dev(fo, fi)).wait_recv()
    for c in sent:
        c.wait_send()
    own.wait()


def exchange_sems(grp):
    n = grp.no * grp.ni - 1
    return [DMA((n,)), DMA((n,)), DMA((1,))]


def barrier(groups):
    sem = pltpu.get_barrier_semaphore()
    count = 0
    for grp in groups:
        o, i = grp.me()
        for a in range(grp.no):
            for b in range(grp.ni):
                if a == 0 and b == 0:
                    continue
                to, ti = lax.rem(o + a, grp.no), lax.rem(i + b, grp.ni)
                pl.semaphore_signal(sem, inc=1, device_id=grp.dev(to, ti), device_id_type=MESH)
                count += 1
    pl.semaphore_wait(sem, count)


def run_all(gens):
    live = list(gens)
    while live:
        left = []
        for g in live:
            try:
                next(g)
                left.append(g)
            except StopIteration:
                pass
        live = left


def fused(name, ident, groups, ins, outs, scratch, main, pre=None):
    keys = list(ins) + list(outs)
    in_specs = [pl.BlockSpec(memory_space=space) for _, space in ins.values()]
    out_specs = [pl.BlockSpec(memory_space=space) for _, _, space in outs.values()]
    out_shapes = [jax.ShapeDtypeStruct(shape, dtype) for shape, dtype, _ in outs.values()]
    flat = [x for group in scratch.values() for x in group]

    def kernel(*refs):
        named = dict(zip(keys, refs))
        at = len(keys)
        for key, group in scratch.items():
            named[key] = refs[at : at + len(group)]
            at += len(group)
        if pre is not None:
            pre(named)
        barrier(groups)
        main(named)

    got = pl.pallas_call(
        kernel,
        out_shape=out_shapes,
        in_specs=in_specs,
        out_specs=out_specs,
        scratch_shapes=flat,
        compiler_params=pltpu.CompilerParams(
            collective_id=ident, has_side_effects=True, vmem_limit_bytes=63 * 1024 * 1024
        ),
        name=name,
    )(*[a for a, _ in ins.values()])
    return dict(zip(outs, got))


def step(gen):
    next(gen, None)


def finish(*gens):
    run_all(gens)


def row_loop(rows, fn, size=16):
    def one(r, _):
        fn(pl.ds(pl.multiple_of(r * size, size), size))
        return 0

    lax.fori_loop(0, rows // size, one, 0)


def cols(k, width):
    return pl.ds(pl.multiple_of(k * width, width), width)


def the(k, name):
    got = k[name]
    return got[0] if isinstance(got, tuple) else got


def gelu_tanh(values):
    return (
        0.5
        * values
        * (
            1.0
            + jnp.tanh(math.sqrt(2.0 / math.pi) * (values + 0.044715 * values * values * values))
        )
    )


def dot(a, b, dims=((1,), (0,))):
    return lax.dot_general(a, b, (dims, ((), ())), preferred_element_type=F32)


def make_body(mesh):
    zy, sq = ZY(mesh), SEQ(mesh)
    S = mesh.shape["seq"]
    G = mesh.shape["batch"] * mesh.shape["ctx"]
    W = D // G
    QC = (HEADS // S) * HD

    def gather_steps_inplace(grp, view, ss, rs):
        o, i = grp.me()
        no = grp.no
        mate = grp.dev(o, 1 - i)
        sent = []
        for d in list(range(1, no)) + [0]:
            to = grp.dev(lax.rem(o + d, no), i) if d else mate
            c = rcopy(view(o, i), view(o, i), ss.at[d], rs.at[d], to)
            c.start()
            sent.append(c)
        yield
        for d in range(1, no):
            v = view(lax.rem(o - d + no, no), i)
            rcopy(v, v, ss.at[d], rs.at[d], mate).wait_recv()
            c = rcopy(v, v, ss.at[no + d - 1], rs.at[no + d - 1], mate)
            c.start()
            sent.append(c)
        yield
        v = view(o, 1 - i)
        rcopy(v, v, ss.at[0], rs.at[0], mate).wait_recv()
        for d in range(1, no):
            v = view(lax.rem(o - d + no, no), 1 - i)
            rcopy(v, v, ss.at[no + d - 1], rs.at[no + d - 1], mate).wait_recv()
        for c in sent:
            c.wait_send()

    def body(
        inputs,
        w_qkv,
        q_bias,
        v_bias,
        w_out,
        out_bias,
        gain_attn,
        shift_attn,
        w_fc,
        fc_bias,
        w_proj,
        proj_bias,
        gain_mlp,
        shift_mlp,
        cotangent,
    ):
        rows_in = inputs[0]
        R = rows_in.shape[0]
        g_out = cotangent[0]
        vb = v_bias.shape[0]
        place_zy = lax.axis_index(("batch", "ctx"))
        lift = lambda v: v.astype(F32)
        line_of = lax.broadcasted_iota(jnp.int32, (8, W), 0)
        small = jnp.broadcast_to(
            lax.dynamic_update_slice_in_dim(jnp.zeros((W,), F32), lift(v_bias), place_zy * vb, 0), (8, W)
        )
        for n, v in enumerate(
            (gain_attn, shift_attn, q_bias, out_bias, proj_bias, gain_mlp, shift_mlp)
        ):
            small = jnp.where(line_of == n, lift(v), small)
        T = S * R
        NQ = min(256, T)
        HL = QC // HD
        NB = HL * (T // NQ)
        HALF = T // 2
        score_scale = 1.0 / math.sqrt(HD)
        ffl = w_fc.shape[1] // G
        fc_rows = W // S

        def front_main(k):
            c, sid = lax.axis_index("ctx"), lax.axis_index("seq")
            vec, span, normed = k["vec"], k["span"][0], k["normed_s"][0]
            w_in, w_back = k["w_in_s"][0], k["w_back_s"][0]
            row_of = lambda o, i: cols(o * zy.ni + i, W)
            sm = gather_steps(zy, k["small"], lambda o, i: vec.at[:, row_of(o, i)], *k["sm_g"])
            sp = gather_steps(sq, k["rows"], lambda o, i: span.at[cols(2 * o + i, R)], *k["sp_g"])
            wk = gather_steps(
                zy,
                k["w_qkv"].at[:, D : D + 2 * HD],
                lambda o, i: w_in.at[row_of(o, i), QC : QC + 2 * HD],
                *k["wk_g"],
            )
            wq = gather_steps(
                zy,
                k["w_qkv"].at[:, cols(sid, QC)],
                lambda o, i: w_in.at[row_of(o, i), :QC],
                *k["wq_g"],
            )
            wb = gather_steps(
                zy, k["w_out"].at[:, cols(sid, QC)], lambda o, i: w_back.at[row_of(o, i)], *k["wb_g"]
            )
            gg = gather_steps(
                zy, k["cot"], lambda o, i: k["g_all"].at[o * zy.ni + i], *k["gg_g"]
            )

            def spread_fc():
                yield from exchange_steps(
                    zy,
                    lambda o, i: k["w_fc"].at[cols(sid, fc_rows), cols(o * zy.ni + i, ffl)],
                    lambda o, i: k["fc"].at[o * zy.ni + i, sid],
                    *k["fc_x"],
                )
                yield from gather_steps_inplace(sq, lambda o, i: k["fc"].at[:, 2 * o + i], *k["fc_g"])

            fc = spread_fc()
            step(sm)
            step(sp)
            step(wk)
            step(wq)
            for _ in range(zy.no - 1):
                step(sm)
                step(wk)
            finish(sm)
            step(wq)
            finish(sp)
            gain, shift = vec[0:1], vec[1:2]

            def norm_rows(at):
                v = span[at].astype(F32)
                v = v - jnp.mean(v, axis=-1, keepdims=True)
                v = v * lax.rsqrt(jnp.mean(v * v, axis=-1, keepdims=True) + 1e-05)
                normed[at] = (v * gain + shift).astype(BF)

            row_loop(T, norm_rows)
            step(wq)
            finish(wk)
            v_bias_row = sum([vec[7:8, b * W : b * W + HD] for b in range(1, G)], vec[7:8, :HD])

            def key_rows(b, _):
                at = cols(b, NQ)
                mixed = dot(normed[at], w_in[:, QC:])
                k["kv"][at, :HD] = mixed[:, :HD].astype(BF)
                k["kv"][at, HD:] = (mixed[:, HD:] + v_bias_row).astype(BF)
                return 0

            lax.fori_loop(0, T // NQ, key_rows, 0)
            swap = rcopy(
                k["kv"], k["other"], k["swap"][0].at[0], k["swap"][1].at[0], {"ctx": 1 - c}
            )
            swap.start()
            step(wq)
            saves = [
                pltpu.make_async_copy(normed, k["normed"], k["save"][0].at[0]),
                pltpu.make_async_copy(w_in, k["w_in"], k["save"][0].at[1]),
                pltpu.make_async_copy(w_back, k["w_back"], k["save"][0].at[2]),
                pltpu.make_async_copy(k["att_s"][0], k["att_rows"], k["save"][0].at[3]),
            ]
            saves[0].start()
            step(fc)
            step(wb)
            finish(wq)
            saves[1].start()
            q_bias_row = vec[2:3, cols(sid, QC)]

            def query_rows(b, _):
                at = cols(b, NQ)
                k["q"][at] = (dot(normed[at], w_in[:, :QC]) + q_bias_row).astype(BF)
                return 0

            lax.fori_loop(0, T // NQ, query_rows, 0)
            swap.wait()
            step(wb)
            step(gg)
            far_bias = (1 - c).astype(F32) * -1e30
            att = k["att"][0]

            def attend(n, _):
                h, first = lax.rem(n, HL), (n // HL) * NQ
                at = pl.ds(pl.multiple_of(first, NQ), NQ)
                hc = cols(h, HD)
                q = k["q"][at, hc]
                s0 = dot(q, k["kv"][:, :HD], ((1,), (1,))) * score_scale
                s1 = dot(q, k["other"][:, :HD], ((1,), (1,))) * score_scale + far_bias
                qpos = first + lax.broadcasted_iota(jnp.int32, s0.shape, 0)
                kpos = lax.broadcasted_iota(jnp.int32, s0.shape, 1)
                s0 = jnp.where(kpos <= qpos, s0, -1e30)
                top = jnp.maximum(
                    jnp.max(s0, axis=-1, keepdims=True), jnp.max(s1, axis=-1, keepdims=True)
                )
                p0, p1 = jnp.exp(s0 - top), jnp.exp(s1 - top)
                total = jnp.sum(p0, axis=-1, keepdims=True) + jnp.sum(p1, axis=-1, keepdims=True)
                inv = 1.0 / total
                att[at, hc] = (
                    dot((p0 * inv).astype(BF), k["kv"][:, HD:])
                    + dot((p1 * inv).astype(BF), k["other"][:, HD:])
                ).astype(BF)
                return 0

            att_s = k["att_s"][0]
            ag = []
            for half in range(2):
                lax.fori_loop(half * NB // 2, (half + 1) * NB // 2, attend, 0)
                lines = pl.ds(half * HALF, HALF)
                g = gather_steps(
                    sq,
                    att.at[lines],
                    lambda o, i, lines=lines: att_s.at[lines, cols(2 * o + i, QC)],
                    *k["at_g%d" % half],
                )
                step(g)
                ag.append(g)
                step(wb)
                step(fc)
            finish(wb)
            saves[2].start()
            br, brn = k["br"][0], k["brn"][0]
            for half in range(2):
                step(gg)
                finish(ag[half])

                def branch_rows(b, _):
                    at = cols(half * (S // 2) + b, R)
                    br[at] = dot(att_s[at], w_back[...]).astype(BF)
                    return 0

                lax.fori_loop(0, S // 2, branch_rows, 0)
            saves[3].start()
            bx = exchange_steps(
                sq,
                lambda o, i: br.at[cols(2 * o + i, R)],
                lambda o, i: brn.at[:, cols(2 * o + i, QC)],
                *k["br_x"],
            )
            step(bx)
            step(fc)
            finish(bx)
            ob, gain2, shift2 = vec[3:4], vec[5:6], vec[6:7]
            nm = k["nm"][0]

            def norm_rows_two(at):
                v = k["rows"][at].astype(F32) + brn[at].astype(F32) + ob
                k["residual"][at] = v
                v = v - jnp.mean(v, axis=-1, keepdims=True)
                v = v * lax.rsqrt(jnp.mean(v * v, axis=-1, keepdims=True) + 1e-05)
                nm[at] = (v * gain2 + shift2).astype(BF)

            row_loop(R, norm_rows_two)
            xg = gather_steps(zy, nm, lambda o, i: k["x_all"].at[o * zy.ni + i], *k["xg_g"])
            step(xg)
            finish(gg, xg, fc)
            for c_ in saves:
                c_.wait()

        f = fused(
            "front",
            1,
            [zy, sq],
            dict(
                small=(small, VMEM),
                rows=(rows_in, VMEM),
                w_qkv=(w_qkv, VMEM),
                w_out=(w_out, VMEM),
                w_fc=(w_fc, VMEM),
                cot=(g_out, VMEM),
            ),
            dict(
                vec=((8, D), F32, VMEM),
                normed=((T, D), BF, ANY),
                w_in=((D, QC + 2 * HD), BF, ANY),
                w_back=((D, QC), BF, ANY),
                q=((T, QC), BF, VMEM),
                kv=((T, 2 * HD), BF, VMEM),
                other=((T, 2 * HD), BF, VMEM),
                att_rows=((T, D), BF, ANY),
                residual=((R, D), F32, VMEM),
                fc=((G, S, fc_rows, ffl), BF, ANY),
                g_all=((G, R, D), BF, ANY),
                x_all=((G, R, D), BF, ANY),
            ),
            dict(
                span=[VMEM((T, D), BF)],
                normed_s=[VMEM((T, D), BF)],
                w_in_s=[VMEM((D, QC + 2 * HD), BF)],
                w_back_s=[VMEM((D, QC), BF)],
                att=[VMEM((T, QC), BF)],
                att_s=[VMEM((T, D), BF)],
                br=[VMEM((T, QC), BF)],
                brn=[VMEM((R, D), BF)],
                nm=[VMEM((R, D), BF)],
                sm_g=gather_sems(zy),
                sp_g=gather_sems(sq),
                wk_g=gather_sems(zy),
                wq_g=gather_sems(zy),
                wb_g=gather_sems(zy),
                gg_g=gather_sems(zy),
                xg_g=gather_sems(zy),
                fc_x=exchange_sems(zy),
                fc_g=gather_sems(sq)[:2],
                at_g0=gather_sems(sq),
                at_g1=gather_sems(sq),
                br_x=exchange_sems(sq),
                swap=[DMA((1,)), DMA((1,))],
                save=[DMA((4,))],
            ),
            front_main,
        )
        vec = f["vec"]
        normed, w_in, w_back, att_rows = f["normed"], f["w_in"], f["w_back"], f["att_rows"]
        queries, keyval, other, residual = f["q"], f["kv"], f["other"], f["residual"]
        x_all, g_all, fc_cols = f["x_all"], f["g_all"], f["fc"]
        x_all = x_all.reshape(G * R, D)
        g_rows = g_all.reshape(G * R, D)
        fc = fc_cols.reshape(D, ffl)
        hidden = dot(x_all, fc) + fc_bias.astype(F32)
        active, gelu_back = jax.vjp(gelu_tanh, hidden)
        active_low = active.astype(BF)
        y_part = dot(active_low, w_proj).astype(BF)
        grad_active = dot(g_rows, w_proj, ((1,), (1,)))
        grad_hidden = gelu_back(grad_active)[0].astype(BF)
        grad_fc_bias = jnp.sum(grad_hidden.astype(F32), axis=0)
        gx_part = dot(grad_hidden, fc, ((1,), (1,))).astype(BF)
        d_proj = dot(active_low, g_rows, ((0,), (0,))).astype(BF)
        d_fc = dot(x_all, grad_hidden, ((0,), (0,))).astype(BF)
        rows_d = (R, D)
        far_out = (ffl // S, D)

        def load(k, n):
            name, key = (("w_back", "mats"), ("att_rows", "lines"), ("w_in", "mats"), ("normed", "lines"))[n]
            src, dst = k[name], k[key][0]
            if n == 0:
                dst = dst.at[:, :QC]
            return pltpu.make_async_copy(src, dst, k["load"][0].at[n])

        merged = T * D <= 1024 * 2048

        def back_pre(k):
            load(k, 0).start()
            if merged:
                load(k, 1).start()

        def output_rows(k):
            def rows_at(at):
                total = k["residual"][at] + k["sum_one"][0][at] + k["vec"][4:5]
                k["layer_out"][at] = total.astype(BF)

            row_loop(R, rows_at)

        def out_weight(k):
            do = k["do"][0]

            def weight_o(b, _):
                do[b] = dot(k["lines"][0][:, cols(b, W)], the(k, "gbs")[...], ((0,), (0,))).astype(BF)
                return 0

            lax.fori_loop(0, G, weight_o, 0)
            load(k, 3).start()
            og = scatter_steps(
                zy, lambda o, i: do.at[o * zy.ni + i], k["o_acc"][0], *k["o_s"], inplace=True
            )
            step(og)
            return og

        def back_main(k):
            if merged:
                back_rest(k, *back_first(k))
                return
            back_first(k)

        def back_first(k):
            mats, wide = k["mats"][0], k["wide"][0]
            small, sum_one = the(k, "small"), k["sum_one"][0]
            gx = scatter_steps(zy, lambda o, i: k["gx"].at[o * zy.ni + i], sum_one, *k["gx_s"])
            y_scr = [k["y_s"][0], k["gx_s"][1], *k["y_s"][2:]]
            yy = scatter_steps(zy, lambda o, i: k["y"].at[o * zy.ni + i], sum_one, *y_scr)

            def sum_proj():
                acc = k["pj_acc"][0]
                yield from scatter_steps(
                    sq, lambda o, i: k["d_proj"].at[2 * o + i], acc, *k["pj_s"]
                )
                yield from gather_steps(
                    sq, acc, lambda o, i: k["d_proj_all"].at[2 * o + i], *k["pj_g"]
                )

            pj = sum_proj()
            step(gx)
            step(pj)
            small[...] = jnp.zeros(small.shape, F32)
            step(pj)
            step(gx)
            step(pj)
            step(gx)
            step(pj)
            step(gx)
            finish(gx)
            gain_mlp_row, g_res, gbs = k["vec"][5:6], the(k, "g_res"), the(k, "gbs")

            def norm_back_mlp(at):
                v = k["residual"][at]
                center = jnp.mean(v, axis=-1, keepdims=True)
                v = v - center
                scale = lax.rsqrt(jnp.mean(v * v, axis=-1, keepdims=True) + 1e-05)
                v = v * scale
                dn = sum_one[at]
                g = k["cot"][at].astype(F32)
                small[4:5] += jnp.sum(g, axis=0, keepdims=True)
                small[5:6] += jnp.sum(dn * v, axis=0, keepdims=True)
                small[6:7] += jnp.sum(dn, axis=0, keepdims=True)
                dn = dn * gain_mlp_row
                c1 = jnp.mean(dn, axis=-1, keepdims=True)
                c2 = jnp.mean(dn * v, axis=-1, keepdims=True)
                total = g + scale * (dn - c1 - v * c2)
                small[1:2] += jnp.sum(total, axis=0, keepdims=True)
                g_res[at] = total
                k["gb"][0][at] = total.astype(BF)

            row_loop(R, norm_back_mlp)
            gb = exchange_steps(
                sq,
                lambda o, i: k["gb"][0].at[:, cols(2 * o + i, QC)],
                lambda o, i: gbs.at[cols(2 * o + i, R)],
                *k["gb_x"],
            )
            step(gb)
            step(yy)
            step(pj)
            load(k, 0).wait()
            finish(gb)

            def back_cols(b, _):
                at = cols(b, QC)
                wide[:, at] = dot(gbs[...], mats[at, :QC], ((1,), (1,))).astype(BF)
                return 0

            lax.fori_loop(0, S, back_cols, 0)
            at_ = scatter_steps(
                sq,
                lambda o, i: wide.at[:, cols(2 * o + i, QC)],
                the(k, "g_att"),
                *k["ga_s"],
                inplace=True,
            )
            step(at_)
            if merged:
                load(k, 2).start()
                load(k, 1).wait()
            step(at_)
            og = out_weight(k) if merged else None
            finish(at_)
            finish(pj)
            if not merged:
                finish(yy)
                output_rows(k)
            return og, yy

        def back_rest(k, og, yy):
            mats, lines, wide = k["mats"][0], k["lines"][0], k["wide"][0]
            small, g_res = k["small"][0], the(k, "g_res")
            own, oth = k["dkv_own"][0], k["dkv_oth"][0]
            own[...] = jnp.zeros(own.shape, F32)
            oth[...] = jnp.zeros(oth.shape, F32)
            fcg = grad_fc(k)
            step(fcg)
            far_bias = (1 - lax.axis_index("ctx")).astype(F32) * -1e30

            def attend_back(n, _):
                h, first = n // (T // NQ), lax.rem(n, T // NQ) * NQ
                at = pl.ds(pl.multiple_of(first, NQ), NQ)
                hc = cols(h, HD)
                q, g = k["q"][at, hc], the(k, "g_att")[at, hc]
                kv0, kv1 = k["kv"], k["other"]
                s0 = dot(q, kv0[:, :HD], ((1,), (1,))) * score_scale
                s1 = dot(q, kv1[:, :HD], ((1,), (1,))) * score_scale + far_bias
                qpos = first + lax.broadcasted_iota(jnp.int32, s0.shape, 0)
                kpos = lax.broadcasted_iota(jnp.int32, s0.shape, 1)
                s0 = jnp.where(kpos <= qpos, s0, -1e30)
                top = jnp.maximum(
                    jnp.max(s0, axis=-1, keepdims=True), jnp.max(s1, axis=-1, keepdims=True)
                )
                p0, p1 = jnp.exp(s0 - top), jnp.exp(s1 - top)
                total = jnp.sum(p0, axis=-1, keepdims=True) + jnp.sum(p1, axis=-1, keepdims=True)
                inv = 1.0 / total
                p0, p1 = p0 * inv, p1 * inv
                own[:, HD:] += dot(p0.astype(BF), g, ((0,), (0,)))
                oth[:, HD:] += dot(p1.astype(BF), g, ((0,), (0,)))
                e0 = dot(g, kv0[:, HD:], ((1,), (1,)))
                e1 = dot(g, kv1[:, HD:], ((1,), (1,)))
                inner = jnp.sum(p0 * e0, axis=-1, keepdims=True) + jnp.sum(
                    p1 * e1, axis=-1, keepdims=True
                )
                d0 = (p0 * (e0 - inner) * score_scale).astype(BF)
                d1 = (p1 * (e1 - inner) * score_scale).astype(BF)
                own[:, :HD] += dot(d0, q, ((0,), (0,)))
                oth[:, :HD] += dot(d1, q, ((0,), (0,)))
                k["gq"][0][at, hc] = (dot(d0, kv0[:, :HD]) + dot(d1, kv1[:, :HD])).astype(BF)
                return 0

            def part_of(lo, hi):
                lax.fori_loop(NB * lo // 4, NB * hi // 4, attend_back, 0)

            part_of(0, 1)
            if merged:
                step(yy)
            step(fcg)
            part_of(1, 2)
            if merged:
                step(yy)
            step(fcg)
            part_of(2, 3)
            if merged:
                step(yy)
            step(og)
            step(fcg)
            part_of(3, 4)
            c = lax.axis_index("ctx")
            k["gkv_out"][0][...] = oth[...].astype(BF)
            swap = rcopy(
                k["gkv_out"][0],
                k["gkv_in"][0],
                k["swap"][0].at[0],
                k["swap"][1].at[0],
                {"ctx": 1 - c},
            )
            swap.start()
            gq, dq = k["gq"][0], k["dq"][0]
            step(og)
            load(k, 2).wait()
            load(k, 3).wait()

            def weight_q(b, _):
                dq[b] = dot(lines[:, cols(b, W)], gq[...], ((0,), (0,))).astype(BF)
                return 0

            lax.fori_loop(0, G, weight_q, 0)
            qg = scatter_steps(
                zy, lambda o, i: dq.at[o * zy.ni + i], k["q_acc"][0], *k["q_s"], inplace=True
            )
            step(og)
            step(qg)
            swap.wait()
            gkv = k["gkv"][0]
            gkv[...] = (own[...] + k["gkv_in"][0][...].astype(F32)).astype(BF)

            def back_in(b, _):
                at = cols(b, R)
                wide[at] = (
                    dot(gq[at], mats[:, :QC], ((1,), (1,)))
                    + dot(gkv[at], mats[:, QC:], ((1,), (1,)))
                ).astype(BF)
                return 0

            lax.fori_loop(0, S, back_in, 0)
            gng = scatter_steps(
                sq,
                lambda o, i: wide.at[cols(2 * o + i, R)],
                k["gn_sum"][0],
                *k["gn_s"],
                inplace=True,
            )
            step(gng)
            dkv = k["dkv"][0]

            def weight_kv(b, _):
                dkv[b] = dot(lines[:, cols(b, W)], gkv[...], ((0,), (0,))).astype(BF)
                return 0

            lax.fori_loop(0, G, weight_kv, 0)
            vg = scatter_steps(
                zy, lambda o, i: dkv.at[o * zy.ni + i], k["v_acc"][0], *k["v_s"], inplace=True
            )
            step(gng)
            step(vg)
            if merged:
                finish(yy)
                output_rows(k)
            finish(og)
            step(qg)
            step(fcg)
            finish(gng)
            gain_row = k["vec"][0:1]

            def norm_back_rows(at):
                v = k["rows"][at].astype(F32)
                center = jnp.mean(v, axis=-1, keepdims=True)
                v = v - center
                scale = lax.rsqrt(jnp.mean(v * v, axis=-1, keepdims=True) + 1e-05)
                v = v * scale
                dn = k["gn_sum"][0][at]
                small[2:3] += jnp.sum(dn * v, axis=0, keepdims=True)
                small[3:4] += jnp.sum(dn, axis=0, keepdims=True)
                dn = dn * gain_row
                c1 = jnp.mean(dn, axis=-1, keepdims=True)
                c2 = jnp.mean(dn * v, axis=-1, keepdims=True)
                k["input_grad"][at] = g_res[at] + scale * (dn - c1 - v * c2)

            row_loop(R, norm_back_rows)
            small[0:1, cols(lax.axis_index("seq"), QC)] = jnp.sum(
                gq[...].astype(F32), axis=0, keepdims=True
            )
            v_sum = jnp.sum(gkv[:, HD:].astype(F32), axis=0, keepdims=True)
            for b in range(G):
                small[7:8, b * W : b * W + HD] = v_sum

            def small_sums():
                got, line = k["s_got"][0], k["s_line"][0]
                yield from exchange_steps(
                    zy,
                    lambda o, i: small.at[:, cols(o * zy.ni + i, W)],
                    lambda o, i: got.at[o * zy.ni + i],
                    *k["s_x"],
                )
                line[:, :W] = sum([got[b] for b in range(1, G)], got[0])
                line[:, W:] = k["fc_terms"][...]
                yield
                yield from gather_steps(
                    sq, line, lambda o, i: k["s_all"][0].at[2 * o + i], *k["s_g"]
                )

            sg = small_sums()
            step(sg)
            step(qg)
            step(vg)
            step(fcg)
            step(sg)
            step(qg)
            step(vg)
            step(fcg)
            step(sg)
            finish(qg, vg)
            tails = [
                gather_steps(
                    sq, k["o_acc"][0], lambda o, i: k["o_all"].at[:, cols(2 * o + i, QC)], *k["o_g"]
                ),
                gather_steps(
                    sq, k["q_acc"][0], lambda o, i: k["q_all"].at[:, cols(2 * o + i, QC)], *k["q_g"]
                ),
                gather_steps(sq, k["v_acc"][0], lambda o, i: k["v_all"].at[2 * o + i], *k["v_g"]),
            ]
            finish(sg, *tails, fcg)
            tot = k["s_all"][0][0]
            for b in range(1, S):
                tot = tot + k["s_all"][0][b]
            k["s_sum"][...] = tot

        def grad_fc(k):
            acc, line = k["fc_acc"][0], k["fc_line"][0]
            yield from scatter_steps(sq, lambda o, i: k["d_fc"].at[:, 2 * o + i], acc, *k["fc_s"])
            yield from exchange_steps(
                zy,
                lambda o, i: acc.at[o * zy.ni + i],
                lambda o, i: line.at[:, cols(o * zy.ni + i, ffl)],
                *k["fc_x"],
            )
            yield from gather_steps(
                sq, line, lambda o, i: k["fc_all"].at[cols(2 * o + i, fc_rows)], *k["fc_g"]
            )

        fc_shape = (G, fc_rows, ffl)
        ins_one = dict(
            gx=(gx_part.reshape(G, R, D), ANY),
            y=(y_part.reshape(G, R, D), ANY),
            d_proj=(d_proj.reshape((S,) + far_out), ANY),
            cot=(g_out, VMEM),
            residual=(residual, VMEM),
            vec=(vec, VMEM),
            w_back=(w_back, ANY),
        )
        ins_two = dict(
            d_fc=(d_fc.reshape(G, S, fc_rows, ffl), ANY),
            rows=(rows_in, VMEM),
            att_rows=(att_rows, ANY),
            normed=(normed, ANY),
            w_in=(w_in, ANY),
            q=(queries, VMEM),
            kv=(keyval, VMEM),
            other=(other, VMEM),
            fc_terms=(grad_fc_bias.reshape(8, -1), VMEM),
        )
        outs_one = dict(
            layer_out=(rows_d, BF, VMEM),
            d_proj_all=((S,) + far_out, BF, ANY),
        )
        outs_two = dict(
            input_grad=((R, D), F32, VMEM),
            o_all=((W, D), BF, ANY),
            q_all=((W, D), BF, ANY),
            v_all=((S, W, 2 * HD), BF, ANY),
            fc_all=((W, G * ffl), BF, ANY),
            s_sum=((8, W + ffl // 8), F32, VMEM),
        )
        scr_one = dict(
            gx_s=scatter_scratch(zy, rows_d, BF),
            y_s=scatter_scratch(zy, rows_d, BF, mid=False),
            pj_acc=[VMEM(far_out, BF)],
            pj_s=scatter_scratch(sq, far_out, BF),
            pj_g=gather_sems(sq),
            gb=[VMEM(rows_d, BF)],
            gb_x=exchange_sems(sq),
            ga_s=scatter_scratch(sq, (T, QC), BF, mid=False),
            sum_one=[VMEM(rows_d, F32)],
        )
        scr_two = dict(
            lines=[VMEM((T, D), BF)],
            do=[VMEM((G, W, QC), BF)],
            dkv_own=[VMEM((T, 2 * HD), F32)],
            dkv_oth=[VMEM((T, 2 * HD), F32)],
            gkv_out=[VMEM((T, 2 * HD), BF)],
            gkv_in=[VMEM((T, 2 * HD), BF)],
            gkv=[VMEM((T, 2 * HD), BF)],
            swap=[DMA((1,)), DMA((1,))],
            gq=[VMEM((T, QC), BF)],
            dq=[VMEM((G, W, QC), BF)],
            dkv=[VMEM((G, W, 2 * HD), BF)],
            gn_sum=[VMEM((R, D), F32)],
            gn_s=scatter_scratch(sq, (R, D), BF, mid=False),
            o_acc=[VMEM((W, QC), BF)],
            q_acc=[VMEM((W, QC), BF)],
            v_acc=[VMEM((W, 2 * HD), BF)],
            o_s=scatter_scratch(zy, (W, QC), BF, mid=False),
            q_s=scatter_scratch(zy, (W, QC), BF, mid=False),
            v_s=scatter_scratch(zy, (W, 2 * HD), BF, mid=False),
            o_g=gather_sems(sq),
            q_g=gather_sems(sq),
            v_g=gather_sems(sq),
            fc_acc=[VMEM(fc_shape, BF)],
            fc_line=[VMEM((fc_rows, G * ffl), BF)],
            fc_s=scatter_scratch(sq, fc_shape, BF),
            fc_x=exchange_sems(zy),
            fc_g=gather_sems(sq),
            s_got=[VMEM((G, 8, W), F32)],
            s_line=[VMEM((8, W + ffl // 8), F32)],
            s_all=[VMEM((S, 8, W + ffl // 8), F32)],
            s_x=exchange_sems(zy),
            s_g=gather_sems(sq),
        )
        scr_both = dict(
            load=[DMA((4,))],
            mats=[VMEM((D, QC + 2 * HD), BF)],
            wide=[VMEM((T, D), BF)],
        )
        passed = dict(
            gbs=[VMEM((T, QC), BF)],
            g_res=[VMEM(rows_d, F32)],
            g_att=[VMEM((T, QC), BF)],
            small=[VMEM((8, D), F32)],
        )
        if merged:
            b2 = fused(
                "back",
                6,
                [zy, sq],
                {**ins_one, **ins_two},
                {**outs_one, **outs_two},
                {**scr_one, **scr_two, **scr_both, **passed},
                back_main,
                back_pre,
            )
        else:
            left = {n: (v[0].shape, v[0].dtype, VMEM) for n, v in passed.items()}
            b1 = fused(
                "back_one",
                6,
                [zy, sq],
                ins_one,
                {**outs_one, **left},
                {**scr_one, **scr_both},
                back_main,
                back_pre,
            )
            given = {n: (b1[n], VMEM) for n in passed if n != "small"}
            given["start"] = (b1["small"], VMEM)

            def rest_main(k):
                for n in (1, 2):
                    load(k, n).start()
                k["small"][0][...] = k["start"][...]
                load(k, 1).wait()
                back_rest(k, out_weight(k), None)

            b2 = fused(
                "back_two",
                7,
                [zy, sq],
                {**ins_two, **given, "vec": (vec, VMEM)},
                outs_two,
                {**scr_two, **scr_both, "small": passed["small"]},
                rest_main,
            )
            b2 = {**b1, **b2}
        d_proj_all = b2["d_proj_all"]
        sums = b2["s_sum"]
        grad_w_qkv = jnp.concatenate(
            [b2["q_all"].astype(F32), jnp.sum(b2["v_all"].astype(F32), axis=0)], axis=1
        )
        return (
            b2["layer_out"][None],
            b2["input_grad"][None],
            grad_w_qkv,
            sums[0, :W],
            lax.dynamic_slice_in_dim(sums[7, :HD], place_zy * vb, vb, 0),
            b2["o_all"].astype(F32),
            sums[1, :W],
            sums[2, :W],
            sums[3, :W],
            b2["fc_all"].astype(F32),
            sums[:, W:].reshape(-1),
            d_proj_all.reshape(-1, D).astype(F32),
            sums[4, :W],
            sums[5, :W],
            sums[6, :W],
        )

    return body


def solution(mesh):
    rows = P("batch", ("ctx", "seq"), None)
    mat = P(("batch", "ctx"), None)
    vec = P(("batch", "ctx"))
    in_specs = (rows, mat, vec, vec, mat, vec, vec, vec, mat, vec, mat, vec, vec, vec, rows)
    out_specs = (rows, rows, mat, vec, vec, mat, vec, vec, vec, mat, vec, mat, vec, vec, vec)
    return jax.shard_map(
        make_body(mesh), mesh=mesh, in_specs=in_specs, out_specs=out_specs, check_vma=False
    )
```

```python
import functools
import math

import jax
import jax.numpy as jnp
from jax import lax
from jax.experimental import pallas as pl
from jax.experimental.pallas import tpu as pltpu
from jax.sharding import PartitionSpec as P

D = 2048
HEADS = 16
HD = 128
MESH = pl.DeviceIdType.MESH
BF = jnp.bfloat16
F32 = jnp.float32
ANY = pl.ANY
VMEM = pltpu.VMEM
DMA = pltpu.SemaphoreType.DMA


class ZY:
    line = True

    def __init__(self, mesh):
        self.no, self.ni = mesh.shape["batch"], mesh.shape["ctx"]

    def me(self):
        return lax.axis_index("batch"), lax.axis_index("ctx")

    def dev(self, o, i):
        return {"batch": o, "ctx": i}


class SEQ:
    line = False

    def __init__(self, mesh):
        self.no, self.ni = mesh.shape["seq"] // 2, 2

    def me(self):
        s = lax.axis_index("seq")
        return s // 2, lax.rem(s, 2)

    def dev(self, o, i):
        return {"seq": 2 * o + i}


def rcopy(src, dst, ss, rs, dev):
    return pltpu.make_async_remote_copy(
        src_ref=src, dst_ref=dst, send_sem=ss, recv_sem=rs, device_id=dev, device_id_type=MESH
    )


def gather_steps(grp, src, view, ss, rs, ls, ready=None):
    if grp.line:
        return line_gather_steps(grp, src, view, ss, rs, ls, ready)
    return star_gather_steps(grp, src, view, ss, rs, ls)


def star_gather_steps(grp, src, view, ss, rs, ls):
    o, i = grp.me()
    no = grp.no
    mate = grp.dev(o, 1 - i)
    own = pltpu.make_async_copy(src, view(o, i), ls.at[0])
    own.start()
    sent = []
    for d in range(1, no):
        c = rcopy(src, view(o, i), ss.at[d], rs.at[d], grp.dev(lax.rem(o + d, no), i))
        c.start()
        sent.append(c)
    c = rcopy(src, view(o, i), ss.at[0], rs.at[0], mate)
    c.start()
    sent.append(c)
    yield
    for d in range(1, no):
        f = lax.rem(o - d + no, no)
        rcopy(view(f, i), view(f, i), ss.at[d], rs.at[d], mate).wait_recv()
        c = rcopy(view(f, i), view(f, i), ss.at[no + d - 1], rs.at[no + d - 1], mate)
        c.start()
        sent.append(c)
        yield
    rcopy(view(o, 1 - i), view(o, 1 - i), ss.at[0], rs.at[0], mate).wait_recv()
    for d in range(1, no):
        f = lax.rem(o - d + no, no)
        v = view(f, 1 - i)
        rcopy(v, v, ss.at[no + d - 1], rs.at[no + d - 1], mate).wait_recv()
    for c in sent:
        c.wait_send()
    own.wait()


def gather_sems(grp):
    if grp.line:
        return line_gather_sems(grp)
    n = 2 * grp.no - 1
    return [DMA((n,)), DMA((n,)), DMA((1,))]


def add_all(dst, refs, rows, step=16):
    if len(dst.shape) == 3:
        for b in range(dst.shape[0]):
            add_all(dst.at[b], [ref.at[b] for ref in refs], dst.shape[1], step)
        return

    def one(r, _):
        at = pl.ds(pl.multiple_of(r * step, step), step)
        total = refs[0][at].astype(F32)
        for ref in refs[1:]:
            total = total + ref[at].astype(F32)
        dst[at] = total.astype(dst.dtype)
        return 0

    lax.fori_loop(0, rows // step, one, 0)


def scatter_steps(grp, part, out, *scr, inplace=False):
    if grp.line:
        return line_scatter_steps(grp, part, out, *scr, inplace=inplace)
    return star_scatter_steps(grp, part, out, *scr, inplace=inplace)


def star_scatter_steps(grp, part, out, near, mid, far, ss, rs, ls, inplace):
    o, i = grp.me()
    no = grp.no
    mate = grp.dev(o, 1 - i)
    sent, own = [], []
    order = list(range(1, no)) + [0]
    rows = out.shape[0]
    for d in order:
        t = lax.rem(o + d, no)
        c = rcopy(part(t, 1 - i), near.at[d], ss.at[d], rs.at[d], mate)
        c.start()
        sent.append(c)
        if not inplace:
            c = pltpu.make_async_copy(part(t, i), mid.at[d], ls.at[d])
            c.start()
            own.append(c)
    yield
    for n, d in enumerate(order):
        t = lax.rem(o + d, no)
        held = part(t, i) if inplace else mid.at[d]
        if not inplace:
            own[n].wait()
        rcopy(near.at[d], near.at[d], ss.at[d], rs.at[d], mate).wait_recv()
        if d == 0:
            add_all(out, [held, near.at[d]], rows)
        else:
            add_all(held, [held, near.at[d]], rows)
            c = rcopy(
                held, far.at[d - 1], ss.at[no + d - 1], rs.at[no + d - 1], grp.dev(t, i)
            )
            c.start()
            sent.append(c)
            yield
    yield
    for d in range(1, no):
        v = far.at[d - 1]
        rcopy(v, v, ss.at[no + d - 1], rs.at[no + d - 1], mate).wait_recv()
        add_all(out, [out, v], rows)
    for c in sent:
        c.wait_send()


def scatter_scratch(grp, shape, dtype, mid=True):
    no = grp.no
    held = (no,) + shape if mid else (1, 8, 128)
    if grp.line:
        return [
            VMEM((no,) + shape, dtype),
            VMEM(held, dtype),
            VMEM((no + 1,) + shape, dtype),
            DMA((2 * no - 1,)),
            DMA((2 * no + 1,)),
            DMA((no,)),
        ]
    n = 2 * no - 1
    return [
        VMEM((no,) + shape, dtype),
        VMEM(held, dtype),
        VMEM((no - 1,) + shape, dtype),
        DMA((n,)),
        DMA((n,)),
        DMA((no,)),
    ]


def line_gather_steps(grp, src, view, ss, rs, ls, ready):
    o, i = grp.me()
    n = grp.no
    mate, right, left = grp.dev(o, 1 - i), grp.dev(o + 1, i), grp.dev(o - 1, i)
    own = pltpu.make_async_copy(src, view(o, i), ls.at[0])
    own.start()
    sent = []

    def send(pred, ref, dst, k, to):
        def copy():
            return rcopy(ref, dst, ss.at[k], rs.at[k], to)

        pl.when(pred)(lambda: copy().start())
        sent.append((pred, copy))

    def got(v, k):
        rcopy(v, v, ss.at[k], rs.at[k], mate).wait_recv()

    def mates(k):
        a, b = lax.max(o - k, 0), lax.min(o + k, n - 1)
        if k == 0:
            got(view(o, 1 - i), Y)
            own.wait()
            if ready is not None:
                ready(o)
            return
        pl.when(o >= k)(lambda: got(view(a, 1 - i), Y + k))
        pl.when(o + k <= n - 1)(lambda: got(view(b, 1 - i), Y + n - 1 + k))
        if ready is not None:

            def one(t, _):
                ready(jnp.where(t == 0, a, b))
                return 0

            first, last = jnp.where(o >= k, 0, 1), jnp.where(o + k <= n - 1, 2, 1)
            lax.fori_loop(first, last, one, 0)

    R, L, Y = -1, n - 2, 2 * n - 2
    send(o < n - 1, src, view(o, i), R + 1, right)
    send(o > 0, src, view(o, i), L + 1, left)
    c = rcopy(src, view(o, i), ss.at[Y], rs.at[Y], mate)
    c.start()
    yield
    for k in range(1, n):
        a, b = lax.max(o - k, 0), lax.min(o + k, n - 1)
        from_left, from_right = o >= k, o + k <= n - 1
        pl.when(from_left)(lambda: got(view(a, i), R + k))
        if k < n - 1:
            send(from_left & (o < n - 1), view(a, i), view(a, i), R + k + 1, right)
        send(from_left, view(a, i), view(a, i), Y + k, mate)
        pl.when(from_right)(lambda: got(view(b, i), L + k))
        if k < n - 1:
            send(from_right & (o > 0), view(b, i), view(b, i), L + k + 1, left)
        send(from_right, view(b, i), view(b, i), Y + n - 1 + k, mate)
        if ready is not None:
            mates(k - 1)
        yield
    for k in range(n) if ready is None else [n - 1]:
        mates(k)
    for pred, copy in sent:
        pl.when(pred)(lambda: copy().wait_send())
    c.wait_send()


def line_gather_sems(grp):
    n = 4 * grp.no - 3
    return [DMA((n,)), DMA((n,)), DMA((1,))]


def line_scatter_steps(grp, part, out, near, mid, far, ss, rs, ls, inplace):
    o, i = grp.me()
    n = grp.no
    mate = grp.dev(o, 1 - i)
    rows = out.shape[0]
    low = o < n // 2

    def target(j):
        if j == n - 1:
            return o
        down = jnp.where(n - 1 - j > o, n - 1 - j, n - 2 - j)
        up = jnp.where(j < o, j, j + 1)
        return jnp.where(low, down, up)

    sent, own = [], []
    for j in range(n):
        c = rcopy(part(target(j), 1 - i), near.at[j], ss.at[j], rs.at[j], mate)
        c.start()
        sent.append(c)
        if not inplace:
            c = pltpu.make_async_copy(part(target(j), i), mid.at[j], ls.at[j])
            c.start()
            own.append(c)
    yield
    moved = []
    for j in range(n - 1):
        t = target(j)
        held = part(t, i) if inplace else mid.at[j]
        if not inplace:
            own[j].wait()
        rcopy(near.at[j], near.at[j], ss.at[j], rs.at[j], mate).wait_recv()
        for right in (True, False):
            towards = (t > o) if right else (t < o)
            inner = (o > 0) if right else (o < n - 1)
            slot = t if right else jnp.where(t == o - 1, n, t)
            to = grp.dev(o + 1, i) if right else grp.dev(o - 1, i)

            def copy(j=j, slot=slot, to=to, held=held):
                return rcopy(held, far.at[slot], ss.at[n + j], rs.at[n + slot], to)

            @pl.when(towards & inner)
            def _():
                rcopy(far.at[t], far.at[t], ss.at[n + j], rs.at[n + t], mate).wait_recv()
                add_all(held, [held, near.at[j], far.at[t]], rows)

            @pl.when(towards & jnp.logical_not(inner))
            def _():
                add_all(held, [held, near.at[j]], rows)

            pl.when(towards)(lambda: copy().start())
            moved.append((towards, copy))
        yield
    j = n - 1
    held = part(o, i) if inplace else mid.at[j]
    if not inplace:
        own[j].wait()
    rcopy(near.at[j], near.at[j], ss.at[j], rs.at[j], mate).wait_recv()

    def arrived(k):
        rcopy(far.at[k], far.at[k], ss.at[j], rs.at[n + k], mate).wait_recv()

    pl.when(o > 0)(lambda: arrived(o))
    pl.when(o < n - 1)(lambda: arrived(n))
    mine = [held, near.at[j]]
    inside = (o > 0) & (o < n - 1)
    pl.when(inside)(lambda: add_all(out, mine + [far.at[o], far.at[n]], rows))
    pl.when(o == 0)(lambda: add_all(out, mine + [far.at[n]], rows))
    pl.when(o == n - 1)(lambda: add_all(out, mine + [far.at[o]], rows))
    for c in sent:
        c.wait_send()
    for pred, copy in moved:
        pl.when(pred)(lambda: copy().wait_send())


def exchange_steps(grp, src, dst, ss, rs, ls):
    o, i = grp.me()
    no, ni = grp.no, grp.ni
    sent = []
    own = pltpu.make_async_copy(src(o, i), dst(o, i), ls.at[0])
    own.start()
    for a in range(no):
        for b in range(ni):
            if a == 0 and b == 0:
                continue
            to, ti = lax.rem(o + a, no), lax.rem(i + b, ni)
            k = a * ni + b - 1
            c = rcopy(src(to, ti), dst(o, i), ss.at[k], rs.at[k], grp.dev(to, ti))
            c.start()
            sent.append(c)
    yield
    for a in range(no):
        for b in range(ni):
            if a == 0 and b == 0:
                continue
            fo, fi = lax.rem(o - a + no, no), lax.rem(i - b + ni, ni)
            k = a * ni + b - 1
            v = dst(fo, fi)
            rcopy(v, v, ss.at[k], rs.at[k], grp.dev(fo, fi)).wait_recv()
    for c in sent:
        c.wait_send()
    own.wait()


def exchange_sems(grp):
    n = grp.no * grp.ni - 1
    return [DMA((n,)), DMA((n,)), DMA((1,))]


def barrier(groups):
    sem = pltpu.get_barrier_semaphore()
    count = 0
    for grp in groups:
        o, i = grp.me()
        for a in range(grp.no):
            for b in range(grp.ni):
                if a == 0 and b == 0:
                    continue
                to, ti = lax.rem(o + a, grp.no), lax.rem(i + b, grp.ni)
                pl.semaphore_signal(sem, inc=1, device_id=grp.dev(to, ti), device_id_type=MESH)
                count += 1
    pl.semaphore_wait(sem, count)


def run_all(gens):
    live = list(gens)
    while live:
        left = []
        for g in live:
            try:
                next(g)
                left.append(g)
            except StopIteration:
                pass
        live = left


def fused(name, ident, groups, ins, outs, scratch, main, pre=None):
    keys = list(ins) + list(outs)
    in_specs = [pl.BlockSpec(memory_space=space) for _, space in ins.values()]
    out_specs = [pl.BlockSpec(memory_space=space) for _, _, space in outs.values()]
    out_shapes = [jax.ShapeDtypeStruct(shape, dtype) for shape, dtype, _ in outs.values()]
    flat = [x for group in scratch.values() for x in group]

    def kernel(*refs):
        named = dict(zip(keys, refs))
        at = len(keys)
        for key, group in scratch.items():
            named[key] = refs[at : at + len(group)]
            at += len(group)
        if pre is not None:
            pre(named)
        barrier(groups)
        main(named)

    got = pl.pallas_call(
        kernel,
        out_shape=out_shapes,
        in_specs=in_specs,
        out_specs=out_specs,
        scratch_shapes=flat,
        compiler_params=pltpu.CompilerParams(
            collective_id=ident, has_side_effects=True, vmem_limit_bytes=63 * 1024 * 1024
        ),
        name=name,
    )(*[a for a, _ in ins.values()])
    return dict(zip(outs, got))


def step(gen):
    next(gen, None)


def finish(*gens):
    run_all(gens)


def row_loop(rows, fn, size=16):
    def one(r, _):
        fn(pl.ds(pl.multiple_of(r * size, size), size))
        return 0

    lax.fori_loop(0, rows // size, one, 0)


def cols(k, width):
    return pl.ds(pl.multiple_of(k * width, width), width)


def the(k, name):
    got = k[name]
    return got[0] if isinstance(got, tuple) else got


def gelu_tanh(values):
    return (
        0.5
        * values
        * (
            1.0
            + jnp.tanh(math.sqrt(2.0 / math.pi) * (values + 0.044715 * values * values * values))
        )
    )


def dot(a, b, dims=((1,), (0,))):
    return lax.dot_general(a, b, (dims, ((), ())), preferred_element_type=F32)


def make_body(mesh):
    zy, sq = ZY(mesh), SEQ(mesh)
    S = mesh.shape["seq"]
    G = mesh.shape["batch"] * mesh.shape["ctx"]
    W = D // G
    QC = (HEADS // S) * HD

    def gather_steps_inplace(grp, view, ss, rs):
        o, i = grp.me()
        no = grp.no
        mate = grp.dev(o, 1 - i)
        sent = []
        for d in list(range(1, no)) + [0]:
            to = grp.dev(lax.rem(o + d, no), i) if d else mate
            c = rcopy(view(o, i), view(o, i), ss.at[d], rs.at[d], to)
            c.start()
            sent.append(c)
        yield
        for d in range(1, no):
            v = view(lax.rem(o - d + no, no), i)
            rcopy(v, v, ss.at[d], rs.at[d], mate).wait_recv()
            c = rcopy(v, v, ss.at[no + d - 1], rs.at[no + d - 1], mate)
            c.start()
            sent.append(c)
        yield
        v = view(o, 1 - i)
        rcopy(v, v, ss.at[0], rs.at[0], mate).wait_recv()
        for d in range(1, no):
            v = view(lax.rem(o - d + no, no), 1 - i)
            rcopy(v, v, ss.at[no + d - 1], rs.at[no + d - 1], mate).wait_recv()
        for c in sent:
            c.wait_send()

    def body(
        inputs,
        w_qkv,
        q_bias,
        v_bias,
        w_out,
        out_bias,
        gain_attn,
        shift_attn,
        w_fc,
        fc_bias,
        w_proj,
        proj_bias,
        gain_mlp,
        shift_mlp,
        cotangent,
    ):
        rows_in = inputs[0]
        R = rows_in.shape[0]
        g_out = cotangent[0]
        vb = v_bias.shape[0]
        place_zy = lax.axis_index(("batch", "ctx"))
        lift = lambda v: v.astype(F32)
        line_of = lax.broadcasted_iota(jnp.int32, (8, W), 0)
        small = jnp.broadcast_to(
            lax.dynamic_update_slice_in_dim(jnp.zeros((W,), F32), lift(v_bias), place_zy * vb, 0), (8, W)
        )
        for n, v in enumerate(
            (gain_attn, shift_attn, q_bias, out_bias, proj_bias, gain_mlp, shift_mlp)
        ):
            small = jnp.where(line_of == n, lift(v), small)
        T = S * R
        NQ = min(256, T)
        HL = QC // HD
        NB = HL * (T // NQ)
        HALF = T // 2
        score_scale = 1.0 / math.sqrt(HD)
        ffl = w_fc.shape[1] // G
        fc_rows = W // S

        merged = T * D <= 1024 * 2048
        GR = G * R
        FC = min(256, ffl)
        upper = max(T, GR - T)
        mlp_ins, mlp_outs, mlp_scr = {}, {}, {}
        if merged:
            mlp_ins = dict(w_proj=(w_proj, ANY), fcb=(fc_bias.astype(F32)[None], VMEM))
            mlp_outs = dict(
                active=((GR, ffl), BF, ANY),
                grad_hidden=((GR, ffl), BF, ANY),
                y_part=((GR, D), BF, ANY),
                gx_part=((GR, D), BF, ANY),
                gsum=((1, ffl), F32, VMEM),
            )
            mlp_scr = dict(
                xv=[VMEM((G, R, D), BF)],
                gv=[VMEM((G, R, D), BF)],
                fcv=[VMEM((G, S, fc_rows, ffl), BF)],
                wpv=[VMEM((ffl, D), BF)],
                act=[VMEM((GR, ffl), BF)],
                back=[VMEM((GR, ffl), BF)],
                mlp_out=[DMA((5,))],
            )

        def front_main(k):
            c, sid = lax.axis_index("ctx"), lax.axis_index("seq")
            vec, span, normed = k["vec"], k["first"][0].at[:T], k["second"][0].at[:T]
            w_in, w_back = k["w_in_s"][0], k["w_back_s"][0]
            row_of = lambda o, i: cols(o * zy.ni + i, W)
            sm = gather_steps(zy, k["small"], lambda o, i: vec.at[:, row_of(o, i)], *k["sm_g"])
            sp = gather_steps(sq, k["rows"], lambda o, i: span.at[cols(2 * o + i, R)], *k["sp_g"])
            wk = gather_steps(
                zy,
                k["w_qkv"].at[:, D : D + 2 * HD],
                lambda o, i: w_in.at[row_of(o, i), QC : QC + 2 * HD],
                *k["wk_g"],
            )
            wq = gather_steps(
                zy,
                k["w_qkv"].at[:, cols(sid, QC)],
                lambda o, i: w_in.at[row_of(o, i), :QC],
                *k["wq_g"],
            )
            wb = gather_steps(
                zy, k["w_out"].at[:, cols(sid, QC)], lambda o, i: w_back.at[row_of(o, i)], *k["wb_g"]
            )
            g_to, fc_to = (k["gv"][0], k["fcv"][0]) if merged else (k["g_all"], k["fc"])
            gg = gather_steps(zy, k["cot"], lambda o, i: g_to.at[o * zy.ni + i], *k["gg_g"])
            if merged:
                w_load = pltpu.make_async_copy(k["w_proj"], k["wpv"][0], k["save"][0].at[4])
                w_load.start()

            def spread_fc():
                yield from exchange_steps(
                    zy,
                    lambda o, i: k["w_fc"].at[cols(sid, fc_rows), cols(o * zy.ni + i, ffl)],
                    lambda o, i: fc_to.at[o * zy.ni + i, sid],
                    *k["fc_x"],
                )
                yield from gather_steps_inplace(sq, lambda o, i: fc_to.at[:, 2 * o + i], *k["fc_g"])

            fc = spread_fc()
            step(sm)
            step(sp)
            step(wk)
            step(wq)
            for _ in range(zy.no - 1):
                step(sm)
                step(wk)
            finish(sm)
            step(wq)
            finish(sp)
            gain, shift = vec[0:1], vec[1:2]

            def norm_rows(at):
                v = span[at].astype(F32)
                v = v - jnp.mean(v, axis=-1, keepdims=True)
                v = v * lax.rsqrt(jnp.mean(v * v, axis=-1, keepdims=True) + 1e-05)
                normed[at] = (v * gain + shift).astype(BF)

            row_loop(T, norm_rows)
            step(wq)
            finish(wk)
            v_bias_row = sum([vec[7:8, b * W : b * W + HD] for b in range(1, G)], vec[7:8, :HD])

            def key_rows(b, _):
                at = cols(b, NQ)
                mixed = dot(normed[at], w_in[:, QC:])
                k["kv"][at, :HD] = mixed[:, :HD].astype(BF)
                k["kv"][at, HD:] = (mixed[:, HD:] + v_bias_row).astype(BF)
                return 0

            lax.fori_loop(0, T // NQ, key_rows, 0)
            swap = rcopy(
                k["kv"], k["other"], k["swap"][0].at[0], k["swap"][1].at[0], {"ctx": 1 - c}
            )
            swap.start()
            step(wq)
            saves = [
                pltpu.make_async_copy(normed, k["normed"], k["save"][0].at[0]),
                pltpu.make_async_copy(w_in, k["w_in"], k["save"][0].at[1]),
                pltpu.make_async_copy(w_back, k["w_back"], k["save"][0].at[2]),
                pltpu.make_async_copy(k["first"][0].at[T : 2 * T], k["att_rows"], k["save"][0].at[3]),
            ]
            saves[0].start()
            step(fc)
            step(wb)
            finish(wq)
            saves[1].start()
            q_bias_row = vec[2:3, cols(sid, QC)]

            def query_rows(b, _):
                at = cols(b, NQ)
                k["q"][at] = (dot(normed[at], w_in[:, :QC]) + q_bias_row).astype(BF)
                return 0

            lax.fori_loop(0, T // NQ, query_rows, 0)
            swap.wait()
            step(wb)
            step(gg)
            far_bias = (1 - c).astype(F32) * -1e30
            att = k["att"][0]

            def attend(n, _):
                h, first = lax.rem(n, HL), (n // HL) * NQ
                at = pl.ds(pl.multiple_of(first, NQ), NQ)
                hc = cols(h, HD)
                q = k["q"][at, hc]
                s0 = dot(q, k["kv"][:, :HD], ((1,), (1,))) * score_scale
                s1 = dot(q, k["other"][:, :HD], ((1,), (1,))) * score_scale + far_bias
                qpos = first + lax.broadcasted_iota(jnp.int32, s0.shape, 0)
                kpos = lax.broadcasted_iota(jnp.int32, s0.shape, 1)
                s0 = jnp.where(kpos <= qpos, s0, -1e30)
                top = jnp.maximum(
                    jnp.max(s0, axis=-1, keepdims=True), jnp.max(s1, axis=-1, keepdims=True)
                )
                p0, p1 = jnp.exp(s0 - top), jnp.exp(s1 - top)
                total = jnp.sum(p0, axis=-1, keepdims=True) + jnp.sum(p1, axis=-1, keepdims=True)
                inv = 1.0 / total
                att[at, hc] = (
                    dot((p0 * inv).astype(BF), k["kv"][:, HD:])
                    + dot((p1 * inv).astype(BF), k["other"][:, HD:])
                ).astype(BF)
                return 0

            att_s = k["first"][0].at[T : 2 * T]
            ag = []
            for half in range(2):
                lax.fori_loop(half * NB // 2, (half + 1) * NB // 2, attend, 0)
                lines = pl.ds(half * HALF, HALF)
                g = gather_steps(
                    sq,
                    att.at[lines],
                    lambda o, i, lines=lines: att_s.at[lines, cols(2 * o + i, QC)],
                    *k["at_g%d" % half],
                )
                step(g)
                ag.append(g)
                step(wb)
                step(fc)
            finish(wb)
            saves[2].start()
            br, brn = k["br"][0], k["brn"][0]
            for half in range(2):
                step(gg)
                finish(ag[half])

                def branch_rows(b, _):
                    at = cols(half * (S // 2) + b, R)
                    br[at] = dot(att_s[at], w_back[...]).astype(BF)
                    return 0

                lax.fori_loop(0, S // 2, branch_rows, 0)
            saves[3].start()
            bx = exchange_steps(
                sq,
                lambda o, i: br.at[cols(2 * o + i, R)],
                lambda o, i: brn.at[:, cols(2 * o + i, QC)],
                *k["br_x"],
            )
            step(bx)
            step(fc)
            finish(bx)
            ob, gain2, shift2 = vec[3:4], vec[5:6], vec[6:7]
            nm = k["nm"][0]

            def norm_rows_two(at):
                v = k["rows"][at].astype(F32) + brn[at].astype(F32) + ob
                k["residual"][at] = v
                v = v - jnp.mean(v, axis=-1, keepdims=True)
                v = v * lax.rsqrt(jnp.mean(v * v, axis=-1, keepdims=True) + 1e-05)
                nm[at] = (v * gain2 + shift2).astype(BF)

            row_loop(R, norm_rows_two)
            if not merged:
                xg = gather_steps(zy, nm, lambda o, i: k["x_all"].at[o * zy.ni + i], *k["xg_g"])
                step(xg)
                finish(gg, xg, fc)
                for c_ in saves:
                    c_.wait()
                return
            xv, gv, fcv, wpv = k["xv"][0], k["gv"][0], k["fcv"][0], k["wpv"][0]
            act, back, out_sems = k["act"][0], k["back"][0], k["mlp_out"][0]
            RB = zy.ni * R
            gsum = k["gsum"]
            gsum[...] = jnp.zeros(gsum.shape, F32)
            slope = math.sqrt(2.0 / math.pi)

            def results(p):
                at = cols(p, RB)
                pair = pl.ds(p * zy.ni, zy.ni)
                return [
                    pltpu.make_async_copy(src, dst, out_sems.at[n])
                    for n, (src, dst) in enumerate(
                        [
                            (xv.at[pair], k["x_all"].at[pair]),
                            (act.at[at], k["active"].at[at]),
                            (back.at[at], k["grad_hidden"].at[at]),
                            (k["first"][0].at[at], k["y_part"].at[at]),
                            (k["second"][0].at[at], k["gx_part"].at[at]),
                        ]
                    )
                ]

            def mlp_block(p):
                at = cols(p, RB)
                pair = pl.ds(p * zy.ni, zy.ni)

                def hidden_cols(n, _):
                    fa = cols(n, FC)
                    h = dot(xv[pair].reshape(RB, D), fcv[:, :, :, fa].reshape(D, FC)) + k["fcb"][:, fa]
                    sq_h = h * h
                    th = jnp.tanh(slope * (h + 0.044715 * h * sq_h))
                    act[at, fa] = (0.5 * h * (1.0 + th)).astype(BF)
                    rise = 0.5 * (1.0 + th) + (0.5 * slope) * h * (1.0 - th * th) * (
                        1.0 + 3 * 0.044715 * sq_h
                    )
                    g = dot(gv[pair].reshape(RB, D), wpv[fa, :], ((1,), (1,)))
                    gh = (g * rise).astype(BF)
                    back[at, fa] = gh
                    gsum[:, fa] += jnp.sum(gh.astype(F32), axis=0, keepdims=True)
                    return 0

                lax.fori_loop(0, ffl // FC, hidden_cols, 0)

                def token_cols(n, _):
                    da = cols(n, W)
                    k["second"][0][at, da] = dot(
                        back[at, :], fcv[n].reshape(W, ffl), ((1,), (1,))
                    ).astype(BF)
                    k["first"][0][at, da] = dot(act[at, :], wpv[:, da]).astype(BF)
                    return 0

                lax.fori_loop(0, G, token_cols, 0)
                for c_ in results(p):
                    c_.start()

            saves[0].wait()
            saves[3].wait()
            xg = gather_steps(
                zy, nm, lambda o, i: xv.at[o * zy.ni + i], *k["xg_g"], ready=mlp_block
            )
            step(xg)
            finish(gg, fc)
            w_load.wait()
            saves += [
                pltpu.make_async_copy(gv, k["g_all"], k["save"][0].at[5]),
                pltpu.make_async_copy(fcv, k["fc"], k["save"][0].at[6]),
            ]
            saves[4].start()
            saves[5].start()
            finish(xg)
            for c_ in saves[1:3] + saves[4:]:
                c_.wait()
            for p in range(zy.no):
                for c_ in results(p):
                    c_.wait()

        f = fused(
            "front",
            1,
            [zy, sq],
            dict(
                small=(small, VMEM),
                rows=(rows_in, VMEM),
                w_qkv=(w_qkv, VMEM),
                w_out=(w_out, VMEM),
                w_fc=(w_fc, ANY if merged else VMEM),
                cot=(g_out, VMEM),
                **mlp_ins,
            ),
            dict(
                vec=((8, D), F32, VMEM),
                normed=((T, D), BF, ANY),
                w_in=((D, QC + 2 * HD), BF, ANY),
                w_back=((D, QC), BF, ANY),
                q=((T, QC), BF, VMEM),
                kv=((T, 2 * HD), BF, VMEM),
                other=((T, 2 * HD), BF, VMEM),
                att_rows=((T, D), BF, ANY),
                residual=((R, D), F32, VMEM),
                fc=((G, S, fc_rows, ffl), BF, ANY),
                g_all=((G, R, D), BF, ANY),
                x_all=((G, R, D), BF, ANY),
                **mlp_outs,
            ),
            dict(
                first=[VMEM((T + upper, D), BF)],
                second=[VMEM((max(T, GR) if merged else T, D), BF)],
                w_in_s=[VMEM((D, QC + 2 * HD), BF)],
                w_back_s=[VMEM((D, QC), BF)],
                att=[VMEM((T, QC), BF)],
                br=[VMEM((T, QC), BF)],
                brn=[VMEM((R, D), BF)],
                nm=[VMEM((R, D), BF)],
                sm_g=gather_sems(zy),
                sp_g=gather_sems(sq),
                wk_g=gather_sems(zy),
                wq_g=gather_sems(zy),
                wb_g=gather_sems(zy),
                gg_g=gather_sems(zy),
                xg_g=gather_sems(zy),
                fc_x=exchange_sems(zy),
                fc_g=gather_sems(sq)[:2],
                at_g0=gather_sems(sq),
                at_g1=gather_sems(sq),
                br_x=exchange_sems(sq),
                swap=[DMA((1,)), DMA((1,))],
                save=[DMA((7,))],
                **mlp_scr,
            ),
            front_main,
        )
        vec = f["vec"]
        normed, w_in, w_back, att_rows = f["normed"], f["w_in"], f["w_back"], f["att_rows"]
        queries, keyval, other, residual = f["q"], f["kv"], f["other"], f["residual"]
        x_all, g_all, fc_cols = f["x_all"], f["g_all"], f["fc"]
        x_all = x_all.reshape(G * R, D)
        g_rows = g_all.reshape(G * R, D)
        fc = fc_cols.reshape(D, ffl)
        if merged:
            active_low, grad_hidden = f["active"], f["grad_hidden"]
            y_part, gx_part = f["y_part"], f["gx_part"]
            grad_fc_bias = f["gsum"][0]
        else:
            hidden = dot(x_all, fc) + fc_bias.astype(F32)
            active, gelu_back = jax.vjp(gelu_tanh, hidden)
            active_low = active.astype(BF)
            y_part = dot(active_low, w_proj).astype(BF)
            grad_active = dot(g_rows, w_proj, ((1,), (1,)))
            grad_hidden = gelu_back(grad_active)[0].astype(BF)
            grad_fc_bias = jnp.sum(grad_hidden.astype(F32), axis=0)
            gx_part = dot(grad_hidden, fc, ((1,), (1,))).astype(BF)
        d_proj = dot(active_low, g_rows, ((0,), (0,))).astype(BF)
        d_fc = dot(x_all, grad_hidden, ((0,), (0,))).astype(BF)
        rows_d = (R, D)
        far_out = (ffl // S, D)

        def load(k, n):
            name, key = (("w_back", "mats"), ("att_rows", "lines"), ("w_in", "mats"), ("normed", "lines"))[n]
            src, dst = k[name], k[key][0]
            if n == 0:
                dst = dst.at[:, :QC]
            return pltpu.make_async_copy(src, dst, k["load"][0].at[n])

        def back_pre(k):
            load(k, 0).start()
            if merged:
                load(k, 1).start()

        def output_rows(k):
            def rows_at(at):
                total = k["residual"][at] + k["sum_one"][0][at] + k["vec"][4:5]
                k["layer_out"][at] = total.astype(BF)

            row_loop(R, rows_at)

        def out_weight(k):
            do = k["do"][0]

            def weight_o(b, _):
                do[b] = dot(k["lines"][0][:, cols(b, W)], the(k, "gbs")[...], ((0,), (0,))).astype(BF)
                return 0

            lax.fori_loop(0, G, weight_o, 0)
            load(k, 3).start()
            og = scatter_steps(
                zy, lambda o, i: do.at[o * zy.ni + i], k["o_acc"][0], *k["o_s"], inplace=True
            )
            step(og)
            return og

        def back_main(k):
            if merged:
                back_rest(k, *back_first(k))
                return
            back_first(k)

        def back_first(k):
            mats, wide = k["mats"][0], k["wide"][0]
            small, sum_one = the(k, "small"), k["sum_one"][0]
            gx = scatter_steps(zy, lambda o, i: k["gx"].at[o * zy.ni + i], sum_one, *k["gx_s"])
            y_scr = [k["y_s"][0], k["gx_s"][1], *k["y_s"][2:]]
            yy = scatter_steps(zy, lambda o, i: k["y"].at[o * zy.ni + i], sum_one, *y_scr)

            def sum_proj():
                acc = k["pj_acc"][0]
                yield from scatter_steps(
                    sq, lambda o, i: k["d_proj"].at[2 * o + i], acc, *k["pj_s"]
                )
                yield from gather_steps(
                    sq, acc, lambda o, i: k["d_proj_all"].at[2 * o + i], *k["pj_g"]
                )

            pj = sum_proj()
            step(gx)
            step(pj)
            small[...] = jnp.zeros(small.shape, F32)
            step(pj)
            step(gx)
            step(pj)
            step(gx)
            step(pj)
            step(gx)
            finish(gx)
            gain_mlp_row, g_res, gbs = k["vec"][5:6], the(k, "g_res"), the(k, "gbs")

            def norm_back_mlp(at):
                v = k["residual"][at]
                center = jnp.mean(v, axis=-1, keepdims=True)
                v = v - center
                scale = lax.rsqrt(jnp.mean(v * v, axis=-1, keepdims=True) + 1e-05)
                v = v * scale
                dn = sum_one[at]
                g = k["cot"][at].astype(F32)
                small[4:5] += jnp.sum(g, axis=0, keepdims=True)
                small[5:6] += jnp.sum(dn * v, axis=0, keepdims=True)
                small[6:7] += jnp.sum(dn, axis=0, keepdims=True)
                dn = dn * gain_mlp_row
                c1 = jnp.mean(dn, axis=-1, keepdims=True)
                c2 = jnp.mean(dn * v, axis=-1, keepdims=True)
                total = g + scale * (dn - c1 - v * c2)
                small[1:2] += jnp.sum(total, axis=0, keepdims=True)
                g_res[at] = total
                k["gb"][0][at] = total.astype(BF)

            row_loop(R, norm_back_mlp)
            gb = exchange_steps(
                sq,
                lambda o, i: k["gb"][0].at[:, cols(2 * o + i, QC)],
                lambda o, i: gbs.at[cols(2 * o + i, R)],
                *k["gb_x"],
            )
            step(gb)
            step(yy)
            step(pj)
            load(k, 0).wait()
            finish(gb)

            def back_cols(b, _):
                at = cols(b, QC)
                wide[:, at] = dot(gbs[...], mats[at, :QC], ((1,), (1,))).astype(BF)
                return 0

            lax.fori_loop(0, S, back_cols, 0)
            at_ = scatter_steps(
                sq,
                lambda o, i: wide.at[:, cols(2 * o + i, QC)],
                the(k, "g_att"),
                *k["ga_s"],
                inplace=True,
            )
            step(at_)
            if merged:
                load(k, 2).start()
                load(k, 1).wait()
            step(at_)
            og = out_weight(k) if merged else None
            finish(at_)
            finish(pj)
            if not merged:
                finish(yy)
                output_rows(k)
            return og, yy

        def back_rest(k, og, yy):
            mats, lines, wide = k["mats"][0], k["lines"][0], k["wide"][0]
            small, g_res = k["small"][0], the(k, "g_res")
            own, oth = k["dkv_own"][0], k["dkv_oth"][0]
            own[...] = jnp.zeros(own.shape, F32)
            oth[...] = jnp.zeros(oth.shape, F32)
            fcg = grad_fc(k)
            step(fcg)
            far_bias = (1 - lax.axis_index("ctx")).astype(F32) * -1e30

            def attend_back(n, _):
                h, first = n // (T // NQ), lax.rem(n, T // NQ) * NQ
                at = pl.ds(pl.multiple_of(first, NQ), NQ)
                hc = cols(h, HD)
                q, g = k["q"][at, hc], the(k, "g_att")[at, hc]
                kv0, kv1 = k["kv"], k["other"]
                s0 = dot(q, kv0[:, :HD], ((1,), (1,))) * score_scale
                s1 = dot(q, kv1[:, :HD], ((1,), (1,))) * score_scale + far_bias
                qpos = first + lax.broadcasted_iota(jnp.int32, s0.shape, 0)
                kpos = lax.broadcasted_iota(jnp.int32, s0.shape, 1)
                s0 = jnp.where(kpos <= qpos, s0, -1e30)
                top = jnp.maximum(
                    jnp.max(s0, axis=-1, keepdims=True), jnp.max(s1, axis=-1, keepdims=True)
                )
                p0, p1 = jnp.exp(s0 - top), jnp.exp(s1 - top)
                total = jnp.sum(p0, axis=-1, keepdims=True) + jnp.sum(p1, axis=-1, keepdims=True)
                inv = 1.0 / total
                p0, p1 = p0 * inv, p1 * inv
                own[:, HD:] += dot(p0.astype(BF), g, ((0,), (0,)))
                oth[:, HD:] += dot(p1.astype(BF), g, ((0,), (0,)))
                e0 = dot(g, kv0[:, HD:], ((1,), (1,)))
                e1 = dot(g, kv1[:, HD:], ((1,), (1,)))
                inner = jnp.sum(p0 * e0, axis=-1, keepdims=True) + jnp.sum(
                    p1 * e1, axis=-1, keepdims=True
                )
                d0 = (p0 * (e0 - inner) * score_scale).astype(BF)
                d1 = (p1 * (e1 - inner) * score_scale).astype(BF)
                own[:, :HD] += dot(d0, q, ((0,), (0,)))
                oth[:, :HD] += dot(d1, q, ((0,), (0,)))
                k["gq"][0][at, hc] = (dot(d0, kv0[:, :HD]) + dot(d1, kv1[:, :HD])).astype(BF)
                return 0

            def part_of(lo, hi):
                lax.fori_loop(NB * lo // 4, NB * hi // 4, attend_back, 0)

            part_of(0, 1)
            if merged:
                step(yy)
            step(fcg)
            part_of(1, 2)
            if merged:
                step(yy)
            step(fcg)
            part_of(2, 3)
            if merged:
                step(yy)
            step(og)
            step(fcg)
            part_of(3, 4)
            c = lax.axis_index("ctx")
            k["gkv_out"][0][...] = oth[...].astype(BF)
            swap = rcopy(
                k["gkv_out"][0],
                k["gkv_in"][0],
                k["swap"][0].at[0],
                k["swap"][1].at[0],
                {"ctx": 1 - c},
            )
            swap.start()
            gq, dq = k["gq"][0], k["dq"][0]
            step(og)
            load(k, 2).wait()
            load(k, 3).wait()

            def weight_q(b, _):
                dq[b] = dot(lines[:, cols(b, W)], gq[...], ((0,), (0,))).astype(BF)
                return 0

            lax.fori_loop(0, G, weight_q, 0)
            qg = scatter_steps(
                zy, lambda o, i: dq.at[o * zy.ni + i], k["q_acc"][0], *k["q_s"], inplace=True
            )
            step(og)
            step(qg)
            swap.wait()
            gkv = k["gkv"][0]
            gkv[...] = (own[...] + k["gkv_in"][0][...].astype(F32)).astype(BF)

            def back_in(b, _):
                at = cols(b, R)
                wide[at] = (
                    dot(gq[at], mats[:, :QC], ((1,), (1,)))
                    + dot(gkv[at], mats[:, QC:], ((1,), (1,)))
                ).astype(BF)
                return 0

            lax.fori_loop(0, S, back_in, 0)
            gng = scatter_steps(
                sq,
                lambda o, i: wide.at[cols(2 * o + i, R)],
                k["gn_sum"][0],
                *k["gn_s"],
                inplace=True,
            )
            step(gng)
            dkv = k["dkv"][0]

            def weight_kv(b, _):
                dkv[b] = dot(lines[:, cols(b, W)], gkv[...], ((0,), (0,))).astype(BF)
                return 0

            lax.fori_loop(0, G, weight_kv, 0)
            vg = scatter_steps(
                zy, lambda o, i: dkv.at[o * zy.ni + i], k["v_acc"][0], *k["v_s"], inplace=True
            )
            step(gng)
            step(vg)
            if merged:
                finish(yy)
                output_rows(k)
            finish(og)
            step(qg)
            step(fcg)
            finish(gng)
            gain_row = k["vec"][0:1]

            def norm_back_rows(at):
                v = k["rows"][at].astype(F32)
                center = jnp.mean(v, axis=-1, keepdims=True)
                v = v - center
                scale = lax.rsqrt(jnp.mean(v * v, axis=-1, keepdims=True) + 1e-05)
                v = v * scale
                dn = k["gn_sum"][0][at]
                small[2:3] += jnp.sum(dn * v, axis=0, keepdims=True)
                small[3:4] += jnp.sum(dn, axis=0, keepdims=True)
                dn = dn * gain_row
                c1 = jnp.mean(dn, axis=-1, keepdims=True)
                c2 = jnp.mean(dn * v, axis=-1, keepdims=True)
                k["input_grad"][at] = g_res[at] + scale * (dn - c1 - v * c2)

            row_loop(R, norm_back_rows)
            small[0:1, cols(lax.axis_index("seq"), QC)] = jnp.sum(
                gq[...].astype(F32), axis=0, keepdims=True
            )
            v_sum = jnp.sum(gkv[:, HD:].astype(F32), axis=0, keepdims=True)
            for b in range(G):
                small[7:8, b * W : b * W + HD] = v_sum

            def small_sums():
                got, line = k["s_got"][0], k["s_line"][0]
                yield from exchange_steps(
                    zy,
                    lambda o, i: small.at[:, cols(o * zy.ni + i, W)],
                    lambda o, i: got.at[o * zy.ni + i],
                    *k["s_x"],
                )
                line[:, :W] = sum([got[b] for b in range(1, G)], got[0])
                line[:, W:] = k["fc_terms"][...]
                yield
                yield from gather_steps(
                    sq, line, lambda o, i: k["s_all"][0].at[2 * o + i], *k["s_g"]
                )

            sg = small_sums()
            step(sg)
            step(qg)
            step(vg)
            step(fcg)
            step(sg)
            step(qg)
            step(vg)
            step(fcg)
            step(sg)
            finish(qg, vg)
            tails = [
                gather_steps(
                    sq, k["o_acc"][0], lambda o, i: k["o_all"].at[:, cols(2 * o + i, QC)], *k["o_g"]
                ),
                gather_steps(
                    sq, k["q_acc"][0], lambda o, i: k["q_all"].at[:, cols(2 * o + i, QC)], *k["q_g"]
                ),
                gather_steps(sq, k["v_acc"][0], lambda o, i: k["v_all"].at[2 * o + i], *k["v_g"]),
            ]
            finish(sg, *tails, fcg)
            tot = k["s_all"][0][0]
            for b in range(1, S):
                tot = tot + k["s_all"][0][b]
            k["s_sum"][...] = tot

        def grad_fc(k):
            acc, line = k["fc_acc"][0], k["fc_line"][0]
            yield from scatter_steps(sq, lambda o, i: k["d_fc"].at[:, 2 * o + i], acc, *k["fc_s"])
            yield from exchange_steps(
                zy,
                lambda o, i: acc.at[o * zy.ni + i],
                lambda o, i: line.at[:, cols(o * zy.ni + i, ffl)],
                *k["fc_x"],
            )
            yield from gather_steps(
                sq, line, lambda o, i: k["fc_all"].at[cols(2 * o + i, fc_rows)], *k["fc_g"]
            )

        fc_shape = (G, fc_rows, ffl)
        ins_one = dict(
            gx=(gx_part.reshape(G, R, D), ANY),
            y=(y_part.reshape(G, R, D), ANY),
            d_proj=(d_proj.reshape((S,) + far_out), ANY),
            cot=(g_out, VMEM),
            residual=(residual, VMEM),
            vec=(vec, VMEM),
            w_back=(w_back, ANY),
        )
        ins_two = dict(
            d_fc=(d_fc.reshape(G, S, fc_rows, ffl), ANY),
            rows=(rows_in, VMEM),
            att_rows=(att_rows, ANY),
            normed=(normed, ANY),
            w_in=(w_in, ANY),
            q=(queries, VMEM),
            kv=(keyval, VMEM),
            other=(other, VMEM),
            fc_terms=(grad_fc_bias.reshape(8, -1), VMEM),
        )
        outs_one = dict(
            layer_out=(rows_d, BF, VMEM),
            d_proj_all=((S,) + far_out, BF, ANY),
        )
        outs_two = dict(
            input_grad=((R, D), F32, VMEM),
            o_all=((W, D), BF, ANY),
            q_all=((W, D), BF, ANY),
            v_all=((S, W, 2 * HD), BF, ANY),
            fc_all=((W, G * ffl), BF, ANY),
            s_sum=((8, W + ffl // 8), F32, VMEM),
        )
        scr_one = dict(
            gx_s=scatter_scratch(zy, rows_d, BF),
            y_s=scatter_scratch(zy, rows_d, BF, mid=False),
            pj_acc=[VMEM(far_out, BF)],
            pj_s=scatter_scratch(sq, far_out, BF),
            pj_g=gather_sems(sq),
            gb=[VMEM(rows_d, BF)],
            gb_x=exchange_sems(sq),
            ga_s=scatter_scratch(sq, (T, QC), BF, mid=False),
            sum_one=[VMEM(rows_d, F32)],
        )
        scr_two = dict(
            lines=[VMEM((T, D), BF)],
            do=[VMEM((G, W, QC), BF)],
            dkv_own=[VMEM((T, 2 * HD), F32)],
            dkv_oth=[VMEM((T, 2 * HD), F32)],
            gkv_out=[VMEM((T, 2 * HD), BF)],
            gkv_in=[VMEM((T, 2 * HD), BF)],
            gkv=[VMEM((T, 2 * HD), BF)],
            swap=[DMA((1,)), DMA((1,))],
            gq=[VMEM((T, QC), BF)],
            dq=[VMEM((G, W, QC), BF)],
            dkv=[VMEM((G, W, 2 * HD), BF)],
            gn_sum=[VMEM((R, D), F32)],
            gn_s=scatter_scratch(sq, (R, D), BF, mid=False),
            o_acc=[VMEM((W, QC), BF)],
            q_acc=[VMEM((W, QC), BF)],
            v_acc=[VMEM((W, 2 * HD), BF)],
            o_s=scatter_scratch(zy, (W, QC), BF, mid=False),
            q_s=scatter_scratch(zy, (W, QC), BF, mid=False),
            v_s=scatter_scratch(zy, (W, 2 * HD), BF, mid=False),
            o_g=gather_sems(sq),
            q_g=gather_sems(sq),
            v_g=gather_sems(sq),
            fc_acc=[VMEM(fc_shape, BF)],
            fc_line=[VMEM((fc_rows, G * ffl), BF)],
            fc_s=scatter_scratch(sq, fc_shape, BF),
            fc_x=exchange_sems(zy),
            fc_g=gather_sems(sq),
            s_got=[VMEM((G, 8, W), F32)],
            s_line=[VMEM((8, W + ffl // 8), F32)],
            s_all=[VMEM((S, 8, W + ffl // 8), F32)],
            s_x=exchange_sems(zy),
            s_g=gather_sems(sq),
        )
        scr_both = dict(
            load=[DMA((4,))],
            mats=[VMEM((D, QC + 2 * HD), BF)],
            wide=[VMEM((T, D), BF)],
        )
        passed = dict(
            gbs=[VMEM((T, QC), BF)],
            g_res=[VMEM(rows_d, F32)],
            g_att=[VMEM((T, QC), BF)],
            small=[VMEM((8, D), F32)],
        )
        if merged:
            b2 = fused(
                "back",
                6,
                [zy, sq],
                {**ins_one, **ins_two},
                {**outs_one, **outs_two},
                {**scr_one, **scr_two, **scr_both, **passed},
                back_main,
                back_pre,
            )
        else:
            left = {n: (v[0].shape, v[0].dtype, VMEM) for n, v in passed.items()}
            b1 = fused(
                "back_one",
                6,
                [zy, sq],
                ins_one,
                {**outs_one, **left},
                {**scr_one, **scr_both},
                back_main,
                back_pre,
            )
            given = {n: (b1[n], VMEM) for n in passed if n != "small"}
            given["start"] = (b1["small"], VMEM)

            def rest_main(k):
                for n in (1, 2):
                    load(k, n).start()
                k["small"][0][...] = k["start"][...]
                load(k, 1).wait()
                back_rest(k, out_weight(k), None)

            b2 = fused(
                "back_two",
                7,
                [zy, sq],
                {**ins_two, **given, "vec": (vec, VMEM)},
                outs_two,
                {**scr_two, **scr_both, "small": passed["small"]},
                rest_main,
            )
            b2 = {**b1, **b2}
        d_proj_all = b2["d_proj_all"]
        sums = b2["s_sum"]
        grad_w_qkv = jnp.concatenate(
            [b2["q_all"].astype(F32), jnp.sum(b2["v_all"].astype(F32), axis=0)], axis=1
        )
        return (
            b2["layer_out"][None],
            b2["input_grad"][None],
            grad_w_qkv,
            sums[0, :W],
            lax.dynamic_slice_in_dim(sums[7, :HD], place_zy * vb, vb, 0),
            b2["o_all"].astype(F32),
            sums[1, :W],
            sums[2, :W],
            sums[3, :W],
            b2["fc_all"].astype(F32),
            sums[:, W:].reshape(-1),
            d_proj_all.reshape(-1, D).astype(F32),
            sums[4, :W],
            sums[5, :W],
            sums[6, :W],
        )

    return body


def solution(mesh):
    rows = P("batch", ("ctx", "seq"), None)
    mat = P(("batch", "ctx"), None)
    vec = P(("batch", "ctx"))
    in_specs = (rows, mat, vec, vec, mat, vec, vec, vec, mat, vec, mat, vec, vec, vec, rows)
    out_specs = (rows, rows, mat, vec, vec, mat, vec, vec, vec, mat, vec, mat, vec, vec, vec)
    return jax.shard_map(
        make_body(mesh), mesh=mesh, in_specs=in_specs, out_specs=out_specs, check_vma=False
    )
```

```python
import functools
import math
from types import SimpleNamespace

import jax
import jax.numpy as jnp
from jax import lax
from jax.experimental import pallas as pl
from jax.experimental.pallas import tpu as pltpu
from jax.sharding import PartitionSpec as P

D = 2048
HEADS = 16
HD = 128
MESH = pl.DeviceIdType.MESH
BF = jnp.bfloat16
F32 = jnp.float32
ANY = pl.ANY
VMEM = pltpu.VMEM
DMA = pltpu.SemaphoreType.DMA


class ZY:
    line = True

    def __init__(self, mesh):
        self.no, self.ni = mesh.shape["batch"], mesh.shape["ctx"]

    def me(self):
        return lax.axis_index("batch"), lax.axis_index("ctx")

    def dev(self, o, i):
        return {"batch": o, "ctx": i}


class SEQ:
    line = False

    def __init__(self, mesh):
        self.no, self.ni = mesh.shape["seq"] // 2, 2

    def me(self):
        s = lax.axis_index("seq")
        return s // 2, lax.rem(s, 2)

    def dev(self, o, i):
        return {"seq": 2 * o + i}


def rcopy(src, dst, ss, rs, dev):
    return pltpu.make_async_remote_copy(
        src_ref=src, dst_ref=dst, send_sem=ss, recv_sem=rs, device_id=dev, device_id_type=MESH
    )


def gather_steps(grp, src, view, ss, rs, ls, ready=None):
    if grp.line:
        return line_gather_steps(grp, src, view, ss, rs, ls, ready)
    return star_gather_steps(grp, src, view, ss, rs, ls)


def star_gather_steps(grp, src, view, ss, rs, ls):
    o, i = grp.me()
    no = grp.no
    mate = grp.dev(o, 1 - i)
    own = pltpu.make_async_copy(src, view(o, i), ls.at[0])
    own.start()
    sent = []
    for d in range(1, no):
        c = rcopy(src, view(o, i), ss.at[d], rs.at[d], grp.dev(lax.rem(o + d, no), i))
        c.start()
        sent.append(c)
    c = rcopy(src, view(o, i), ss.at[0], rs.at[0], mate)
    c.start()
    sent.append(c)
    yield
    for d in range(1, no):
        f = lax.rem(o - d + no, no)
        rcopy(view(f, i), view(f, i), ss.at[d], rs.at[d], mate).wait_recv()
        c = rcopy(view(f, i), view(f, i), ss.at[no + d - 1], rs.at[no + d - 1], mate)
        c.start()
        sent.append(c)
        yield
    rcopy(view(o, 1 - i), view(o, 1 - i), ss.at[0], rs.at[0], mate).wait_recv()
    for d in range(1, no):
        f = lax.rem(o - d + no, no)
        v = view(f, 1 - i)
        rcopy(v, v, ss.at[no + d - 1], rs.at[no + d - 1], mate).wait_recv()
    for c in sent:
        c.wait_send()
    own.wait()


def gather_sems(grp):
    if grp.line:
        return line_gather_sems(grp)
    n = 2 * grp.no - 1
    return [DMA((n,)), DMA((n,)), DMA((1,))]


def add_all(dst, refs, rows, step=16):
    if len(dst.shape) == 3:
        for b in range(dst.shape[0]):
            add_all(dst.at[b], [ref.at[b] for ref in refs], dst.shape[1], step)
        return

    def one(r, _):
        at = pl.ds(pl.multiple_of(r * step, step), step)
        total = refs[0][at].astype(F32)
        for ref in refs[1:]:
            total = total + ref[at].astype(F32)
        dst[at] = total.astype(dst.dtype)
        return 0

    lax.fori_loop(0, rows // step, one, 0)


def scatter_steps(grp, part, out, *scr, inplace=False):
    if grp.line:
        return line_scatter_steps(grp, part, out, *scr, inplace=inplace)
    return star_scatter_steps(grp, part, out, *scr, inplace=inplace)


def star_scatter_steps(grp, part, out, near, mid, far, ss, rs, ls, inplace):
    o, i = grp.me()
    no = grp.no
    mate = grp.dev(o, 1 - i)
    sent, own = [], []
    order = list(range(1, no)) + [0]
    rows = out.shape[0]
    for d in order:
        t = lax.rem(o + d, no)
        c = rcopy(part(t, 1 - i), near.at[d], ss.at[d], rs.at[d], mate)
        c.start()
        sent.append(c)
        if not inplace:
            c = pltpu.make_async_copy(part(t, i), mid.at[d], ls.at[d])
            c.start()
            own.append(c)
    yield
    for n, d in enumerate(order):
        t = lax.rem(o + d, no)
        held = part(t, i) if inplace else mid.at[d]
        if not inplace:
            own[n].wait()
        rcopy(near.at[d], near.at[d], ss.at[d], rs.at[d], mate).wait_recv()
        if d == 0:
            add_all(out, [held, near.at[d]], rows)
        else:
            add_all(held, [held, near.at[d]], rows)
            c = rcopy(
                held, far.at[d - 1], ss.at[no + d - 1], rs.at[no + d - 1], grp.dev(t, i)
            )
            c.start()
            sent.append(c)
            yield
    yield
    for d in range(1, no):
        v = far.at[d - 1]
        rcopy(v, v, ss.at[no + d - 1], rs.at[no + d - 1], mate).wait_recv()
        add_all(out, [out, v], rows)
    for c in sent:
        c.wait_send()


def scatter_scratch(grp, shape, dtype, mid=True):
    no = grp.no
    held = (no,) + shape if mid else (1, 8, 128)
    if grp.line:
        return [
            VMEM((no,) + shape, dtype),
            VMEM(held, dtype),
            VMEM((no + 1,) + shape, dtype),
            DMA((2 * no - 1,)),
            DMA((2 * no + 1,)),
            DMA((no,)),
        ]
    n = 2 * no - 1
    return [
        VMEM((no,) + shape, dtype),
        VMEM(held, dtype),
        VMEM((no - 1,) + shape, dtype),
        DMA((n,)),
        DMA((n,)),
        DMA((no,)),
    ]


def line_gather_steps(grp, src, view, ss, rs, ls, ready):
    o, i = grp.me()
    n = grp.no
    mate, right, left = grp.dev(o, 1 - i), grp.dev(o + 1, i), grp.dev(o - 1, i)
    own = pltpu.make_async_copy(src, view(o, i), ls.at[0])
    own.start()
    sent = []

    def send(pred, ref, dst, k, to):
        def copy():
            return rcopy(ref, dst, ss.at[k], rs.at[k], to)

        pl.when(pred)(lambda: copy().start())
        sent.append((pred, copy))

    def got(v, k):
        rcopy(v, v, ss.at[k], rs.at[k], mate).wait_recv()

    def mates(k):
        a, b = lax.max(o - k, 0), lax.min(o + k, n - 1)
        if k == 0:
            got(view(o, 1 - i), Y)
            own.wait()
            if ready is not None:
                ready(o)
            return
        pl.when(o >= k)(lambda: got(view(a, 1 - i), Y + k))
        pl.when(o + k <= n - 1)(lambda: got(view(b, 1 - i), Y + n - 1 + k))
        if ready is not None:

            def one(t, _):
                ready(jnp.where(t == 0, a, b))
                return 0

            first, last = jnp.where(o >= k, 0, 1), jnp.where(o + k <= n - 1, 2, 1)
            lax.fori_loop(first, last, one, 0)

    R, L, Y = -1, n - 2, 2 * n - 2
    send(o < n - 1, src, view(o, i), R + 1, right)
    send(o > 0, src, view(o, i), L + 1, left)
    c = rcopy(src, view(o, i), ss.at[Y], rs.at[Y], mate)
    c.start()
    yield
    for k in range(1, n):
        a, b = lax.max(o - k, 0), lax.min(o + k, n - 1)
        from_left, from_right = o >= k, o + k <= n - 1
        pl.when(from_left)(lambda: got(view(a, i), R + k))
        if k < n - 1:
            send(from_left & (o < n - 1), view(a, i), view(a, i), R + k + 1, right)
        send(from_left, view(a, i), view(a, i), Y + k, mate)
        pl.when(from_right)(lambda: got(view(b, i), L + k))
        if k < n - 1:
            send(from_right & (o > 0), view(b, i), view(b, i), L + k + 1, left)
        send(from_right, view(b, i), view(b, i), Y + n - 1 + k, mate)
        if ready is not None:
            mates(k - 1)
        yield
    for k in range(n) if ready is None else [n - 1]:
        mates(k)
    for pred, copy in sent:
        pl.when(pred)(lambda: copy().wait_send())
    c.wait_send()


def line_gather_sems(grp):
    n = 4 * grp.no - 3
    return [DMA((n,)), DMA((n,)), DMA((1,))]


def line_scatter_steps(grp, part, out, near, mid, far, ss, rs, ls, inplace):
    o, i = grp.me()
    n = grp.no
    mate = grp.dev(o, 1 - i)
    rows = out.shape[0]
    low = o < n // 2

    def target(j):
        if j == n - 1:
            return o
        down = jnp.where(n - 1 - j > o, n - 1 - j, n - 2 - j)
        up = jnp.where(j < o, j, j + 1)
        return jnp.where(low, down, up)

    sent, own = [], []
    for j in range(n):
        c = rcopy(part(target(j), 1 - i), near.at[j], ss.at[j], rs.at[j], mate)
        c.start()
        sent.append(c)
        if not inplace:
            c = pltpu.make_async_copy(part(target(j), i), mid.at[j], ls.at[j])
            c.start()
            own.append(c)
    yield
    moved = []
    for j in range(n - 1):
        t = target(j)
        held = part(t, i) if inplace else mid.at[j]
        if not inplace:
            own[j].wait()
        rcopy(near.at[j], near.at[j], ss.at[j], rs.at[j], mate).wait_recv()
        for right in (True, False):
            towards = (t > o) if right else (t < o)
            inner = (o > 0) if right else (o < n - 1)
            slot = t if right else jnp.where(t == o - 1, n, t)
            to = grp.dev(o + 1, i) if right else grp.dev(o - 1, i)

            def copy(j=j, slot=slot, to=to, held=held):
                return rcopy(held, far.at[slot], ss.at[n + j], rs.at[n + slot], to)

            @pl.when(towards & inner)
            def _():
                rcopy(far.at[t], far.at[t], ss.at[n + j], rs.at[n + t], mate).wait_recv()
                add_all(held, [held, near.at[j], far.at[t]], rows)

            @pl.when(towards & jnp.logical_not(inner))
            def _():
                add_all(held, [held, near.at[j]], rows)

            pl.when(towards)(lambda: copy().start())
            moved.append((towards, copy))
        yield
    j = n - 1
    held = part(o, i) if inplace else mid.at[j]
    if not inplace:
        own[j].wait()
    rcopy(near.at[j], near.at[j], ss.at[j], rs.at[j], mate).wait_recv()

    def arrived(k):
        rcopy(far.at[k], far.at[k], ss.at[j], rs.at[n + k], mate).wait_recv()

    pl.when(o > 0)(lambda: arrived(o))
    pl.when(o < n - 1)(lambda: arrived(n))
    mine = [held, near.at[j]]
    inside = (o > 0) & (o < n - 1)
    pl.when(inside)(lambda: add_all(out, mine + [far.at[o], far.at[n]], rows))
    pl.when(o == 0)(lambda: add_all(out, mine + [far.at[n]], rows))
    pl.when(o == n - 1)(lambda: add_all(out, mine + [far.at[o]], rows))
    for c in sent:
        c.wait_send()
    for pred, copy in moved:
        pl.when(pred)(lambda: copy().wait_send())


def exchange_steps(grp, src, dst, ss, rs, ls):
    o, i = grp.me()
    no, ni = grp.no, grp.ni
    sent = []
    own = pltpu.make_async_copy(src(o, i), dst(o, i), ls.at[0])
    own.start()
    for a in range(no):
        for b in range(ni):
            if a == 0 and b == 0:
                continue
            to, ti = lax.rem(o + a, no), lax.rem(i + b, ni)
            k = a * ni + b - 1
            c = rcopy(src(to, ti), dst(o, i), ss.at[k], rs.at[k], grp.dev(to, ti))
            c.start()
            sent.append(c)
    yield
    for a in range(no):
        for b in range(ni):
            if a == 0 and b == 0:
                continue
            fo, fi = lax.rem(o - a + no, no), lax.rem(i - b + ni, ni)
            k = a * ni + b - 1
            v = dst(fo, fi)
            rcopy(v, v, ss.at[k], rs.at[k], grp.dev(fo, fi)).wait_recv()
    for c in sent:
        c.wait_send()
    own.wait()


def exchange_sems(grp):
    n = grp.no * grp.ni - 1
    return [DMA((n,)), DMA((n,)), DMA((1,))]


def barrier(groups):
    sem = pltpu.get_barrier_semaphore()
    count = 0
    for grp in groups:
        o, i = grp.me()
        for a in range(grp.no):
            for b in range(grp.ni):
                if a == 0 and b == 0:
                    continue
                to, ti = lax.rem(o + a, grp.no), lax.rem(i + b, grp.ni)
                pl.semaphore_signal(sem, inc=1, device_id=grp.dev(to, ti), device_id_type=MESH)
                count += 1
    pl.semaphore_wait(sem, count)


def run_all(gens):
    live = list(gens)
    while live:
        left = []
        for g in live:
            try:
                next(g)
                left.append(g)
            except StopIteration:
                pass
        live = left


def fused(name, ident, groups, ins, outs, scratch, main, pre=None):
    keys = list(ins) + list(outs)
    in_specs = [pl.BlockSpec(memory_space=space) for _, space in ins.values()]
    out_specs = [pl.BlockSpec(memory_space=space) for _, _, space in outs.values()]
    out_shapes = [jax.ShapeDtypeStruct(shape, dtype) for shape, dtype, _ in outs.values()]
    flat = [x for group in scratch.values() for x in group]

    def kernel(*refs):
        named = dict(zip(keys, refs))
        at = len(keys)
        for key, group in scratch.items():
            named[key] = refs[at : at + len(group)]
            at += len(group)
        if pre is not None:
            pre(SimpleNamespace(**named))
        barrier(groups)
        main(SimpleNamespace(**named))

    got = pl.pallas_call(
        kernel,
        out_shape=out_shapes,
        in_specs=in_specs,
        out_specs=out_specs,
        scratch_shapes=flat,
        compiler_params=pltpu.CompilerParams(
            collective_id=ident, has_side_effects=True, vmem_limit_bytes=63 * 1024 * 1024
        ),
        name=name,
    )(*[a for a, _ in ins.values()])
    return SimpleNamespace(**dict(zip(outs, got)))


def step(gen):
    next(gen, None)


def finish(*gens):
    run_all(gens)


def row_loop(rows, fn, size=16):
    def one(r, _):
        fn(pl.ds(pl.multiple_of(r * size, size), size))
        return 0

    lax.fori_loop(0, rows // size, one, 0)


def cols(k, width):
    return pl.ds(pl.multiple_of(k * width, width), width)


def the(got):
    return got[0] if isinstance(got, tuple) else got


def gelu_tanh(values):
    return (
        0.5
        * values
        * (
            1.0
            + jnp.tanh(math.sqrt(2.0 / math.pi) * (values + 0.044715 * values * values * values))
        )
    )


def dot(a, b, dims=((1,), (0,))):
    return lax.dot_general(a, b, (dims, ((), ())), preferred_element_type=F32)


def make_body(mesh):
    zy, sq = ZY(mesh), SEQ(mesh)
    S = mesh.shape["seq"]
    G = mesh.shape["batch"] * mesh.shape["ctx"]
    W = D // G
    QC = (HEADS // S) * HD

    def gather_steps_inplace(grp, view, ss, rs):
        o, i = grp.me()
        no = grp.no
        mate = grp.dev(o, 1 - i)
        sent = []
        for d in list(range(1, no)) + [0]:
            to = grp.dev(lax.rem(o + d, no), i) if d else mate
            c = rcopy(view(o, i), view(o, i), ss.at[d], rs.at[d], to)
            c.start()
            sent.append(c)
        yield
        for d in range(1, no):
            v = view(lax.rem(o - d + no, no), i)
            rcopy(v, v, ss.at[d], rs.at[d], mate).wait_recv()
            c = rcopy(v, v, ss.at[no + d - 1], rs.at[no + d - 1], mate)
            c.start()
            sent.append(c)
        yield
        v = view(o, 1 - i)
        rcopy(v, v, ss.at[0], rs.at[0], mate).wait_recv()
        for d in range(1, no):
            v = view(lax.rem(o - d + no, no), 1 - i)
            rcopy(v, v, ss.at[no + d - 1], rs.at[no + d - 1], mate).wait_recv()
        for c in sent:
            c.wait_send()

    def body(
        inputs,
        w_qkv,
        q_bias,
        v_bias,
        w_out,
        out_bias,
        gain_attn,
        shift_attn,
        w_fc,
        fc_bias,
        w_proj,
        proj_bias,
        gain_mlp,
        shift_mlp,
        cotangent,
    ):
        rows_in = inputs[0]
        R = rows_in.shape[0]
        g_out = cotangent[0]
        vb = v_bias.shape[0]
        place_zy = lax.axis_index(("batch", "ctx"))
        lift = lambda v: v.astype(F32)
        line_of = lax.broadcasted_iota(jnp.int32, (8, W), 0)
        small = jnp.broadcast_to(
            lax.dynamic_update_slice_in_dim(jnp.zeros((W,), F32), lift(v_bias), place_zy * vb, 0), (8, W)
        )
        for n, v in enumerate(
            (gain_attn, shift_attn, q_bias, out_bias, proj_bias, gain_mlp, shift_mlp)
        ):
            small = jnp.where(line_of == n, lift(v), small)
        T = S * R
        NQ = min(256, T)
        HL = QC // HD
        NB = HL * (T // NQ)
        HALF = T // 2
        score_scale = 1.0 / math.sqrt(HD)
        ffl = w_fc.shape[1] // G
        fc_rows = W // S

        merged = T * D <= 1024 * 2048
        GR = G * R
        FC = min(256, ffl)
        upper = max(T, GR - T)
        mlp_ins, mlp_outs, mlp_scr = {}, {}, {}
        if merged:
            mlp_ins = dict(w_proj=(w_proj, ANY), fcb=(fc_bias.astype(F32)[None], VMEM))
            mlp_outs = dict(
                active=((GR, ffl), BF, ANY),
                grad_hidden=((GR, ffl), BF, ANY),
                y_part=((GR, D), BF, ANY),
                gx_part=((GR, D), BF, ANY),
                gsum=((1, ffl), F32, VMEM),
            )
            mlp_scr = dict(
                xv=[VMEM((G, R, D), BF)],
                gv=[VMEM((G, R, D), BF)],
                fcv=[VMEM((G, S, fc_rows, ffl), BF)],
                wpv=[VMEM((ffl, D), BF)],
                act=[VMEM((GR, ffl), BF)],
                back=[VMEM((GR, ffl), BF)],
                mlp_out=[DMA((5,))],
            )

        def front_main(k):
            c, sid = lax.axis_index("ctx"), lax.axis_index("seq")
            vec, span, normed = k.vec, k.first[0].at[:T], k.second[0].at[:T]
            w_in, w_back = k.w_in_s[0], k.w_back_s[0]
            row_of = lambda o, i: cols(o * zy.ni + i, W)
            sm = gather_steps(zy, k.small, lambda o, i: vec.at[:, row_of(o, i)], *k.sm_g)
            sp = gather_steps(sq, k.rows, lambda o, i: span.at[cols(2 * o + i, R)], *k.sp_g)
            wk = gather_steps(
                zy,
                k.w_qkv.at[:, D : D + 2 * HD],
                lambda o, i: w_in.at[row_of(o, i), QC : QC + 2 * HD],
                *k.wk_g,
            )
            wq = gather_steps(
                zy,
                k.w_qkv.at[:, cols(sid, QC)],
                lambda o, i: w_in.at[row_of(o, i), :QC],
                *k.wq_g,
            )
            wb = gather_steps(
                zy, k.w_out.at[:, cols(sid, QC)], lambda o, i: w_back.at[row_of(o, i)], *k.wb_g
            )
            g_to, fc_to = (k.gv[0], k.fcv[0]) if merged else (k.g_all, k.fc)
            gg = gather_steps(zy, k.cot, lambda o, i: g_to.at[o * zy.ni + i], *k.gg_g)
            if merged:
                w_load = pltpu.make_async_copy(k.w_proj, k.wpv[0], k.save[0].at[4])
                w_load.start()

            def spread_fc():
                yield from exchange_steps(
                    zy,
                    lambda o, i: k.w_fc.at[cols(sid, fc_rows), cols(o * zy.ni + i, ffl)],
                    lambda o, i: fc_to.at[o * zy.ni + i, sid],
                    *k.fc_x,
                )
                yield from gather_steps_inplace(sq, lambda o, i: fc_to.at[:, 2 * o + i], *k.fc_g)

            fc = spread_fc()
            step(sm)
            step(sp)
            step(wk)
            step(wq)
            for _ in range(zy.no - 1):
                step(sm)
                step(wk)
            finish(sm)
            step(wq)
            finish(sp)
            gain, shift = vec[0:1], vec[1:2]

            def norm_rows(at):
                v = span[at].astype(F32)
                v = v - jnp.mean(v, axis=-1, keepdims=True)
                v = v * lax.rsqrt(jnp.mean(v * v, axis=-1, keepdims=True) + 1e-05)
                normed[at] = (v * gain + shift).astype(BF)

            row_loop(T, norm_rows)
            step(wq)
            finish(wk)
            v_bias_row = sum([vec[7:8, b * W : b * W + HD] for b in range(1, G)], vec[7:8, :HD])

            def key_rows(b, _):
                at = cols(b, NQ)
                mixed = dot(normed[at], w_in[:, QC:])
                k.kv[at, :HD] = mixed[:, :HD].astype(BF)
                k.kv[at, HD:] = (mixed[:, HD:] + v_bias_row).astype(BF)
                return 0

            lax.fori_loop(0, T // NQ, key_rows, 0)
            swap = rcopy(
                k.kv, k.other, k.swap[0].at[0], k.swap[1].at[0], {"ctx": 1 - c}
            )
            swap.start()
            step(wq)
            saves = [
                pltpu.make_async_copy(normed, k.normed, k.save[0].at[0]),
                pltpu.make_async_copy(w_in, k.w_in, k.save[0].at[1]),
                pltpu.make_async_copy(w_back, k.w_back, k.save[0].at[2]),
                pltpu.make_async_copy(k.first[0].at[T : 2 * T], k.att_rows, k.save[0].at[3]),
            ]
            saves[0].start()
            step(fc)
            step(wb)
            finish(wq)
            saves[1].start()
            q_bias_row = vec[2:3, cols(sid, QC)]

            def query_rows(b, _):
                at = cols(b, NQ)
                k.q[at] = (dot(normed[at], w_in[:, :QC]) + q_bias_row).astype(BF)
                return 0

            lax.fori_loop(0, T // NQ, query_rows, 0)
            swap.wait()
            step(wb)
            step(gg)
            far_bias = (1 - c).astype(F32) * -1e30
            att = k.att[0]

            def attend(n, _):
                h, first = lax.rem(n, HL), (n // HL) * NQ
                at = pl.ds(pl.multiple_of(first, NQ), NQ)
                hc = cols(h, HD)
                q = k.q[at, hc]
                s0 = dot(q, k.kv[:, :HD], ((1,), (1,))) * score_scale
                s1 = dot(q, k.other[:, :HD], ((1,), (1,))) * score_scale + far_bias
                qpos = first + lax.broadcasted_iota(jnp.int32, s0.shape, 0)
                kpos = lax.broadcasted_iota(jnp.int32, s0.shape, 1)
                s0 = jnp.where(kpos <= qpos, s0, -1e30)
                top = jnp.maximum(
                    jnp.max(s0, axis=-1, keepdims=True), jnp.max(s1, axis=-1, keepdims=True)
                )
                p0, p1 = jnp.exp(s0 - top), jnp.exp(s1 - top)
                total = jnp.sum(p0, axis=-1, keepdims=True) + jnp.sum(p1, axis=-1, keepdims=True)
                inv = 1.0 / total
                att[at, hc] = (
                    dot((p0 * inv).astype(BF), k.kv[:, HD:])
                    + dot((p1 * inv).astype(BF), k.other[:, HD:])
                ).astype(BF)
                return 0

            att_s = k.first[0].at[T : 2 * T]
            ag = []
            for half in range(2):
                lax.fori_loop(half * NB // 2, (half + 1) * NB // 2, attend, 0)
                lines = pl.ds(half * HALF, HALF)
                g = gather_steps(
                    sq,
                    att.at[lines],
                    lambda o, i, lines=lines: att_s.at[lines, cols(2 * o + i, QC)],
                    *(k.at_g0, k.at_g1)[half],
                )
                step(g)
                ag.append(g)
                step(wb)
                step(fc)
            finish(wb)
            saves[2].start()
            br, brn = k.br[0], k.brn[0]
            for half in range(2):
                step(gg)
                finish(ag[half])

                def branch_rows(b, _):
                    at = cols(half * (S // 2) + b, R)
                    br[at] = dot(att_s[at], w_back[...]).astype(BF)
                    return 0

                lax.fori_loop(0, S // 2, branch_rows, 0)
            saves[3].start()
            bx = exchange_steps(
                sq,
                lambda o, i: br.at[cols(2 * o + i, R)],
                lambda o, i: brn.at[:, cols(2 * o + i, QC)],
                *k.br_x,
            )
            step(bx)
            step(fc)
            finish(bx)
            ob, gain2, shift2 = vec[3:4], vec[5:6], vec[6:7]
            nm = k.nm[0]

            def norm_rows_two(at):
                v = k.rows[at].astype(F32) + brn[at].astype(F32) + ob
                k.residual[at] = v
                v = v - jnp.mean(v, axis=-1, keepdims=True)
                v = v * lax.rsqrt(jnp.mean(v * v, axis=-1, keepdims=True) + 1e-05)
                nm[at] = (v * gain2 + shift2).astype(BF)

            row_loop(R, norm_rows_two)
            if not merged:
                xg = gather_steps(zy, nm, lambda o, i: k.x_all.at[o * zy.ni + i], *k.xg_g)
                step(xg)
                finish(gg, xg, fc)
                for c_ in saves:
                    c_.wait()
                return
            xv, gv, fcv, wpv = k.xv[0], k.gv[0], k.fcv[0], k.wpv[0]
            act, back, out_sems = k.act[0], k.back[0], k.mlp_out[0]
            RB = zy.ni * R
            gsum = k.gsum
            gsum[...] = jnp.zeros(gsum.shape, F32)
            slope = math.sqrt(2.0 / math.pi)

            def results(p):
                at = cols(p, RB)
                pair = pl.ds(p * zy.ni, zy.ni)
                return [
                    pltpu.make_async_copy(src, dst, out_sems.at[n])
                    for n, (src, dst) in enumerate(
                        [
                            (xv.at[pair], k.x_all.at[pair]),
                            (act.at[at], k.active.at[at]),
                            (back.at[at], k.grad_hidden.at[at]),
                            (k.first[0].at[at], k.y_part.at[at]),
                            (k.second[0].at[at], k.gx_part.at[at]),
                        ]
                    )
                ]

            def mlp_block(p):
                at = cols(p, RB)
                pair = pl.ds(p * zy.ni, zy.ni)

                def hidden_cols(n, _):
                    fa = cols(n, FC)
                    h = dot(xv[pair].reshape(RB, D), fcv[:, :, :, fa].reshape(D, FC)) + k.fcb[:, fa]
                    sq_h = h * h
                    th = jnp.tanh(slope * (h + 0.044715 * h * sq_h))
                    act[at, fa] = (0.5 * h * (1.0 + th)).astype(BF)
                    rise = 0.5 * (1.0 + th) + (0.5 * slope) * h * (1.0 - th * th) * (
                        1.0 + 3 * 0.044715 * sq_h
                    )
                    g = dot(gv[pair].reshape(RB, D), wpv[fa, :], ((1,), (1,)))
                    gh = (g * rise).astype(BF)
                    back[at, fa] = gh
                    gsum[:, fa] += jnp.sum(gh.astype(F32), axis=0, keepdims=True)
                    return 0

                lax.fori_loop(0, ffl // FC, hidden_cols, 0)

                def token_cols(n, _):
                    da = cols(n, W)
                    k.second[0][at, da] = dot(
                        back[at, :], fcv[n].reshape(W, ffl), ((1,), (1,))
                    ).astype(BF)
                    k.first[0][at, da] = dot(act[at, :], wpv[:, da]).astype(BF)
                    return 0

                lax.fori_loop(0, G, token_cols, 0)
                for c_ in results(p):
                    c_.start()

            saves[0].wait()
            saves[3].wait()
            xg = gather_steps(
                zy, nm, lambda o, i: xv.at[o * zy.ni + i], *k.xg_g, ready=mlp_block
            )
            step(xg)
            finish(gg, fc)
            w_load.wait()
            saves += [
                pltpu.make_async_copy(gv, k.g_all, k.save[0].at[5]),
                pltpu.make_async_copy(fcv, k.fc, k.save[0].at[6]),
            ]
            saves[4].start()
            saves[5].start()
            finish(xg)
            for c_ in saves[1:3] + saves[4:]:
                c_.wait()
            for p in range(zy.no):
                for c_ in results(p):
                    c_.wait()

        f = fused(
            "front",
            1,
            [zy, sq],
            dict(
                small=(small, VMEM),
                rows=(rows_in, VMEM),
                w_qkv=(w_qkv, VMEM),
                w_out=(w_out, VMEM),
                w_fc=(w_fc, ANY if merged else VMEM),
                cot=(g_out, VMEM),
                **mlp_ins,
            ),
            dict(
                vec=((8, D), F32, VMEM),
                normed=((T, D), BF, ANY),
                w_in=((D, QC + 2 * HD), BF, ANY),
                w_back=((D, QC), BF, ANY),
                q=((T, QC), BF, VMEM),
                kv=((T, 2 * HD), BF, VMEM),
                other=((T, 2 * HD), BF, VMEM),
                att_rows=((T, D), BF, ANY),
                residual=((R, D), F32, VMEM),
                fc=((G, S, fc_rows, ffl), BF, ANY),
                g_all=((G, R, D), BF, ANY),
                x_all=((G, R, D), BF, ANY),
                **mlp_outs,
            ),
            dict(
                first=[VMEM((T + upper, D), BF)],
                second=[VMEM((max(T, GR) if merged else T, D), BF)],
                w_in_s=[VMEM((D, QC + 2 * HD), BF)],
                w_back_s=[VMEM((D, QC), BF)],
                att=[VMEM((T, QC), BF)],
                br=[VMEM((T, QC), BF)],
                brn=[VMEM((R, D), BF)],
                nm=[VMEM((R, D), BF)],
                sm_g=gather_sems(zy),
                sp_g=gather_sems(sq),
                wk_g=gather_sems(zy),
                wq_g=gather_sems(zy),
                wb_g=gather_sems(zy),
                gg_g=gather_sems(zy),
                xg_g=gather_sems(zy),
                fc_x=exchange_sems(zy),
                fc_g=gather_sems(sq)[:2],
                at_g0=gather_sems(sq),
                at_g1=gather_sems(sq),
                br_x=exchange_sems(sq),
                swap=[DMA((1,)), DMA((1,))],
                save=[DMA((7,))],
                **mlp_scr,
            ),
            front_main,
        )
        vec = f.vec
        normed, w_in, w_back, att_rows = f.normed, f.w_in, f.w_back, f.att_rows
        queries, keyval, other, residual = f.q, f.kv, f.other, f.residual
        x_all, g_all, fc_cols = f.x_all, f.g_all, f.fc
        x_all = x_all.reshape(G * R, D)
        g_rows = g_all.reshape(G * R, D)
        fc = fc_cols.reshape(D, ffl)
        if merged:
            active_low, grad_hidden = f.active, f.grad_hidden
            y_part, gx_part = f.y_part, f.gx_part
            grad_fc_bias = f.gsum[0]
        else:
            hidden = dot(x_all, fc) + fc_bias.astype(F32)
            active, gelu_back = jax.vjp(gelu_tanh, hidden)
            active_low = active.astype(BF)
            y_part = dot(active_low, w_proj).astype(BF)
            grad_active = dot(g_rows, w_proj, ((1,), (1,)))
            grad_hidden = gelu_back(grad_active)[0].astype(BF)
            grad_fc_bias = jnp.sum(grad_hidden.astype(F32), axis=0)
            gx_part = dot(grad_hidden, fc, ((1,), (1,))).astype(BF)
        d_proj = dot(active_low, g_rows, ((0,), (0,))).astype(BF)
        d_fc = dot(x_all, grad_hidden, ((0,), (0,))).astype(BF)
        rows_d = (R, D)
        far_out = (ffl // S, D)

        def load(k, n):
            if n == 0:
                src, dst = k.w_back, k.mats[0].at[:, :QC]
            elif n == 2:
                src, dst = k.w_in, k.mats[0]
            else:
                src, dst = k.att_rows if n == 1 else k.normed, k.lines[0]
            return pltpu.make_async_copy(src, dst, k.load[0].at[n])

        def back_pre(k):
            load(k, 0).start()
            if merged:
                load(k, 1).start()

        def output_rows(k):
            def rows_at(at):
                total = k.residual[at] + k.sum_one[0][at] + k.vec[4:5]
                k.layer_out[at] = total.astype(BF)

            row_loop(R, rows_at)

        def out_weight(k):
            do = k.do[0]

            def weight_o(b, _):
                do[b] = dot(k.lines[0][:, cols(b, W)], the(k.gbs)[...], ((0,), (0,))).astype(BF)
                return 0

            lax.fori_loop(0, G, weight_o, 0)
            load(k, 3).start()
            og = scatter_steps(
                zy, lambda o, i: do.at[o * zy.ni + i], k.o_acc[0], *k.o_s, inplace=True
            )
            step(og)
            return og

        def back_main(k):
            if merged:
                back_rest(k, *back_first(k))
                return
            back_first(k)

        def back_first(k):
            mats, wide = k.mats[0], k.wide[0]
            small, sum_one = the(k.small), k.sum_one[0]
            gx = scatter_steps(zy, lambda o, i: k.gx.at[o * zy.ni + i], sum_one, *k.gx_s)
            y_scr = [k.y_s[0], k.gx_s[1], *k.y_s[2:]]
            yy = scatter_steps(zy, lambda o, i: k.y.at[o * zy.ni + i], sum_one, *y_scr)

            def sum_proj():
                acc = k.pj_acc[0]
                yield from scatter_steps(
                    sq, lambda o, i: k.d_proj.at[2 * o + i], acc, *k.pj_s
                )
                yield from gather_steps(
                    sq, acc, lambda o, i: k.d_proj_all.at[2 * o + i], *k.pj_g
                )

            pj = sum_proj()
            step(gx)
            step(pj)
            small[...] = jnp.zeros(small.shape, F32)
            step(pj)
            step(gx)
            step(pj)
            step(gx)
            step(pj)
            step(gx)
            finish(gx)
            gain_mlp_row, g_res, gbs = k.vec[5:6], the(k.g_res), the(k.gbs)

            def norm_back_mlp(at):
                v = k.residual[at]
                center = jnp.mean(v, axis=-1, keepdims=True)
                v = v - center
                scale = lax.rsqrt(jnp.mean(v * v, axis=-1, keepdims=True) + 1e-05)
                v = v * scale
                dn = sum_one[at]
                g = k.cot[at].astype(F32)
                small[4:5] += jnp.sum(g, axis=0, keepdims=True)
                small[5:6] += jnp.sum(dn * v, axis=0, keepdims=True)
                small[6:7] += jnp.sum(dn, axis=0, keepdims=True)
                dn = dn * gain_mlp_row
                c1 = jnp.mean(dn, axis=-1, keepdims=True)
                c2 = jnp.mean(dn * v, axis=-1, keepdims=True)
                total = g + scale * (dn - c1 - v * c2)
                small[1:2] += jnp.sum(total, axis=0, keepdims=True)
                g_res[at] = total
                k.gb[0][at] = total.astype(BF)

            row_loop(R, norm_back_mlp)
            gb = exchange_steps(
                sq,
                lambda o, i: k.gb[0].at[:, cols(2 * o + i, QC)],
                lambda o, i: gbs.at[cols(2 * o + i, R)],
                *k.gb_x,
            )
            step(gb)
            step(yy)
            step(pj)
            load(k, 0).wait()
            finish(gb)

            def back_cols(b, _):
                at = cols(b, QC)
                wide[:, at] = dot(gbs[...], mats[at, :QC], ((1,), (1,))).astype(BF)
                return 0

            lax.fori_loop(0, S, back_cols, 0)
            at_ = scatter_steps(
                sq,
                lambda o, i: wide.at[:, cols(2 * o + i, QC)],
                the(k.g_att),
                *k.ga_s,
                inplace=True,
            )
            step(at_)
            if merged:
                load(k, 2).start()
                load(k, 1).wait()
            step(at_)
            og = out_weight(k) if merged else None
            finish(at_)
            finish(pj)
            if not merged:
                finish(yy)
                output_rows(k)
            return og, yy

        def back_rest(k, og, yy):
            mats, lines, wide = k.mats[0], k.lines[0], k.wide[0]
            small, g_res = k.small[0], the(k.g_res)
            own, oth = k.dkv_own[0], k.dkv_oth[0]
            own[...] = jnp.zeros(own.shape, F32)
            oth[...] = jnp.zeros(oth.shape, F32)
            fcg = grad_fc(k)
            step(fcg)
            far_bias = (1 - lax.axis_index("ctx")).astype(F32) * -1e30

            def attend_back(n, _):
                h, first = n // (T // NQ), lax.rem(n, T // NQ) * NQ
                at = pl.ds(pl.multiple_of(first, NQ), NQ)
                hc = cols(h, HD)
                q, g = k.q[at, hc], the(k.g_att)[at, hc]
                kv0, kv1 = k.kv, k.other
                s0 = dot(q, kv0[:, :HD], ((1,), (1,))) * score_scale
                s1 = dot(q, kv1[:, :HD], ((1,), (1,))) * score_scale + far_bias
                qpos = first + lax.broadcasted_iota(jnp.int32, s0.shape, 0)
                kpos = lax.broadcasted_iota(jnp.int32, s0.shape, 1)
                s0 = jnp.where(kpos <= qpos, s0, -1e30)
                top = jnp.maximum(
                    jnp.max(s0, axis=-1, keepdims=True), jnp.max(s1, axis=-1, keepdims=True)
                )
                p0, p1 = jnp.exp(s0 - top), jnp.exp(s1 - top)
                total = jnp.sum(p0, axis=-1, keepdims=True) + jnp.sum(p1, axis=-1, keepdims=True)
                inv = 1.0 / total
                p0, p1 = p0 * inv, p1 * inv
                own[:, HD:] += dot(p0.astype(BF), g, ((0,), (0,)))
                oth[:, HD:] += dot(p1.astype(BF), g, ((0,), (0,)))
                e0 = dot(g, kv0[:, HD:], ((1,), (1,)))
                e1 = dot(g, kv1[:, HD:], ((1,), (1,)))
                inner = jnp.sum(p0 * e0, axis=-1, keepdims=True) + jnp.sum(
                    p1 * e1, axis=-1, keepdims=True
                )
                d0 = (p0 * (e0 - inner) * score_scale).astype(BF)
                d1 = (p1 * (e1 - inner) * score_scale).astype(BF)
                own[:, :HD] += dot(d0, q, ((0,), (0,)))
                oth[:, :HD] += dot(d1, q, ((0,), (0,)))
                k.gq[0][at, hc] = (dot(d0, kv0[:, :HD]) + dot(d1, kv1[:, :HD])).astype(BF)
                return 0

            def part_of(lo, hi):
                lax.fori_loop(NB * lo // 4, NB * hi // 4, attend_back, 0)

            part_of(0, 1)
            if merged:
                step(yy)
            step(fcg)
            part_of(1, 2)
            if merged:
                step(yy)
            step(fcg)
            part_of(2, 3)
            if merged:
                step(yy)
            step(og)
            step(fcg)
            part_of(3, 4)
            c = lax.axis_index("ctx")
            k.gkv_out[0][...] = oth[...].astype(BF)
            swap = rcopy(
                k.gkv_out[0],
                k.gkv_in[0],
                k.swap[0].at[0],
                k.swap[1].at[0],
                {"ctx": 1 - c},
            )
            swap.start()
            gq, dq = k.gq[0], k.dq[0]
            step(og)
            load(k, 2).wait()
            load(k, 3).wait()

            def weight_q(b, _):
                dq[b] = dot(lines[:, cols(b, W)], gq[...], ((0,), (0,))).astype(BF)
                return 0

            lax.fori_loop(0, G, weight_q, 0)
            qg = scatter_steps(
                zy, lambda o, i: dq.at[o * zy.ni + i], k.q_acc[0], *k.q_s, inplace=True
            )
            step(og)
            step(qg)
            swap.wait()
            gkv = k.gkv[0]
            gkv[...] = (own[...] + k.gkv_in[0][...].astype(F32)).astype(BF)

            def back_in(b, _):
                at = cols(b, R)
                wide[at] = (
                    dot(gq[at], mats[:, :QC], ((1,), (1,)))
                    + dot(gkv[at], mats[:, QC:], ((1,), (1,)))
                ).astype(BF)
                return 0

            lax.fori_loop(0, S, back_in, 0)
            gng = scatter_steps(
                sq,
                lambda o, i: wide.at[cols(2 * o + i, R)],
                k.gn_sum[0],
                *k.gn_s,
                inplace=True,
            )
            step(gng)
            dkv = k.dkv[0]

            def weight_kv(b, _):
                dkv[b] = dot(lines[:, cols(b, W)], gkv[...], ((0,), (0,))).astype(BF)
                return 0

            lax.fori_loop(0, G, weight_kv, 0)
            vg = scatter_steps(
                zy, lambda o, i: dkv.at[o * zy.ni + i], k.v_acc[0], *k.v_s, inplace=True
            )
            step(gng)
            step(vg)
            if merged:
                finish(yy)
                output_rows(k)
            finish(og)
            step(qg)
            step(fcg)
            finish(gng)
            gain_row = k.vec[0:1]

            def norm_back_rows(at):
                v = k.rows[at].astype(F32)
                center = jnp.mean(v, axis=-1, keepdims=True)
                v = v - center
                scale = lax.rsqrt(jnp.mean(v * v, axis=-1, keepdims=True) + 1e-05)
                v = v * scale
                dn = k.gn_sum[0][at]
                small[2:3] += jnp.sum(dn * v, axis=0, keepdims=True)
                small[3:4] += jnp.sum(dn, axis=0, keepdims=True)
                dn = dn * gain_row
                c1 = jnp.mean(dn, axis=-1, keepdims=True)
                c2 = jnp.mean(dn * v, axis=-1, keepdims=True)
                k.input_grad[at] = g_res[at] + scale * (dn - c1 - v * c2)

            row_loop(R, norm_back_rows)
            small[0:1, cols(lax.axis_index("seq"), QC)] = jnp.sum(
                gq[...].astype(F32), axis=0, keepdims=True
            )
            v_sum = jnp.sum(gkv[:, HD:].astype(F32), axis=0, keepdims=True)
            for b in range(G):
                small[7:8, b * W : b * W + HD] = v_sum

            def small_sums():
                got, line = k.s_got[0], k.s_line[0]
                yield from exchange_steps(
                    zy,
                    lambda o, i: small.at[:, cols(o * zy.ni + i, W)],
                    lambda o, i: got.at[o * zy.ni + i],
                    *k.s_x,
                )
                line[:, :W] = sum([got[b] for b in range(1, G)], got[0])
                line[:, W:] = k.fc_terms[...]
                yield
                yield from gather_steps(
                    sq, line, lambda o, i: k.s_all[0].at[2 * o + i], *k.s_g
                )

            sg = small_sums()
            step(sg)
            step(qg)
            step(vg)
            step(fcg)
            step(sg)
            step(qg)
            step(vg)
            step(fcg)
            step(sg)
            finish(qg, vg)
            tails = [
                gather_steps(
                    sq, k.o_acc[0], lambda o, i: k.o_all.at[:, cols(2 * o + i, QC)], *k.o_g
                ),
                gather_steps(
                    sq, k.q_acc[0], lambda o, i: k.q_all.at[:, cols(2 * o + i, QC)], *k.q_g
                ),
                gather_steps(sq, k.v_acc[0], lambda o, i: k.v_all.at[2 * o + i], *k.v_g),
            ]
            finish(sg, *tails, fcg)
            tot = k.s_all[0][0]
            for b in range(1, S):
                tot = tot + k.s_all[0][b]
            k.s_sum[...] = tot

        def grad_fc(k):
            acc, line = k.fc_acc[0], k.fc_line[0]
            yield from scatter_steps(sq, lambda o, i: k.d_fc.at[:, 2 * o + i], acc, *k.fc_s)
            yield from exchange_steps(
                zy,
                lambda o, i: acc.at[o * zy.ni + i],
                lambda o, i: line.at[:, cols(o * zy.ni + i, ffl)],
                *k.fc_x,
            )
            yield from gather_steps(
                sq, line, lambda o, i: k.fc_all.at[cols(2 * o + i, fc_rows)], *k.fc_g
            )

        fc_shape = (G, fc_rows, ffl)
        ins_one = dict(
            gx=(gx_part.reshape(G, R, D), ANY),
            y=(y_part.reshape(G, R, D), ANY),
            d_proj=(d_proj.reshape((S,) + far_out), ANY),
            cot=(g_out, VMEM),
            residual=(residual, VMEM),
            vec=(vec, VMEM),
            w_back=(w_back, ANY),
        )
        ins_two = dict(
            d_fc=(d_fc.reshape(G, S, fc_rows, ffl), ANY),
            rows=(rows_in, VMEM),
            att_rows=(att_rows, ANY),
            normed=(normed, ANY),
            w_in=(w_in, ANY),
            q=(queries, VMEM),
            kv=(keyval, VMEM),
            other=(other, VMEM),
            fc_terms=(grad_fc_bias.reshape(8, -1), VMEM),
        )
        outs_one = dict(
            layer_out=(rows_d, BF, VMEM),
            d_proj_all=((S,) + far_out, BF, ANY),
        )
        outs_two = dict(
            input_grad=((R, D), F32, VMEM),
            o_all=((W, D), BF, ANY),
            q_all=((W, D), BF, ANY),
            v_all=((S, W, 2 * HD), BF, ANY),
            fc_all=((W, G * ffl), BF, ANY),
            s_sum=((8, W + ffl // 8), F32, VMEM),
        )
        scr_one = dict(
            gx_s=scatter_scratch(zy, rows_d, BF),
            y_s=scatter_scratch(zy, rows_d, BF, mid=False),
            pj_acc=[VMEM(far_out, BF)],
            pj_s=scatter_scratch(sq, far_out, BF),
            pj_g=gather_sems(sq),
            gb=[VMEM(rows_d, BF)],
            gb_x=exchange_sems(sq),
            ga_s=scatter_scratch(sq, (T, QC), BF, mid=False),
            sum_one=[VMEM(rows_d, F32)],
        )
        scr_two = dict(
            lines=[VMEM((T, D), BF)],
            do=[VMEM((G, W, QC), BF)],
            dkv_own=[VMEM((T, 2 * HD), F32)],
            dkv_oth=[VMEM((T, 2 * HD), F32)],
            gkv_out=[VMEM((T, 2 * HD), BF)],
            gkv_in=[VMEM((T, 2 * HD), BF)],
            gkv=[VMEM((T, 2 * HD), BF)],
            swap=[DMA((1,)), DMA((1,))],
            gq=[VMEM((T, QC), BF)],
            dq=[VMEM((G, W, QC), BF)],
            dkv=[VMEM((G, W, 2 * HD), BF)],
            gn_sum=[VMEM((R, D), F32)],
            gn_s=scatter_scratch(sq, (R, D), BF, mid=False),
            o_acc=[VMEM((W, QC), BF)],
            q_acc=[VMEM((W, QC), BF)],
            v_acc=[VMEM((W, 2 * HD), BF)],
            o_s=scatter_scratch(zy, (W, QC), BF, mid=False),
            q_s=scatter_scratch(zy, (W, QC), BF, mid=False),
            v_s=scatter_scratch(zy, (W, 2 * HD), BF, mid=False),
            o_g=gather_sems(sq),
            q_g=gather_sems(sq),
            v_g=gather_sems(sq),
            fc_acc=[VMEM(fc_shape, BF)],
            fc_line=[VMEM((fc_rows, G * ffl), BF)],
            fc_s=scatter_scratch(sq, fc_shape, BF),
            fc_x=exchange_sems(zy),
            fc_g=gather_sems(sq),
            s_got=[VMEM((G, 8, W), F32)],
            s_line=[VMEM((8, W + ffl // 8), F32)],
            s_all=[VMEM((S, 8, W + ffl // 8), F32)],
            s_x=exchange_sems(zy),
            s_g=gather_sems(sq),
        )
        scr_both = dict(
            load=[DMA((4,))],
            mats=[VMEM((D, QC + 2 * HD), BF)],
            wide=[VMEM((T, D), BF)],
        )
        passed = dict(
            gbs=[VMEM((T, QC), BF)],
            g_res=[VMEM(rows_d, F32)],
            g_att=[VMEM((T, QC), BF)],
            small=[VMEM((8, D), F32)],
        )
        if merged:
            b2 = fused(
                "back",
                6,
                [zy, sq],
                {**ins_one, **ins_two},
                {**outs_one, **outs_two},
                {**scr_one, **scr_two, **scr_both, **passed},
                back_main,
                back_pre,
            )
        else:
            left = {n: (v[0].shape, v[0].dtype, VMEM) for n, v in passed.items()}
            b1 = fused(
                "back_one",
                6,
                [zy, sq],
                ins_one,
                {**outs_one, **left},
                {**scr_one, **scr_both},
                back_main,
                back_pre,
            )
            given = {n: (getattr(b1, n), VMEM) for n in passed if n != "small"}
            given.update(start=(b1.small, VMEM))

            def rest_main(k):
                for n in (1, 2):
                    load(k, n).start()
                k.small[0][...] = k.start[...]
                load(k, 1).wait()
                back_rest(k, out_weight(k), None)

            b2 = fused(
                "back_two",
                7,
                [zy, sq],
                {**ins_two, **given, "vec": (vec, VMEM)},
                outs_two,
                {**scr_two, **scr_both, "small": passed["small"]},
                rest_main,
            )
            b2 = SimpleNamespace(**{**vars(b1), **vars(b2)})
        d_proj_all = b2.d_proj_all
        sums = b2.s_sum
        grad_w_qkv = jnp.concatenate(
            [b2.q_all.astype(F32), jnp.sum(b2.v_all.astype(F32), axis=0)], axis=1
        )
        return (
            b2.layer_out[None],
            b2.input_grad[None],
            grad_w_qkv,
            sums[0, :W],
            lax.dynamic_slice_in_dim(sums[7, :HD], place_zy * vb, vb, 0),
            b2.o_all.astype(F32),
            sums[1, :W],
            sums[2, :W],
            sums[3, :W],
            b2.fc_all.astype(F32),
            sums[:, W:].reshape(-1),
            d_proj_all.reshape(-1, D).astype(F32),
            sums[4, :W],
            sums[5, :W],
            sums[6, :W],
        )

    return body


def solution(mesh):
    rows = P("batch", ("ctx", "seq"), None)
    mat = P(("batch", "ctx"), None)
    vec = P(("batch", "ctx"))
    in_specs = (rows, mat, vec, vec, mat, vec, vec, vec, mat, vec, mat, vec, vec, vec, rows)
    out_specs = (rows, rows, mat, vec, vec, mat, vec, vec, vec, mat, vec, mat, vec, vec, vec)
    return jax.shard_map(
        make_body(mesh), mesh=mesh, in_specs=in_specs, out_specs=out_specs, check_vma=False
    )
```

```python
import functools
import math
from types import SimpleNamespace

import jax
import jax.numpy as jnp
from jax import lax
from jax.experimental import pallas as pl
from jax.experimental.pallas import tpu as pltpu
from jax.sharding import PartitionSpec as P

D = 2048
HEADS = 16
HD = 128
MESH = pl.DeviceIdType.MESH
BF = jnp.bfloat16
F32 = jnp.float32
ANY = pl.ANY
VMEM = pltpu.VMEM
DMA = pltpu.SemaphoreType.DMA


class ZY:
    line = True

    def __init__(self, mesh):
        self.no, self.ni = mesh.shape["batch"], mesh.shape["ctx"]

    def me(self):
        return lax.axis_index("batch"), lax.axis_index("ctx")

    def dev(self, o, i):
        return {"batch": o, "ctx": i}


class SEQ:
    line = False

    def __init__(self, mesh):
        self.no, self.ni = mesh.shape["seq"] // 2, 2

    def me(self):
        s = lax.axis_index("seq")
        return s // 2, lax.rem(s, 2)

    def dev(self, o, i):
        return {"seq": 2 * o + i}


def rcopy(src, dst, ss, rs, dev):
    return pltpu.make_async_remote_copy(
        src_ref=src, dst_ref=dst, send_sem=ss, recv_sem=rs, device_id=dev, device_id_type=MESH
    )


def gather_steps(grp, src, view, ss, rs, ls, ready=None):
    if grp.line:
        return line_gather_steps(grp, src, view, ss, rs, ls, ready)
    return star_gather_steps(grp, src, view, ss, rs, ls)


def star_gather_steps(grp, src, view, ss, rs, ls):
    o, i = grp.me()
    no = grp.no
    mate = grp.dev(o, 1 - i)
    own = pltpu.make_async_copy(src, view(o, i), ls.at[0])
    own.start()
    sent = []
    for d in range(1, no):
        c = rcopy(src, view(o, i), ss.at[d], rs.at[d], grp.dev(lax.rem(o + d, no), i))
        c.start()
        sent.append(c)
    c = rcopy(src, view(o, i), ss.at[0], rs.at[0], mate)
    c.start()
    sent.append(c)
    yield
    for d in range(1, no):
        f = lax.rem(o - d + no, no)
        rcopy(view(f, i), view(f, i), ss.at[d], rs.at[d], mate).wait_recv()
        c = rcopy(view(f, i), view(f, i), ss.at[no + d - 1], rs.at[no + d - 1], mate)
        c.start()
        sent.append(c)
        yield
    rcopy(view(o, 1 - i), view(o, 1 - i), ss.at[0], rs.at[0], mate).wait_recv()
    for d in range(1, no):
        f = lax.rem(o - d + no, no)
        v = view(f, 1 - i)
        rcopy(v, v, ss.at[no + d - 1], rs.at[no + d - 1], mate).wait_recv()
    for c in sent:
        c.wait_send()
    own.wait()


def gather_sems(grp):
    if grp.line:
        return line_gather_sems(grp)
    n = 2 * grp.no - 1
    return [DMA((n,)), DMA((n,)), DMA((1,))]


def add_all(dst, refs, rows, step=16):
    if len(dst.shape) == 3:
        for b in range(dst.shape[0]):
            add_all(dst.at[b], [ref.at[b] for ref in refs], dst.shape[1], step)
        return

    def one(r, _):
        at = pl.ds(pl.multiple_of(r * step, step), step)
        total = refs[0][at].astype(F32)
        for ref in refs[1:]:
            total = total + ref[at].astype(F32)
        dst[at] = total.astype(dst.dtype)
        return 0

    lax.fori_loop(0, rows // step, one, 0)


def scatter_steps(grp, part, out, *scr, inplace=False):
    if grp.line:
        return line_scatter_steps(grp, part, out, *scr, inplace=inplace)
    return star_scatter_steps(grp, part, out, *scr, inplace=inplace)


def star_scatter_steps(grp, part, out, near, mid, far, ss, rs, ls, inplace):
    o, i = grp.me()
    no = grp.no
    mate = grp.dev(o, 1 - i)
    sent, own = [], []
    order = list(range(1, no)) + [0]
    rows = out.shape[0]
    for d in order:
        t = lax.rem(o + d, no)
        c = rcopy(part(t, 1 - i), near.at[d], ss.at[d], rs.at[d], mate)
        c.start()
        sent.append(c)
        if not inplace:
            c = pltpu.make_async_copy(part(t, i), mid.at[d], ls.at[d])
            c.start()
            own.append(c)
    yield
    for n, d in enumerate(order):
        t = lax.rem(o + d, no)
        held = part(t, i) if inplace else mid.at[d]
        if not inplace:
            own[n].wait()
        rcopy(near.at[d], near.at[d], ss.at[d], rs.at[d], mate).wait_recv()
        if d == 0:
            add_all(out, [held, near.at[d]], rows)
        else:
            add_all(held, [held, near.at[d]], rows)
            c = rcopy(
                held, far.at[d - 1], ss.at[no + d - 1], rs.at[no + d - 1], grp.dev(t, i)
            )
            c.start()
            sent.append(c)
            yield
    yield
    for d in range(1, no):
        v = far.at[d - 1]
        rcopy(v, v, ss.at[no + d - 1], rs.at[no + d - 1], mate).wait_recv()
        add_all(out, [out, v], rows)
    for c in sent:
        c.wait_send()


def scatter_scratch(grp, shape, dtype, mid=True):
    no = grp.no
    held = (no,) + shape if mid else (1, 8, 128)
    if grp.line:
        return [
            VMEM((no,) + shape, dtype),
            VMEM(held, dtype),
            VMEM((no + 1,) + shape, dtype),
            DMA((2 * no - 1,)),
            DMA((2 * no + 1,)),
            DMA((no,)),
        ]
    n = 2 * no - 1
    return [
        VMEM((no,) + shape, dtype),
        VMEM(held, dtype),
        VMEM((no - 1,) + shape, dtype),
        DMA((n,)),
        DMA((n,)),
        DMA((no,)),
    ]


def line_gather_steps(grp, src, view, ss, rs, ls, ready):
    o, i = grp.me()
    n = grp.no
    mate, right, left = grp.dev(o, 1 - i), grp.dev(o + 1, i), grp.dev(o - 1, i)
    own = pltpu.make_async_copy(src, view(o, i), ls.at[0])
    own.start()
    sent = []

    def send(pred, ref, dst, k, to):
        def copy():
            return rcopy(ref, dst, ss.at[k], rs.at[k], to)

        pl.when(pred)(lambda: copy().start())
        sent.append((pred, copy))

    def got(v, k):
        rcopy(v, v, ss.at[k], rs.at[k], mate).wait_recv()

    def mates(k):
        a, b = lax.max(o - k, 0), lax.min(o + k, n - 1)
        if k == 0:
            got(view(o, 1 - i), Y)
            own.wait()
            if ready is not None:
                ready(o)
            return
        pl.when(o >= k)(lambda: got(view(a, 1 - i), Y + k))
        pl.when(o + k <= n - 1)(lambda: got(view(b, 1 - i), Y + n - 1 + k))
        if ready is not None:

            def one(t, _):
                ready(jnp.where(t == 0, a, b))
                return 0

            first, last = jnp.where(o >= k, 0, 1), jnp.where(o + k <= n - 1, 2, 1)
            lax.fori_loop(first, last, one, 0)

    R, L, Y = -1, n - 2, 2 * n - 2
    send(o < n - 1, src, view(o, i), R + 1, right)
    send(o > 0, src, view(o, i), L + 1, left)
    c = rcopy(src, view(o, i), ss.at[Y], rs.at[Y], mate)
    c.start()
    yield
    for k in range(1, n):
        a, b = lax.max(o - k, 0), lax.min(o + k, n - 1)
        from_left, from_right = o >= k, o + k <= n - 1
        pl.when(from_left)(lambda: got(view(a, i), R + k))
        if k < n - 1:
            send(from_left & (o < n - 1), view(a, i), view(a, i), R + k + 1, right)
        send(from_left, view(a, i), view(a, i), Y + k, mate)
        pl.when(from_right)(lambda: got(view(b, i), L + k))
        if k < n - 1:
            send(from_right & (o > 0), view(b, i), view(b, i), L + k + 1, left)
        send(from_right, view(b, i), view(b, i), Y + n - 1 + k, mate)
        if ready is not None:
            mates(k - 1)
        yield
    for k in range(n) if ready is None else [n - 1]:
        mates(k)
    for pred, copy in sent:
        pl.when(pred)(lambda: copy().wait_send())
    c.wait_send()


def line_gather_sems(grp):
    n = 4 * grp.no - 3
    return [DMA((n,)), DMA((n,)), DMA((1,))]


def line_scatter_steps(grp, part, out, near, mid, far, ss, rs, ls, inplace):
    o, i = grp.me()
    n = grp.no
    mate = grp.dev(o, 1 - i)
    rows = out.shape[0]
    low = o < n // 2

    def target(j):
        if j == n - 1:
            return o
        down = jnp.where(n - 1 - j > o, n - 1 - j, n - 2 - j)
        up = jnp.where(j < o, j, j + 1)
        return jnp.where(low, down, up)

    sent, own = [], []
    for j in range(n):
        c = rcopy(part(target(j), 1 - i), near.at[j], ss.at[j], rs.at[j], mate)
        c.start()
        sent.append(c)
        if not inplace:
            c = pltpu.make_async_copy(part(target(j), i), mid.at[j], ls.at[j])
            c.start()
            own.append(c)
    yield
    moved = []
    for j in range(n - 1):
        t = target(j)
        held = part(t, i) if inplace else mid.at[j]
        if not inplace:
            own[j].wait()
        rcopy(near.at[j], near.at[j], ss.at[j], rs.at[j], mate).wait_recv()
        for right in (True, False):
            towards = (t > o) if right else (t < o)
            inner = (o > 0) if right else (o < n - 1)
            slot = t if right else jnp.where(t == o - 1, n, t)
            to = grp.dev(o + 1, i) if right else grp.dev(o - 1, i)

            def copy(j=j, slot=slot, to=to, held=held):
                return rcopy(held, far.at[slot], ss.at[n + j], rs.at[n + slot], to)

            @pl.when(towards & inner)
            def _():
                rcopy(far.at[t], far.at[t], ss.at[n + j], rs.at[n + t], mate).wait_recv()
                add_all(held, [held, near.at[j], far.at[t]], rows)

            @pl.when(towards & jnp.logical_not(inner))
            def _():
                add_all(held, [held, near.at[j]], rows)

            pl.when(towards)(lambda: copy().start())
            moved.append((towards, copy))
        yield
    j = n - 1
    held = part(o, i) if inplace else mid.at[j]
    if not inplace:
        own[j].wait()
    rcopy(near.at[j], near.at[j], ss.at[j], rs.at[j], mate).wait_recv()

    def arrived(k):
        rcopy(far.at[k], far.at[k], ss.at[j], rs.at[n + k], mate).wait_recv()

    pl.when(o > 0)(lambda: arrived(o))
    pl.when(o < n - 1)(lambda: arrived(n))
    mine = [held, near.at[j]]
    inside = (o > 0) & (o < n - 1)
    pl.when(inside)(lambda: add_all(out, mine + [far.at[o], far.at[n]], rows))
    pl.when(o == 0)(lambda: add_all(out, mine + [far.at[n]], rows))
    pl.when(o == n - 1)(lambda: add_all(out, mine + [far.at[o]], rows))
    for c in sent:
        c.wait_send()
    for pred, copy in moved:
        pl.when(pred)(lambda: copy().wait_send())


def exchange_steps(grp, src, dst, ss, rs, ls):
    o, i = grp.me()
    no, ni = grp.no, grp.ni
    sent = []
    own = pltpu.make_async_copy(src(o, i), dst(o, i), ls.at[0])
    own.start()
    for a in range(no):
        for b in range(ni):
            if a == 0 and b == 0:
                continue
            to, ti = lax.rem(o + a, no), lax.rem(i + b, ni)
            k = a * ni + b - 1
            c = rcopy(src(to, ti), dst(o, i), ss.at[k], rs.at[k], grp.dev(to, ti))
            c.start()
            sent.append(c)
    yield
    for a in range(no):
        for b in range(ni):
            if a == 0 and b == 0:
                continue
            fo, fi = lax.rem(o - a + no, no), lax.rem(i - b + ni, ni)
            k = a * ni + b - 1
            v = dst(fo, fi)
            rcopy(v, v, ss.at[k], rs.at[k], grp.dev(fo, fi)).wait_recv()
    for c in sent:
        c.wait_send()
    own.wait()


def exchange_sems(grp):
    n = grp.no * grp.ni - 1
    return [DMA((n,)), DMA((n,)), DMA((1,))]


def barrier(groups):
    sem = pltpu.get_barrier_semaphore()
    count = 0
    for grp in groups:
        o, i = grp.me()
        for a in range(grp.no):
            for b in range(grp.ni):
                if a == 0 and b == 0:
                    continue
                to, ti = lax.rem(o + a, grp.no), lax.rem(i + b, grp.ni)
                pl.semaphore_signal(sem, inc=1, device_id=grp.dev(to, ti), device_id_type=MESH)
                count += 1
    pl.semaphore_wait(sem, count)


def run_all(gens):
    live = list(gens)
    while live:
        left = []
        for g in live:
            try:
                next(g)
                left.append(g)
            except StopIteration:
                pass
        live = left


def fused(name, ident, groups, ins, outs, scratch, main, pre=None):
    keys = list(ins) + list(outs)
    in_specs = [pl.BlockSpec(memory_space=space) for _, space in ins.values()]
    out_specs = [pl.BlockSpec(memory_space=space) for _, _, space in outs.values()]
    out_shapes = [jax.ShapeDtypeStruct(shape, dtype) for shape, dtype, _ in outs.values()]
    flat = [x for group in scratch.values() for x in group]

    def kernel(*refs):
        named = dict(zip(keys, refs))
        at = len(keys)
        for key, group in scratch.items():
            named[key] = refs[at : at + len(group)]
            at += len(group)
        if pre is not None:
            pre(SimpleNamespace(**named))
        barrier(groups)
        main(SimpleNamespace(**named))

    got = pl.pallas_call(
        kernel,
        out_shape=out_shapes,
        in_specs=in_specs,
        out_specs=out_specs,
        scratch_shapes=flat,
        compiler_params=pltpu.CompilerParams(
            collective_id=ident, has_side_effects=True, vmem_limit_bytes=63 * 1024 * 1024
        ),
        name=name,
    )(*[a for a, _ in ins.values()])
    return SimpleNamespace(**dict(zip(outs, got)))


def step(gen):
    next(gen, None)


def finish(*gens):
    run_all(gens)


def row_loop(rows, fn, size=16):
    def one(r, _):
        fn(pl.ds(pl.multiple_of(r * size, size), size))
        return 0

    lax.fori_loop(0, rows // size, one, 0)


def cols(k, width):
    return pl.ds(pl.multiple_of(k * width, width), width)


def the(got):
    return got[0] if isinstance(got, tuple) else got


def gelu_tanh(values):
    return (
        0.5
        * values
        * (
            1.0
            + jnp.tanh(math.sqrt(2.0 / math.pi) * (values + 0.044715 * values * values * values))
        )
    )


def dot(a, b, dims=((1,), (0,))):
    return lax.dot_general(a, b, (dims, ((), ())), preferred_element_type=F32)


def make_body(mesh):
    zy, sq = ZY(mesh), SEQ(mesh)
    S = mesh.shape["seq"]
    G = mesh.shape["batch"] * mesh.shape["ctx"]
    W = D // G
    QC = (HEADS // S) * HD

    def gather_steps_inplace(grp, view, ss, rs):
        o, i = grp.me()
        no = grp.no
        mate = grp.dev(o, 1 - i)
        sent = []
        for d in list(range(1, no)) + [0]:
            to = grp.dev(lax.rem(o + d, no), i) if d else mate
            c = rcopy(view(o, i), view(o, i), ss.at[d], rs.at[d], to)
            c.start()
            sent.append(c)
        yield
        for d in range(1, no):
            v = view(lax.rem(o - d + no, no), i)
            rcopy(v, v, ss.at[d], rs.at[d], mate).wait_recv()
            c = rcopy(v, v, ss.at[no + d - 1], rs.at[no + d - 1], mate)
            c.start()
            sent.append(c)
        yield
        v = view(o, 1 - i)
        rcopy(v, v, ss.at[0], rs.at[0], mate).wait_recv()
        for d in range(1, no):
            v = view(lax.rem(o - d + no, no), 1 - i)
            rcopy(v, v, ss.at[no + d - 1], rs.at[no + d - 1], mate).wait_recv()
        for c in sent:
            c.wait_send()

    def body(
        inputs,
        w_qkv,
        q_bias,
        v_bias,
        w_out,
        out_bias,
        gain_attn,
        shift_attn,
        w_fc,
        fc_bias,
        w_proj,
        proj_bias,
        gain_mlp,
        shift_mlp,
        cotangent,
    ):
        rows_in = inputs[0]
        R = rows_in.shape[0]
        g_out = cotangent[0]
        vb = v_bias.shape[0]
        place_zy = lax.axis_index(("batch", "ctx"))
        lift = lambda v: v.astype(F32)
        line_of = lax.broadcasted_iota(jnp.int32, (8, W), 0)
        small = jnp.broadcast_to(
            lax.dynamic_update_slice_in_dim(jnp.zeros((W,), F32), lift(v_bias), place_zy * vb, 0), (8, W)
        )
        for n, v in enumerate(
            (gain_attn, shift_attn, q_bias, out_bias, proj_bias, gain_mlp, shift_mlp)
        ):
            small = jnp.where(line_of == n, lift(v), small)
        T = S * R
        NQ = min(256, T)
        HL = QC // HD
        NB = HL * (T // NQ)
        HALF = T // 2
        score_scale = 1.0 / math.sqrt(HD)
        ffl = w_fc.shape[1] // G
        fc_rows = W // S

        merged = T * D <= 1024 * 2048
        GR = G * R
        FC = min(256, ffl)
        upper = max(T, GR - T)
        mlp_ins, mlp_outs, mlp_scr = {}, {}, {}
        if merged:
            mlp_ins = dict(w_proj=(w_proj, ANY), fcb=(fc_bias.astype(F32)[None], VMEM))
            mlp_outs = dict(
                active=((GR, ffl), BF, ANY),
                grad_hidden=((GR, ffl), BF, ANY),
                y_part=((GR, D), BF, ANY),
                gx_part=((GR, D), BF, ANY),
                gsum=((1, ffl), F32, VMEM),
            )
            mlp_scr = dict(
                xv=[VMEM((G, R, D), BF)],
                gv=[VMEM((G, R, D), BF)],
                fcv=[VMEM((G, S, fc_rows, ffl), BF)],
                wpv=[VMEM((ffl, D), BF)],
                act=[VMEM((GR, ffl), BF)],
                back=[VMEM((GR, ffl), BF)],
                mlp_out=[DMA((5,))],
            )

        def front_main(k):
            c, sid = lax.axis_index("ctx"), lax.axis_index("seq")
            vec, span, normed = k.vec, k.first[0].at[:T], k.second[0].at[:T]
            w_in, w_back = k.w_in_s[0], k.w_back_s[0]
            row_of = lambda o, i: cols(o * zy.ni + i, W)
            sm = gather_steps(zy, k.small, lambda o, i: vec.at[:, row_of(o, i)], *k.sm_g)
            sp = gather_steps(sq, k.rows, lambda o, i: span.at[cols(2 * o + i, R)], *k.sp_g)
            wk = gather_steps(
                zy,
                k.w_qkv.at[:, D : D + 2 * HD],
                lambda o, i: w_in.at[row_of(o, i), QC : QC + 2 * HD],
                *k.wk_g,
            )
            wq = gather_steps(
                zy,
                k.w_qkv.at[:, cols(sid, QC)],
                lambda o, i: w_in.at[row_of(o, i), :QC],
                *k.wq_g,
            )
            wb = gather_steps(
                zy, k.w_out.at[:, cols(sid, QC)], lambda o, i: w_back.at[row_of(o, i)], *k.wb_g
            )
            g_to, fc_to = (k.gv[0], k.fcv[0]) if merged else (k.g_all, k.fc)
            gg = gather_steps(zy, k.cot, lambda o, i: g_to.at[o * zy.ni + i], *k.gg_g)
            if merged:
                w_load = pltpu.make_async_copy(k.w_proj, k.wpv[0], k.save[0].at[4])
                w_load.start()

            def spread_fc():
                yield from exchange_steps(
                    zy,
                    lambda o, i: k.w_fc.at[cols(sid, fc_rows), cols(o * zy.ni + i, ffl)],
                    lambda o, i: fc_to.at[o * zy.ni + i, sid],
                    *k.fc_x,
                )
                yield from gather_steps_inplace(sq, lambda o, i: fc_to.at[:, 2 * o + i], *k.fc_g)

            fc = spread_fc()
            step(sm)
            step(sp)
            step(wk)
            step(wq)
            for _ in range(zy.no - 1):
                step(sm)
                step(wk)
            finish(sm)
            step(wq)
            finish(sp)
            gain, shift = vec[0:1], vec[1:2]

            def norm_rows(at):
                v = span[at].astype(F32)
                v = v - jnp.mean(v, axis=-1, keepdims=True)
                v = v * lax.rsqrt(jnp.mean(v * v, axis=-1, keepdims=True) + 1e-05)
                normed[at] = (v * gain + shift).astype(BF)

            row_loop(T, norm_rows)
            step(wq)
            finish(wk)
            v_bias_row = sum([vec[7:8, b * W : b * W + HD] for b in range(1, G)], vec[7:8, :HD])

            def key_rows(b, _):
                at = cols(b, NQ)
                mixed = dot(normed[at], w_in[:, QC:])
                k.kv[at, :HD] = mixed[:, :HD].astype(BF)
                k.kv[at, HD:] = (mixed[:, HD:] + v_bias_row).astype(BF)
                return 0

            lax.fori_loop(0, T // NQ, key_rows, 0)
            swap = rcopy(
                k.kv, k.other, k.swap[0].at[0], k.swap[1].at[0], {"ctx": 1 - c}
            )
            swap.start()
            step(wq)
            saves = [
                pltpu.make_async_copy(normed, k.normed, k.save[0].at[0]),
                pltpu.make_async_copy(w_in, k.w_in, k.save[0].at[1]),
                pltpu.make_async_copy(w_back, k.w_back, k.save[0].at[2]),
                pltpu.make_async_copy(k.first[0].at[T : 2 * T], k.att_rows, k.save[0].at[3]),
            ]
            saves[0].start()
            step(fc)
            step(wb)
            finish(wq)
            saves[1].start()
            q_bias_row = vec[2:3, cols(sid, QC)]

            def query_rows(b, _):
                at = cols(b, NQ)
                k.q[at] = (dot(normed[at], w_in[:, :QC]) + q_bias_row).astype(BF)
                return 0

            lax.fori_loop(0, T // NQ, query_rows, 0)
            swap.wait()
            step(wb)
            step(gg)
            far_bias = (1 - c).astype(F32) * -1e30
            att = k.att[0]

            def attend(n, _):
                h, first = lax.rem(n, HL), (n // HL) * NQ
                at = pl.ds(pl.multiple_of(first, NQ), NQ)
                hc = cols(h, HD)
                q = k.q[at, hc]
                s0 = dot(q, k.kv[:, :HD], ((1,), (1,))) * score_scale
                s1 = dot(q, k.other[:, :HD], ((1,), (1,))) * score_scale + far_bias
                qpos = first + lax.broadcasted_iota(jnp.int32, s0.shape, 0)
                kpos = lax.broadcasted_iota(jnp.int32, s0.shape, 1)
                s0 = jnp.where(kpos <= qpos, s0, -1e30)
                top = jnp.maximum(
                    jnp.max(s0, axis=-1, keepdims=True), jnp.max(s1, axis=-1, keepdims=True)
                )
                p0, p1 = jnp.exp(s0 - top), jnp.exp(s1 - top)
                total = jnp.sum(p0, axis=-1, keepdims=True) + jnp.sum(p1, axis=-1, keepdims=True)
                inv = 1.0 / total
                att[at, hc] = (
                    dot((p0 * inv).astype(BF), k.kv[:, HD:])
                    + dot((p1 * inv).astype(BF), k.other[:, HD:])
                ).astype(BF)
                return 0

            att_s = k.first[0].at[T : 2 * T]
            ag = []
            for half in range(2):
                lax.fori_loop(half * NB // 2, (half + 1) * NB // 2, attend, 0)
                lines = pl.ds(half * HALF, HALF)
                g = gather_steps(
                    sq,
                    att.at[lines],
                    lambda o, i, lines=lines: att_s.at[lines, cols(2 * o + i, QC)],
                    *(k.at_g0, k.at_g1)[half],
                )
                step(g)
                ag.append(g)
                step(wb)
                step(fc)
            finish(wb)
            saves[2].start()
            br, brn = k.br[0], k.brn[0]
            for half in range(2):
                step(gg)
                finish(ag[half])

                def branch_rows(b, _):
                    at = cols(half * (S // 2) + b, R)
                    br[at] = dot(att_s[at], w_back[...]).astype(BF)
                    return 0

                lax.fori_loop(0, S // 2, branch_rows, 0)
            saves[3].start()
            bx = exchange_steps(
                sq,
                lambda o, i: br.at[cols(2 * o + i, R)],
                lambda o, i: brn.at[:, cols(2 * o + i, QC)],
                *k.br_x,
            )
            step(bx)
            step(fc)
            finish(bx)
            ob, gain2, shift2 = vec[3:4], vec[5:6], vec[6:7]
            nm = k.nm[0]

            def norm_rows_two(at):
                v = k.rows[at].astype(F32) + brn[at].astype(F32) + ob
                k.residual[at] = v
                v = v - jnp.mean(v, axis=-1, keepdims=True)
                v = v * lax.rsqrt(jnp.mean(v * v, axis=-1, keepdims=True) + 1e-05)
                nm[at] = (v * gain2 + shift2).astype(BF)

            row_loop(R, norm_rows_two)
            if not merged:
                xg = gather_steps(zy, nm, lambda o, i: k.x_all.at[o * zy.ni + i], *k.xg_g)
                step(xg)
                finish(gg, xg, fc)
                for c_ in saves:
                    c_.wait()
                return
            xv, gv, fcv, wpv = k.xv[0], k.gv[0], k.fcv[0], k.wpv[0]
            act, back, out_sems = k.act[0], k.back[0], k.mlp_out[0]
            RB = zy.ni * R
            gsum = k.gsum
            gsum[...] = jnp.zeros(gsum.shape, F32)
            slope = math.sqrt(2.0 / math.pi)

            def results(p):
                at = cols(p, RB)
                pair = pl.ds(p * zy.ni, zy.ni)
                return [
                    pltpu.make_async_copy(src, dst, out_sems.at[n])
                    for n, (src, dst) in enumerate(
                        [
                            (xv.at[pair], k.x_all.at[pair]),
                            (act.at[at], k.active.at[at]),
                            (back.at[at], k.grad_hidden.at[at]),
                            (k.first[0].at[at], k.y_part.at[at]),
                            (k.second[0].at[at], k.gx_part.at[at]),
                        ]
                    )
                ]

            def mlp_block(p):
                at = cols(p, RB)
                pair = pl.ds(p * zy.ni, zy.ni)

                def hidden_cols(n, _):
                    fa = cols(n, FC)
                    h = dot(xv[pair].reshape(RB, D), fcv[:, :, :, fa].reshape(D, FC)) + k.fcb[:, fa]
                    sq_h = h * h
                    th = jnp.tanh(slope * (h + 0.044715 * h * sq_h))
                    act[at, fa] = (0.5 * h * (1.0 + th)).astype(BF)
                    rise = 0.5 * (1.0 + th) + (0.5 * slope) * h * (1.0 - th * th) * (
                        1.0 + 3 * 0.044715 * sq_h
                    )
                    g = dot(gv[pair].reshape(RB, D), wpv[fa, :], ((1,), (1,)))
                    gh = (g * rise).astype(BF)
                    back[at, fa] = gh
                    gsum[:, fa] += jnp.sum(gh.astype(F32), axis=0, keepdims=True)
                    return 0

                lax.fori_loop(0, ffl // FC, hidden_cols, 0)

                def token_cols(n, _):
                    da = cols(n, W)
                    k.second[0][at, da] = dot(
                        back[at, :], fcv[n].reshape(W, ffl), ((1,), (1,))
                    ).astype(BF)
                    k.first[0][at, da] = dot(act[at, :], wpv[:, da]).astype(BF)
                    return 0

                lax.fori_loop(0, G, token_cols, 0)
                for c_ in results(p):
                    c_.start()

            saves[0].wait()
            saves[3].wait()
            xg = gather_steps(
                zy, nm, lambda o, i: xv.at[o * zy.ni + i], *k.xg_g, ready=mlp_block
            )
            step(xg)
            finish(gg, fc)
            w_load.wait()
            saves += [
                pltpu.make_async_copy(gv, k.g_all, k.save[0].at[5]),
                pltpu.make_async_copy(fcv, k.fc, k.save[0].at[6]),
            ]
            saves[4].start()
            saves[5].start()
            finish(xg)
            for c_ in saves[1:3] + saves[4:]:
                c_.wait()
            for p in range(zy.no):
                for c_ in results(p):
                    c_.wait()

        f = fused(
            "front",
            1,
            [zy, sq],
            dict(
                small=(small, VMEM),
                rows=(rows_in, VMEM),
                w_qkv=(w_qkv, VMEM),
                w_out=(w_out, VMEM),
                w_fc=(w_fc, ANY if merged else VMEM),
                cot=(g_out, VMEM),
                **mlp_ins,
            ),
            dict(
                vec=((8, D), F32, VMEM),
                normed=((T, D), BF, ANY),
                w_in=((D, QC + 2 * HD), BF, ANY),
                w_back=((D, QC), BF, ANY),
                q=((T, QC), BF, VMEM),
                kv=((T, 2 * HD), BF, VMEM),
                other=((T, 2 * HD), BF, VMEM),
                att_rows=((T, D), BF, ANY),
                residual=((R, D), F32, VMEM),
                fc=((G, S, fc_rows, ffl), BF, ANY),
                g_all=((G, R, D), BF, ANY),
                x_all=((G, R, D), BF, ANY),
                **mlp_outs,
            ),
            dict(
                first=[VMEM((T + upper, D), BF)],
                second=[VMEM((max(T, GR) if merged else T, D), BF)],
                w_in_s=[VMEM((D, QC + 2 * HD), BF)],
                w_back_s=[VMEM((D, QC), BF)],
                att=[VMEM((T, QC), BF)],
                br=[VMEM((T, QC), BF)],
                brn=[VMEM((R, D), BF)],
                nm=[VMEM((R, D), BF)],
                sm_g=gather_sems(zy),
                sp_g=gather_sems(sq),
                wk_g=gather_sems(zy),
                wq_g=gather_sems(zy),
                wb_g=gather_sems(zy),
                gg_g=gather_sems(zy),
                xg_g=gather_sems(zy),
                fc_x=exchange_sems(zy),
                fc_g=gather_sems(sq)[:2],
                at_g0=gather_sems(sq),
                at_g1=gather_sems(sq),
                br_x=exchange_sems(sq),
                swap=[DMA((1,)), DMA((1,))],
                save=[DMA((7,))],
                **mlp_scr,
            ),
            front_main,
        )
        vec = f.vec
        normed, w_in, w_back, att_rows = f.normed, f.w_in, f.w_back, f.att_rows
        queries, keyval, other, residual = f.q, f.kv, f.other, f.residual
        x_all, g_all, fc_cols = f.x_all, f.g_all, f.fc
        x_all = x_all.reshape(G * R, D)
        g_rows = g_all.reshape(G * R, D)
        fc = fc_cols.reshape(D, ffl)
        if merged:
            active_low, grad_hidden = f.active, f.grad_hidden
            y_part, gx_part = f.y_part, f.gx_part
            grad_fc_bias = f.gsum[0]
        else:
            hidden = dot(x_all, fc) + fc_bias.astype(F32)
            active, gelu_back = jax.vjp(gelu_tanh, hidden)
            active_low = active.astype(BF)
            y_part = dot(active_low, w_proj).astype(BF)
            grad_active = dot(g_rows, w_proj, ((1,), (1,)))
            grad_hidden = gelu_back(grad_active)[0].astype(BF)
            grad_fc_bias = jnp.sum(grad_hidden.astype(F32), axis=0)
            gx_part = dot(grad_hidden, fc, ((1,), (1,))).astype(BF)
        d_proj = dot(active_low, g_rows, ((0,), (0,))).astype(BF)
        d_fc = dot(x_all, grad_hidden, ((0,), (0,))).astype(BF)
        rows_d = (R, D)
        far_out = (ffl // S, D)

        def load(k, n):
            if n == 0:
                src, dst = k.w_back, k.mats[0].at[:, :QC]
            elif n == 2:
                src, dst = k.w_in, k.mats[0]
            else:
                src, dst = k.att_rows if n == 1 else k.normed, k.lines[0]
            return pltpu.make_async_copy(src, dst, k.load[0].at[n])

        def back_pre(k):
            load(k, 0).start()
            if merged:
                load(k, 1).start()

        def output_rows(k):
            def rows_at(at):
                total = k.residual[at] + k.sum_one[0][at] + k.vec[4:5]
                k.layer_out[at] = total.astype(BF)

            row_loop(R, rows_at)

        def out_weight(k):
            do = k.do[0]

            def weight_o(b, _):
                do[b] = dot(k.lines[0][:, cols(b, W)], the(k.gbs)[...], ((0,), (0,))).astype(BF)
                return 0

            lax.fori_loop(0, G, weight_o, 0)
            load(k, 3).start()
            og = scatter_steps(
                zy, lambda o, i: do.at[o * zy.ni + i], k.o_acc[0], *k.o_s, inplace=True
            )
            step(og)
            return og

        def back_main(k):
            if merged:
                back_rest(k, *back_first(k))
                return
            back_first(k)

        def back_first(k):
            mats, wide = k.mats[0], k.wide[0]
            small, sum_one = the(k.small), k.sum_one[0]
            gx = scatter_steps(zy, lambda o, i: k.gx.at[o * zy.ni + i], sum_one, *k.gx_s)
            y_scr = [k.y_s[0], k.gx_s[1], *k.y_s[2:]]
            yy = scatter_steps(zy, lambda o, i: k.y.at[o * zy.ni + i], sum_one, *y_scr)

            def sum_proj():
                acc = k.pj_acc[0]
                yield from scatter_steps(
                    sq, lambda o, i: k.d_proj.at[2 * o + i], acc, *k.pj_s
                )
                yield from gather_steps(
                    sq, acc, lambda o, i: k.d_proj_all.at[2 * o + i], *k.pj_g
                )

            pj = sum_proj()
            step(gx)
            step(pj)
            small[...] = jnp.zeros(small.shape, F32)
            step(pj)
            step(gx)
            step(pj)
            step(gx)
            step(pj)
            step(gx)
            finish(gx)
            gain_mlp_row, g_res, gbs = k.vec[5:6], the(k.g_res), the(k.gbs)

            def norm_back_mlp(at):
                v = k.residual[at]
                center = jnp.mean(v, axis=-1, keepdims=True)
                v = v - center
                scale = lax.rsqrt(jnp.mean(v * v, axis=-1, keepdims=True) + 1e-05)
                v = v * scale
                dn = sum_one[at]
                g = k.cot[at].astype(F32)
                small[4:5] += jnp.sum(g, axis=0, keepdims=True)
                small[5:6] += jnp.sum(dn * v, axis=0, keepdims=True)
                small[6:7] += jnp.sum(dn, axis=0, keepdims=True)
                dn = dn * gain_mlp_row
                c1 = jnp.mean(dn, axis=-1, keepdims=True)
                c2 = jnp.mean(dn * v, axis=-1, keepdims=True)
                total = g + scale * (dn - c1 - v * c2)
                small[1:2] += jnp.sum(total, axis=0, keepdims=True)
                g_res[at] = total
                k.gb[0][at] = total.astype(BF)

            row_loop(R, norm_back_mlp)
            gb = exchange_steps(
                sq,
                lambda o, i: k.gb[0].at[:, cols(2 * o + i, QC)],
                lambda o, i: gbs.at[cols(2 * o + i, R)],
                *k.gb_x,
            )
            step(gb)
            step(yy)
            if not merged:
                step(pj)
            load(k, 0).wait()
            finish(gb)

            def back_cols(b, _):
                at = cols(b, QC)
                wide[:, at] = dot(gbs[...], mats[at, :QC], ((1,), (1,))).astype(BF)
                return 0

            lax.fori_loop(0, S, back_cols, 0)
            at_ = scatter_steps(
                sq,
                lambda o, i: wide.at[:, cols(2 * o + i, QC)],
                the(k.g_att),
                *k.ga_s,
                inplace=True,
            )
            step(at_)
            if merged:
                load(k, 2).start()
                load(k, 1).wait()
            step(at_)
            og = out_weight(k) if merged else None
            finish(at_)
            if not merged:
                finish(pj)
                finish(yy)
                output_rows(k)
            return og, yy, pj

        def back_rest(k, og, yy, pj):
            mats, lines, wide = k.mats[0], k.lines[0], k.wide[0]
            small, g_res = k.small[0], the(k.g_res)
            own, oth = k.dkv_own[0], k.dkv_oth[0]
            own[...] = jnp.zeros(own.shape, F32)
            oth[...] = jnp.zeros(oth.shape, F32)
            fcg = grad_fc(k)
            if merged:
                step(pj)
            step(fcg)
            far_bias = (1 - lax.axis_index("ctx")).astype(F32) * -1e30

            def attend_back(n, _):
                h, first = n // (T // NQ), lax.rem(n, T // NQ) * NQ
                at = pl.ds(pl.multiple_of(first, NQ), NQ)
                hc = cols(h, HD)
                q, g = k.q[at, hc], the(k.g_att)[at, hc]
                kv0, kv1 = k.kv, k.other
                s0 = dot(q, kv0[:, :HD], ((1,), (1,))) * score_scale
                s1 = dot(q, kv1[:, :HD], ((1,), (1,))) * score_scale + far_bias
                qpos = first + lax.broadcasted_iota(jnp.int32, s0.shape, 0)
                kpos = lax.broadcasted_iota(jnp.int32, s0.shape, 1)
                s0 = jnp.where(kpos <= qpos, s0, -1e30)
                top = jnp.maximum(
                    jnp.max(s0, axis=-1, keepdims=True), jnp.max(s1, axis=-1, keepdims=True)
                )
                p0, p1 = jnp.exp(s0 - top), jnp.exp(s1 - top)
                total = jnp.sum(p0, axis=-1, keepdims=True) + jnp.sum(p1, axis=-1, keepdims=True)
                inv = 1.0 / total
                p0, p1 = p0 * inv, p1 * inv
                own[:, HD:] += dot(p0.astype(BF), g, ((0,), (0,)))
                oth[:, HD:] += dot(p1.astype(BF), g, ((0,), (0,)))
                e0 = dot(g, kv0[:, HD:], ((1,), (1,)))
                e1 = dot(g, kv1[:, HD:], ((1,), (1,)))
                inner = jnp.sum(p0 * e0, axis=-1, keepdims=True) + jnp.sum(
                    p1 * e1, axis=-1, keepdims=True
                )
                d0 = (p0 * (e0 - inner) * score_scale).astype(BF)
                d1 = (p1 * (e1 - inner) * score_scale).astype(BF)
                own[:, :HD] += dot(d0, q, ((0,), (0,)))
                oth[:, :HD] += dot(d1, q, ((0,), (0,)))
                k.gq[0][at, hc] = (dot(d0, kv0[:, :HD]) + dot(d1, kv1[:, :HD])).astype(BF)
                return 0

            def part_of(lo, hi):
                lax.fori_loop(NB * lo // 4, NB * hi // 4, attend_back, 0)

            part_of(0, 1)
            if merged:
                step(yy)
            step(fcg)
            part_of(1, 2)
            if merged:
                step(pj)
                step(yy)
            step(fcg)
            part_of(2, 3)
            if merged:
                step(yy)
            step(og)
            step(fcg)
            part_of(3, 4)
            c = lax.axis_index("ctx")
            k.gkv_out[0][...] = oth[...].astype(BF)
            swap = rcopy(
                k.gkv_out[0],
                k.gkv_in[0],
                k.swap[0].at[0],
                k.swap[1].at[0],
                {"ctx": 1 - c},
            )
            swap.start()
            gq, dq = k.gq[0], k.dq[0]
            step(og)
            load(k, 2).wait()
            load(k, 3).wait()

            def weight_q(b, _):
                dq[b] = dot(lines[:, cols(b, W)], gq[...], ((0,), (0,))).astype(BF)
                return 0

            lax.fori_loop(0, G, weight_q, 0)
            qg = scatter_steps(
                zy, lambda o, i: dq.at[o * zy.ni + i], k.q_acc[0], *k.q_s, inplace=True
            )
            step(og)
            step(qg)
            swap.wait()
            gkv = k.gkv[0]
            gkv[...] = (own[...] + k.gkv_in[0][...].astype(F32)).astype(BF)

            def back_in(b, _):
                at = cols(b, R)
                wide[at] = (
                    dot(gq[at], mats[:, :QC], ((1,), (1,)))
                    + dot(gkv[at], mats[:, QC:], ((1,), (1,)))
                ).astype(BF)
                return 0

            lax.fori_loop(0, S, back_in, 0)
            gng = scatter_steps(
                sq,
                lambda o, i: wide.at[cols(2 * o + i, R)],
                k.gn_sum[0],
                *k.gn_s,
                inplace=True,
            )
            step(gng)
            dkv = k.dkv[0]

            def weight_kv(b, _):
                dkv[b] = dot(lines[:, cols(b, W)], gkv[...], ((0,), (0,))).astype(BF)
                return 0

            lax.fori_loop(0, G, weight_kv, 0)
            vg = scatter_steps(
                zy, lambda o, i: dkv.at[o * zy.ni + i], k.v_acc[0], *k.v_s, inplace=True
            )
            step(gng)
            step(vg)
            if merged:
                finish(yy, pj)
                output_rows(k)
            finish(og)
            step(qg)
            step(fcg)
            finish(gng)
            gain_row = k.vec[0:1]

            def norm_back_rows(at):
                v = k.rows[at].astype(F32)
                center = jnp.mean(v, axis=-1, keepdims=True)
                v = v - center
                scale = lax.rsqrt(jnp.mean(v * v, axis=-1, keepdims=True) + 1e-05)
                v = v * scale
                dn = k.gn_sum[0][at]
                small[2:3] += jnp.sum(dn * v, axis=0, keepdims=True)
                small[3:4] += jnp.sum(dn, axis=0, keepdims=True)
                dn = dn * gain_row
                c1 = jnp.mean(dn, axis=-1, keepdims=True)
                c2 = jnp.mean(dn * v, axis=-1, keepdims=True)
                k.input_grad[at] = g_res[at] + scale * (dn - c1 - v * c2)

            row_loop(R, norm_back_rows)
            small[0:1, cols(lax.axis_index("seq"), QC)] = jnp.sum(
                gq[...].astype(F32), axis=0, keepdims=True
            )
            v_sum = jnp.sum(gkv[:, HD:].astype(F32), axis=0, keepdims=True)
            for b in range(G):
                small[7:8, b * W : b * W + HD] = v_sum

            def small_sums():
                got, line = k.s_got[0], k.s_line[0]
                yield from exchange_steps(
                    zy,
                    lambda o, i: small.at[:, cols(o * zy.ni + i, W)],
                    lambda o, i: got.at[o * zy.ni + i],
                    *k.s_x,
                )
                line[:, :W] = sum([got[b] for b in range(1, G)], got[0])
                line[:, W:] = k.fc_terms[...]
                yield
                yield from gather_steps(
                    sq, line, lambda o, i: k.s_all[0].at[2 * o + i], *k.s_g
                )

            sg = small_sums()
            step(sg)
            step(qg)
            step(vg)
            step(fcg)
            step(sg)
            step(qg)
            step(vg)
            step(fcg)
            step(sg)
            finish(qg, vg)
            tails = [
                gather_steps(
                    sq, k.o_acc[0], lambda o, i: k.o_all.at[:, cols(2 * o + i, QC)], *k.o_g
                ),
                gather_steps(
                    sq, k.q_acc[0], lambda o, i: k.q_all.at[:, cols(2 * o + i, QC)], *k.q_g
                ),
                gather_steps(sq, k.v_acc[0], lambda o, i: k.v_all.at[2 * o + i], *k.v_g),
            ]
            finish(sg, *tails, fcg)
            tot = k.s_all[0][0]
            for b in range(1, S):
                tot = tot + k.s_all[0][b]
            k.s_sum[...] = tot

        def grad_fc(k):
            acc, line = k.fc_acc[0], k.fc_line[0]
            yield from scatter_steps(sq, lambda o, i: k.d_fc.at[:, 2 * o + i], acc, *k.fc_s)
            yield from exchange_steps(
                zy,
                lambda o, i: acc.at[o * zy.ni + i],
                lambda o, i: line.at[:, cols(o * zy.ni + i, ffl)],
                *k.fc_x,
            )
            yield from gather_steps(
                sq, line, lambda o, i: k.fc_all.at[cols(2 * o + i, fc_rows)], *k.fc_g
            )

        fc_shape = (G, fc_rows, ffl)
        ins_one = dict(
            gx=(gx_part.reshape(G, R, D), ANY),
            y=(y_part.reshape(G, R, D), ANY),
            d_proj=(d_proj.reshape((S,) + far_out), ANY),
            cot=(g_out, VMEM),
            residual=(residual, VMEM),
            vec=(vec, VMEM),
            w_back=(w_back, ANY),
        )
        ins_two = dict(
            d_fc=(d_fc.reshape(G, S, fc_rows, ffl), ANY),
            rows=(rows_in, VMEM),
            att_rows=(att_rows, ANY),
            normed=(normed, ANY),
            w_in=(w_in, ANY),
            q=(queries, VMEM),
            kv=(keyval, VMEM),
            other=(other, VMEM),
            fc_terms=(grad_fc_bias.reshape(8, -1), VMEM),
        )
        outs_one = dict(
            layer_out=(rows_d, BF, VMEM),
            d_proj_all=((S,) + far_out, BF, ANY),
        )
        outs_two = dict(
            input_grad=((R, D), F32, VMEM),
            o_all=((W, D), BF, ANY),
            q_all=((W, D), BF, ANY),
            v_all=((S, W, 2 * HD), BF, ANY),
            fc_all=((W, G * ffl), BF, ANY),
            s_sum=((8, W + ffl // 8), F32, VMEM),
        )
        scr_one = dict(
            gx_s=scatter_scratch(zy, rows_d, BF),
            y_s=scatter_scratch(zy, rows_d, BF, mid=False),
            pj_acc=[VMEM(far_out, BF)],
            pj_s=scatter_scratch(sq, far_out, BF),
            pj_g=gather_sems(sq),
            gb=[VMEM(rows_d, BF)],
            gb_x=exchange_sems(sq),
            ga_s=scatter_scratch(sq, (T, QC), BF, mid=False),
            sum_one=[VMEM(rows_d, F32)],
        )
        scr_two = dict(
            lines=[VMEM((T, D), BF)],
            do=[VMEM((G, W, QC), BF)],
            dkv_own=[VMEM((T, 2 * HD), F32)],
            dkv_oth=[VMEM((T, 2 * HD), F32)],
            gkv_out=[VMEM((T, 2 * HD), BF)],
            gkv_in=[VMEM((T, 2 * HD), BF)],
            gkv=[VMEM((T, 2 * HD), BF)],
            swap=[DMA((1,)), DMA((1,))],
            gq=[VMEM((T, QC), BF)],
            dq=[VMEM((G, W, QC), BF)],
            dkv=[VMEM((G, W, 2 * HD), BF)],
            gn_sum=[VMEM((R, D), F32)],
            gn_s=scatter_scratch(sq, (R, D), BF, mid=False),
            o_acc=[VMEM((W, QC), BF)],
            q_acc=[VMEM((W, QC), BF)],
            v_acc=[VMEM((W, 2 * HD), BF)],
            o_s=scatter_scratch(zy, (W, QC), BF, mid=False),
            q_s=scatter_scratch(zy, (W, QC), BF, mid=False),
            v_s=scatter_scratch(zy, (W, 2 * HD), BF, mid=False),
            o_g=gather_sems(sq),
            q_g=gather_sems(sq),
            v_g=gather_sems(sq),
            fc_acc=[VMEM(fc_shape, BF)],
            fc_line=[VMEM((fc_rows, G * ffl), BF)],
            fc_s=scatter_scratch(sq, fc_shape, BF),
            fc_x=exchange_sems(zy),
            fc_g=gather_sems(sq),
            s_got=[VMEM((G, 8, W), F32)],
            s_line=[VMEM((8, W + ffl // 8), F32)],
            s_all=[VMEM((S, 8, W + ffl // 8), F32)],
            s_x=exchange_sems(zy),
            s_g=gather_sems(sq),
        )
        scr_both = dict(
            load=[DMA((4,))],
            mats=[VMEM((D, QC + 2 * HD), BF)],
            wide=[VMEM((T, D), BF)],
        )
        passed = dict(
            gbs=[VMEM((T, QC), BF)],
            g_res=[VMEM(rows_d, F32)],
            g_att=[VMEM((T, QC), BF)],
            small=[VMEM((8, D), F32)],
        )
        if merged:
            b2 = fused(
                "back",
                6,
                [zy, sq],
                {**ins_one, **ins_two},
                {**outs_one, **outs_two},
                {**scr_one, **scr_two, **scr_both, **passed},
                back_main,
                back_pre,
            )
        else:
            left = {n: (v[0].shape, v[0].dtype, VMEM) for n, v in passed.items()}
            b1 = fused(
                "back_one",
                6,
                [zy, sq],
                ins_one,
                {**outs_one, **left},
                {**scr_one, **scr_both},
                back_main,
                back_pre,
            )
            given = {n: (getattr(b1, n), VMEM) for n in passed if n != "small"}
            given.update(start=(b1.small, VMEM))

            def rest_main(k):
                for n in (1, 2):
                    load(k, n).start()
                k.small[0][...] = k.start[...]
                load(k, 1).wait()
                back_rest(k, out_weight(k), None, None)

            b2 = fused(
                "back_two",
                7,
                [zy, sq],
                {**ins_two, **given, "vec": (vec, VMEM)},
                outs_two,
                {**scr_two, **scr_both, "small": passed["small"]},
                rest_main,
            )
            b2 = SimpleNamespace(**{**vars(b1), **vars(b2)})
        d_proj_all = b2.d_proj_all
        sums = b2.s_sum
        grad_w_qkv = jnp.concatenate(
            [b2.q_all.astype(F32), jnp.sum(b2.v_all.astype(F32), axis=0)], axis=1
        )
        return (
            b2.layer_out[None],
            b2.input_grad[None],
            grad_w_qkv,
            sums[0, :W],
            lax.dynamic_slice_in_dim(sums[7, :HD], place_zy * vb, vb, 0),
            b2.o_all.astype(F32),
            sums[1, :W],
            sums[2, :W],
            sums[3, :W],
            b2.fc_all.astype(F32),
            sums[:, W:].reshape(-1),
            d_proj_all.reshape(-1, D).astype(F32),
            sums[4, :W],
            sums[5, :W],
            sums[6, :W],
        )

    return body


def solution(mesh):
    rows = P("batch", ("ctx", "seq"), None)
    mat = P(("batch", "ctx"), None)
    vec = P(("batch", "ctx"))
    in_specs = (rows, mat, vec, vec, mat, vec, vec, vec, mat, vec, mat, vec, vec, vec, rows)
    out_specs = (rows, rows, mat, vec, vec, mat, vec, vec, vec, mat, vec, mat, vec, vec, vec)
    return jax.shard_map(
        make_body(mesh), mesh=mesh, in_specs=in_specs, out_specs=out_specs, check_vma=False
    )
```
